32 devices in a mesh: seq: 8 (over y, x, core), head: 4 (over z).
Axes of the slice: x: 2, y: 2, z: 4, core: 2. Of those that a mesh axis runs over, the one named last changes fastest.
Arguments:
- queries: bfloat16 [8192, 8192], P(('seq', 'head')), may hold values from -64 to 64
- key_rows: bfloat16 [8192, 1024], P(('seq', 'head')), may hold values from -6 to 6
- value_projection_rows: bfloat16 [8192, 1024], P(('seq', 'head')), may hold values from -6 to 6
- upstream: bfloat16 [8192, 8192], P(('seq', 'head')), may hold values from -6 to 6
- ancestors: int32 [128, 2], P('seq'), may hold values from -1 to 126, as said below
Outputs:
- attended: bfloat16 [8192, 8192], P(('seq', 'head'))
- query_grad: bfloat16 [8192, 8192], P(('seq', 'head'))
- key_grad: bfloat16 [8192, 1024], P(('seq', 'head'))
- value_grad: bfloat16 [8192, 1024], P(('seq', 'head'))
The draws below stay inside these ranges and needn't reach their ends.
Inputs may be any that keep to these rules, and one draw needn't show every extreme that they name: `ancestors`: each entry of row b is -1 (no ancestor) or a block index from max(1, b - 32) to b - 1; where that range is not empty the first entry is b - 1, and where b is a multiple of 16 the last entry is the lowest index of that range. Entries of a row may repeat.
All inputs are finite; a program needn't handle non-finite values.
Results may differ from the reference program's by a relative error of at most 0.012.
The reference program's roundings to bfloat16 on the way (of `probs` and `dscore`) count: a program that leaves them out, or rounds other values in their place, can miss the bound.
Values may be sent and summed in bfloat16 or wider, within the bound.
A program may use at most 192 MiB of HBM per device.

```python
import jax
import jax.numpy as jnp
from jax import lax

QUERY_HEAD_COUNT = 64
KEY_VALUE_HEADS = 8
HEAD_SIZE = 128
MASK_BLOCK_SIZE = 64
ROOT = 64
ANC = 2
PACKED_TOKENS = 8192
ROW_MASK_BLOCKS = 128
BPS = 16


def base_keys(key):
    source = jax.random.fold_in(key, 101)
    array_shape = (PACKED_TOKENS, KEY_VALUE_HEADS * HEAD_SIZE)
    value_matrix = jnp.clip(jax.random.normal(source, array_shape, jnp.float32), -6.0, 6.0)
    return value_matrix


def draw_key_rows(key, part):
    return base_keys(key).astype(jnp.bfloat16)


def draw_queries(key, part):
    source = jax.random.fold_in(key, 202)
    array_shape = (PACKED_TOKENS, QUERY_HEAD_COUNT * HEAD_SIZE)
    value_matrix = jnp.clip(jax.random.normal(source, array_shape, jnp.float32), -6.0, 6.0)
    return value_matrix.astype(jnp.bfloat16)


def draw_ancestors(key, part):
    block = jnp.arange(ROW_MASK_BLOCKS, dtype=jnp.int32)[:, None]
    lowest = jnp.maximum(ROOT // MASK_BLOCK_SIZE, block - 2 * BPS)
    highest = block - 1
    span = highest - lowest + 1
    raw = jax.random.randint(jax.random.fold_in(key, 303), (ROW_MASK_BLOCKS, ANC), 0, 1048576, jnp.int32)
    picked = lowest + raw % jnp.maximum(span, 1)
    shard_start = block % BPS == 0
    drawn_count = jax.random.randint(jax.random.fold_in(key, 304), (ROW_MASK_BLOCKS, 1), 1, ANC + 1, jnp.int32)
    count = jnp.where(shard_start, ANC, drawn_count)
    column = jnp.arange(ANC, dtype=jnp.int32)[None, :]
    entry = jnp.where(shard_start & (column == ANC - 1), lowest, picked)
    entry = jnp.where(column == 0, highest, entry)
    return jnp.where((column < count) & (span > 0), entry, -1).astype(jnp.int32)


def block_scale(key, extent, pieces, least, top_value):
    loudness = 1.0
    for position, blocks in pieces:
        heights = jax.random.uniform(jax.random.fold_in(jax.random.fold_in(key, 6), position), (blocks,), jnp.float32, least / len(pieces), top_value / len(pieces))
        loudness = loudness * jnp.repeat(jnp.exp(heights), extent[position] // blocks).reshape((-1,) + (1,) * (len(extent) - 1 - position))
    return loudness


def scatter_about(own_key, extent, deviation, limit, cuts=(), kind=jnp.bfloat16):
    factor_of = block_scale(own_key, extent, cuts, -0.22, 0.18) if cuts else 1.0
    values = jax.random.normal(own_key, extent, jnp.float32) * deviation * factor_of
    return jnp.minimum(jnp.maximum(values, -limit), limit).astype(kind)


def setup_inputs(seed: int = 0) -> dict:
    streams_of = jax.random.split(jax.random.key(seed), 6)
    return {
        "queries": draw_queries(jax.random.fold_in(streams_of[5], 71), 0),
        "key_rows": draw_key_rows(jax.random.fold_in(streams_of[5], 71), 0),
        "value_projection_rows": scatter_about(streams_of[2], (PACKED_TOKENS, KEY_VALUE_HEADS * HEAD_SIZE), 1.0, 6.0, ((0, 32),)),
        "upstream": scatter_about(streams_of[3], (PACKED_TOKENS, QUERY_HEAD_COUNT * HEAD_SIZE), 1.0, 6.0, ((0, 32),)),
        "ancestors": draw_ancestors(jax.random.fold_in(streams_of[5], 71), 0),
    }


NEGATIVE = -1.0e30


def distinct_entries(ancestor_row):
    order = jnp.arange(ANC, dtype=jnp.int32)
    before = order[None, :] < order[:, None]
    repeated = jnp.any((ancestor_row[:, None] == ancestor_row[None, :]) & before, axis=1)
    return (ancestor_row >= 0) & jnp.logical_not(repeated)


def reference(queries, key_rows, value_projection_rows, upstream, ancestors):
    query_groups = QUERY_HEAD_COUNT // KEY_VALUE_HEADS
    scale = HEAD_SIZE ** -0.5
    head_width = KEY_VALUE_HEADS * HEAD_SIZE
    blocked_keys = key_rows.reshape(ROW_MASK_BLOCKS, MASK_BLOCK_SIZE, head_width)
    blocked_values = value_projection_rows.reshape(ROW_MASK_BLOCKS, MASK_BLOCK_SIZE, head_width)
    tree_root_key = key_rows[:ROOT]
    tree_root_value = value_projection_rows[:ROOT]
    query_blocks = queries.reshape(ROW_MASK_BLOCKS, MASK_BLOCK_SIZE, QUERY_HEAD_COUNT * HEAD_SIZE)
    upstream_blocks = upstream.reshape(ROW_MASK_BLOCKS, MASK_BLOCK_SIZE, QUERY_HEAD_COUNT * HEAD_SIZE)
    inner = jnp.arange(MASK_BLOCK_SIZE, dtype=jnp.int32)

    def step(carry, inputs):
        key_acc, value_acc = carry
        block_index, blocked_query, blocked_upstream, ancestor_row = inputs
        valid = distinct_entries(ancestor_row)
        picked = jnp.maximum(ancestor_row, 0).astype(jnp.int32)
        ancestor_key = blocked_keys[picked].reshape(ANC * MASK_BLOCK_SIZE, head_width)
        ancestor_value = blocked_values[picked].reshape(ANC * MASK_BLOCK_SIZE, head_width)
        key_matrix = jnp.concatenate([tree_root_key, blocked_keys[block_index], ancestor_key], 0).astype(jnp.float32).reshape(-1, KEY_VALUE_HEADS, HEAD_SIZE)
        value_matrix = jnp.concatenate([tree_root_value, blocked_values[block_index], ancestor_value], 0).astype(jnp.float32).reshape(-1, KEY_VALUE_HEADS, HEAD_SIZE)
        query_pos = (block_index * MASK_BLOCK_SIZE + inner).astype(jnp.int32)
        root_pos = jnp.arange(ROOT, dtype=jnp.int32)
        anc_rows = (picked[:, None] * MASK_BLOCK_SIZE + inner[None, :]).reshape(-1).astype(jnp.int32)
        root_mask = root_pos[None, :] <= query_pos[:, None]
        own_mask = (query_pos[None, :] <= query_pos[:, None]) & (query_pos[None, :] >= ROOT)
        anc_mask = jnp.broadcast_to(jnp.repeat(valid, MASK_BLOCK_SIZE)[None, :], (MASK_BLOCK_SIZE, ANC * MASK_BLOCK_SIZE))
        mask = jnp.concatenate([root_mask, own_mask, anc_mask], 1)
        heads_of_query = blocked_query.astype(jnp.float32).reshape(MASK_BLOCK_SIZE, KEY_VALUE_HEADS, query_groups, HEAD_SIZE)
        scores = jnp.einsum("qkgd,skd->kgqs", heads_of_query, key_matrix) * scale
        masked = jnp.where(mask, scores, NEGATIVE)
        row_top = jnp.max(masked, axis=-1, keepdims=True)
        row_total = jnp.sum(jnp.where(mask, jnp.exp(masked - row_top), 0.0), axis=-1, keepdims=True)
        lse = row_top + jnp.log(row_total)
        probs = lax.optimization_barrier(jnp.where(mask, jnp.exp(masked - lse), 0.0).astype(jnp.bfloat16)).astype(jnp.float32)
        attended = lax.optimization_barrier(jnp.einsum("kgqs,skd->qkgd", probs, value_matrix).astype(jnp.bfloat16))
        heads_of_upstream = blocked_upstream.astype(jnp.float32).reshape(MASK_BLOCK_SIZE, KEY_VALUE_HEADS, query_groups, HEAD_SIZE)
        delta = jnp.sum(heads_of_upstream * attended.astype(jnp.float32), axis=-1).transpose(1, 2, 0)[..., None]
        dprob = jnp.einsum("qkgd,skd->kgqs", heads_of_upstream, value_matrix)
        dscore = lax.optimization_barrier((probs * (dprob - delta)).astype(jnp.bfloat16)).astype(jnp.float32)
        query_grad = (scale * jnp.einsum("kgqs,skd->qkgd", dscore, key_matrix)).astype(jnp.bfloat16)
        key_grad = (scale * jnp.einsum("kgqs,qkgd->skd", dscore, heads_of_query)).reshape(-1, head_width)
        value_grad = jnp.einsum("kgqs,qkgd->skd", probs, heads_of_upstream).reshape(-1, head_width)
        rows = jnp.concatenate([root_pos, query_pos, anc_rows], 0).astype(jnp.int32)
        key_acc = key_acc.at[rows].add(key_grad)
        value_acc = value_acc.at[rows].add(value_grad)
        return (key_acc, value_acc), (attended.reshape(MASK_BLOCK_SIZE, QUERY_HEAD_COUNT * HEAD_SIZE), query_grad.reshape(MASK_BLOCK_SIZE, QUERY_HEAD_COUNT * HEAD_SIZE))

    start_carry = (jnp.zeros((PACKED_TOKENS, head_width), jnp.float32), jnp.zeros((PACKED_TOKENS, head_width), jnp.float32))
    carry, stacked = lax.scan(step, start_carry, (jnp.arange(ROW_MASK_BLOCKS, dtype=jnp.int32), query_blocks, upstream_blocks, ancestors))
    key_acc, value_acc = carry
    attended = stacked[0].reshape(PACKED_TOKENS, QUERY_HEAD_COUNT * HEAD_SIZE)
    query_grad = stacked[1].reshape(PACKED_TOKENS, QUERY_HEAD_COUNT * HEAD_SIZE)
    return (attended, query_grad, key_acc.astype(jnp.bfloat16), value_acc.astype(jnp.bfloat16))
```

```python
import functools
import math

import jax
import jax.numpy as jnp
from jax import lax
from jax.experimental import pallas as pl
from jax.experimental.pallas import tpu as pltpu
from jax.sharding import PartitionSpec as P

HEAD_SIZE = 128
BLOCK = 64
NEGATIVE = -1e30
MESH = pl.DeviceIdType.MESH


def attention_kernel(
    info, q_ref, up_ref, k_ref, v_ref, k_before, v_before, edge_ref, root_ref, rand_ref,
    att_ref, dq_ref, acc, g_edge, g_rand, g_root, *, groups,
):
    j = pl.program_id(1)
    scale = HEAD_SIZE ** (-0.5)
    first = info[0] + j == 0
    rows = groups * BLOCK
    q = jnp.concatenate(
        [q_ref[:, r * HEAD_SIZE : (r + 1) * HEAD_SIZE] for r in range(groups)], axis=0
    )
    up = jnp.concatenate(
        [up_ref[:, r * HEAD_SIZE : (r + 1) * HEAD_SIZE] for r in range(groups)], axis=0
    )
    prev_k = jnp.where(j == 0, edge_ref[0], k_before[...])
    prev_v = jnp.where(j == 0, edge_ref[1], v_before[...])
    keys = jnp.concatenate([root_ref[0], k_ref[...], prev_k, rand_ref[0, 0, 0]], axis=0)
    values = jnp.concatenate([root_ref[1], v_ref[...], prev_v, rand_ref[0, 1, 0]], axis=0)
    up_t = up.T
    scores = lax.dot_general(
        keys, q, (((1,), (1,)), ((), ())), preferred_element_type=jnp.float32
    ) * (scale * math.log2(math.e))
    key_at = lax.broadcasted_iota(jnp.int32, (BLOCK, rows), 0)
    query_at = lax.broadcasted_iota(jnp.int32, (BLOCK, rows), 1) & (BLOCK - 1)
    causal = key_at <= query_at
    never = jnp.float32(NEGATIVE)
    zero = jnp.float32(0.0)
    root_off = jnp.where(causal, zero, jnp.where(first, never, zero))
    own_off = jnp.where(causal, jnp.where(first, never, zero), never)
    prev_off = jnp.where(info[1 + 2 * j] > 0, zero, never)
    rand_off = jnp.where(info[2 + 2 * j] > 0, zero, never)
    scores = jnp.concatenate(
        [
            scores[:BLOCK] + root_off,
            scores[BLOCK : 2 * BLOCK] + own_off,
            scores[2 * BLOCK : 3 * BLOCK] + prev_off,
            scores[3 * BLOCK :] + rand_off,
        ],
        axis=0,
    )
    top = jnp.max(scores, axis=0, keepdims=True)
    weights = jnp.exp2(scores - top)
    total = jnp.sum(weights, axis=0, keepdims=True)
    probs = (weights * (1.0 / total)).astype(jnp.bfloat16)
    att_t = lax.dot_general(
        values, probs, (((0,), (0,)), ((), ())), preferred_element_type=jnp.float32
    ).astype(jnp.bfloat16)
    delta = jnp.sum(
        att_t.astype(jnp.float32) * up_t.astype(jnp.float32), axis=0, keepdims=True
    )
    dprob = lax.dot_general(
        values, up_t, (((1,), (0,)), ((), ())), preferred_element_type=jnp.float32
    )
    dscore = (probs.astype(jnp.float32) * (dprob - delta)).astype(jnp.bfloat16)
    dq_t = lax.dot_general(
        keys, dscore, (((0,), (0,)), ((), ())), preferred_element_type=jnp.float32
    )
    dq = (dq_t * scale).astype(jnp.bfloat16).T
    att = att_t.T
    for r in range(groups):
        att_ref[:, r * HEAD_SIZE : (r + 1) * HEAD_SIZE] = att[r * BLOCK : (r + 1) * BLOCK]
        dq_ref[:, r * HEAD_SIZE : (r + 1) * HEAD_SIZE] = dq[r * BLOCK : (r + 1) * BLOCK]
    grads = (
        scale * jnp.dot(dscore, q, preferred_element_type=jnp.float32),
        jnp.dot(probs, up, preferred_element_type=jnp.float32),
    )
    here = pl.ds(pl.multiple_of(j * BLOCK, BLOCK), BLOCK)
    for kv, grad in enumerate(grads):
        acc[kv, here] = grad[BLOCK : 2 * BLOCK]
        g_rand[0, kv, 0] = grad[3 * BLOCK :].astype(jnp.bfloat16)

    @pl.when(j == 0)
    def _():
        for kv, grad in enumerate(grads):
            g_root[kv] = grad[:BLOCK]
            g_edge[kv] = grad[2 * BLOCK : 3 * BLOCK].astype(jnp.bfloat16)

    @pl.when(j > 0)
    def _():
        before = pl.ds(pl.multiple_of((j - 1) * BLOCK, BLOCK), BLOCK)
        for kv, grad in enumerate(grads):
            g_root[kv] += grad[:BLOCK]
            acc[kv, before] += grad[2 * BLOCK : 3 * BLOCK]


def attention(info, queries, upstream, key_rows, value_rows, edge, root, rand):
    tokens, width = key_rows.shape
    blocks = tokens // BLOCK
    heads = width // HEAD_SIZE
    groups = queries.shape[1] // width
    wide = groups * HEAD_SIZE
    token_spec = pl.BlockSpec((BLOCK, wide), lambda g, j, _: (j, g))
    here = pl.BlockSpec((BLOCK, HEAD_SIZE), lambda g, j, _: (j, g))
    before = pl.BlockSpec((BLOCK, HEAD_SIZE), lambda g, j, _: (jnp.maximum(j - 1, 0), g))
    pair = pl.BlockSpec((2, BLOCK, HEAD_SIZE), lambda g, j, _: (0, 0, g))
    slot = pl.BlockSpec((1, 2, 1, BLOCK, HEAD_SIZE), lambda g, j, _: (g, 0, j, 0, 0))
    elements = blocks * heads * groups * BLOCK * 4 * BLOCK
    return pl.pallas_call(
        functools.partial(attention_kernel, groups=groups),
        grid_spec=pltpu.PrefetchScalarGridSpec(
            num_scalar_prefetch=1,
            grid=(heads, blocks),
            in_specs=[token_spec, token_spec, here, here, before, before, pair, pair, slot],
            out_specs=[
                token_spec,
                token_spec,
                pl.BlockSpec((2, tokens, HEAD_SIZE), lambda g, j, _: (0, 0, g)),
                pair,
                slot,
                pair,
            ],
        ),
        out_shape=[
            jax.ShapeDtypeStruct(queries.shape, jnp.bfloat16),
            jax.ShapeDtypeStruct(queries.shape, jnp.bfloat16),
            jax.ShapeDtypeStruct((2, tokens, width), jnp.float32),
            jax.ShapeDtypeStruct((2, BLOCK, width), jnp.bfloat16),
            jax.ShapeDtypeStruct((heads, 2, blocks, BLOCK, HEAD_SIZE), jnp.bfloat16),
            jax.ShapeDtypeStruct((2, BLOCK, width), jnp.float32),
        ],
        cost_estimate=pl.CostEstimate(
            flops=12 * elements * HEAD_SIZE,
            transcendentals=elements,
            bytes_accessed=blocks * heads * wide * BLOCK * 8,
        ),
        compiler_params=pltpu.CompilerParams(vmem_limit_bytes=40 * 1024 * 1024),
        name="attention",
    )(info, queries, upstream, key_rows, value_rows, key_rows, value_rows, edge, root, rand)


def tree_steps(length):
    steps, step = [], 1
    while step < length:
        steps.append(step)
        step *= 2
    return steps


def greet(head_size, seq_size):
    shard, part = lax.axis_index("seq"), lax.axis_index("head")
    barrier = pltpu.get_barrier_semaphore()
    count = 0

    def signal(other):
        pl.semaphore_signal(barrier, inc=1, device_id=other, device_id_type=MESH)

    for d in range(1, head_size):
        signal((shard, lax.rem(part + d, head_size)))
        count += 1
    for step in tree_steps(seq_size):
        signal((lax.rem(shard + step, seq_size), part))
        signal((lax.rem(shard + seq_size - step, seq_size), part))
        count += 2
    after, before = lax.rem(shard + 1, seq_size), lax.rem(shard + seq_size - 1, seq_size)

    @pl.when(part == head_size - 1)
    def _():
        signal((after, 0))

    @pl.when(part == 0)
    def _():
        signal((before, head_size - 1))

    at_end = jnp.logical_or(part == 0, part == head_size - 1)
    pl.semaphore_wait(barrier, count + jnp.where(at_end, 1, 0))


def send(source, target, send_sem, recv_sem, other):
    return pltpu.make_async_remote_copy(
        src_ref=source,
        dst_ref=target,
        send_sem=send_sem,
        recv_sem=recv_sem,
        device_id=other,
        device_id_type=MESH,
    )


def rows_of(at, count):
    return pl.ds(at, count)


def gather_kernel(
    head_size, seq_size, chosen, k_ref, v_ref, rand, edge, root,
    *rest,
):
    shard, part = lax.axis_index("seq"), lax.axis_index("head")
    blocks, _, width = k_ref.shape
    slots = blocks * head_size
    each = width // HEAD_SIZE // head_size
    pieces = 2 * each
    window, rest = rest[:pieces], rest[pieces:]
    (stage, a_send, a_recv, near_send, near_recv, far_send, far_recv,
     b_send, b_recv, edge_send, edge_recv, root_send, root_recv) = rest
    inputs = (k_ref, v_ref)
    seq_steps = tree_steps(seq_size)
    after = jnp.minimum(shard + 1, seq_size - 1)
    has_after, has_before = shard + 1 < seq_size, shard > 0
    at_first = jnp.logical_and(shard == 0, part == 0)

    def columns(p, c):
        return pl.ds(pl.multiple_of((p * each + c // 2) * HEAD_SIZE, HEAD_SIZE), HEAD_SIZE)

    greet(head_size, seq_size)

    def slice_out(d, c):
        other = lax.rem(part + d, head_size)
        return send(
            inputs[c % 2].at[:, :, columns(other, c)],
            window[c].at[rows_of(2 * slots + part * blocks, blocks)],
            a_send.at[d, c], a_recv.at[d, c], (shard, other),
        )

    def near_copy(c):
        return send(
            window[c].at[rows_of(2 * slots, slots)], window[c].at[rows_of(slots, slots)],
            near_send.at[c], near_recv.at[c], (after, part),
        )

    def far_copy(c):
        return send(
            window[c].at[rows_of(slots, slots)], window[c].at[rows_of(0, slots)],
            far_send.at[c], far_recv.at[c], (after, part),
        )

    def slice_back(d, c):
        other = lax.rem(part + d, head_size)
        return send(
            stage.at[c, rows_of(other * blocks, blocks)],
            rand.at[part * each + c // 2, c % 2],
            b_send.at[d, c], b_recv.at[d, c], (shard, other),
        )

    def edge_copy(kv):
        last = part == head_size - 1
        other = (jnp.where(last, after, shard), jnp.where(last, 0, part + 1))
        return send(
            inputs[kv].at[blocks - 1], edge.at[kv],
            edge_send.at[kv], edge_recv.at[kv], other,
        )

    gives_edge = jnp.logical_or(part < head_size - 1, has_after)
    gets_edge = jnp.logical_or(part > 0, has_before)

    def root_over_head(z):
        return send(root, root, root_send.at[z - 1], root_recv.at[z - 1], (shard, z))

    def root_over_seq(e):
        step = seq_steps[e]
        other = jnp.minimum(shard + step, seq_size - 1)
        at = head_size - 1 + e
        copy = send(root, root, root_send.at[at], root_recv.at[at], (other, part))
        gives = jnp.logical_and(shard < step, shard + step < seq_size)
        gets = jnp.logical_and(shard >= step, shard < 2 * step)
        return copy, gives, gets

    def root_event(e):
        if e == 0:

            @pl.when(jnp.logical_and(shard == 0, part > 0))
            def _():
                root_over_head(jnp.maximum(part, 1)).wait_recv()

        elif e <= len(seq_steps):
            copy, _, gets = root_over_seq(e - 1)
            pl.when(gets)(copy.wait_recv)
        if e < len(seq_steps):
            copy, gives, _ = root_over_seq(e)
            pl.when(gives)(copy.start)

    def start_slices(c):
        for d in range(1, head_size):
            slice_out(d, c).start()

    start_slices(0)

    @pl.when(at_first)
    def _():
        for kv in range(2):
            root[kv] = inputs[kv][0]
        for z in range(1, head_size):
            root_over_head(z).start()

    if pieces > 1:
        start_slices(1)
    for c in range(pieces):
        window[c][rows_of(2 * slots + part * blocks, blocks)] = inputs[c % 2][
            :, :, columns(part, c)
        ]

    @pl.when(jnp.logical_not(gets_edge))
    def _():
        for kv in range(2):
            edge[kv] = inputs[kv][0]

    done = 0
    for at in range(pieces + 2):
        if at < pieces:
            c = at
            for d in range(1, head_size):
                slice_out(d, c).wait_recv()
            if c + 2 < pieces:
                start_slices(c + 2)
            pl.when(has_after)(near_copy(c).start)
            if c == pieces - 2:
                for kv in range(2):
                    pl.when(gives_edge)(edge_copy(kv).start)
        if 0 <= at - 1 < pieces:
            c = at - 1
            pl.when(has_before)(near_copy(c).wait_recv)
            pl.when(jnp.logical_and(has_before, has_after))(far_copy(c).start)
        if 0 <= at - 2:
            c = at - 2
            pl.when(shard > 1)(far_copy(c).wait_recv)
            for d in range(1, head_size):
                other = lax.rem(part + d, head_size)
                for n in range(blocks):
                    stage[c, other * blocks + n] = window[c][chosen[other * blocks + n]]
                slice_back(d, c).start()
            for n in range(blocks):
                rand[part * each + c // 2, c % 2, n] = window[c][chosen[part * blocks + n]]
        root_event(done)
        done += 1
    while done <= len(seq_steps):
        root_event(done)
        done += 1
    for kv in range(2):
        pl.when(gets_edge)(edge_copy(kv).wait_recv)
    for c in range(pieces):
        for d in range(1, head_size):
            slice_back(d, c).wait_recv()
    for c in range(pieces):
        for d in range(1, head_size):
            slice_out(d, c).wait_send()
            slice_back(d, c).wait_send()
        pl.when(has_after)(near_copy(c).wait_send)
        pl.when(jnp.logical_and(has_before, has_after))(far_copy(c).wait_send)
    for kv in range(2):
        pl.when(gives_edge)(edge_copy(kv).wait_send)
    for e in range(len(seq_steps)):
        copy, gives, _ = root_over_seq(e)
        pl.when(gives)(copy.wait_send)

    @pl.when(at_first)
    def _():
        for z in range(1, head_size):
            root_over_head(z).wait_send()


def gather(chosen, key_rows, value_rows, head_size, seq_size):
    blocks, _, width = key_rows.shape
    heads = width // HEAD_SIZE
    pieces = 2 * heads // head_size
    slots = blocks * head_size
    events = head_size - 1 + len(tree_steps(seq_size))
    vmem, smem = pltpu.MemorySpace.VMEM, pltpu.MemorySpace.SMEM
    dma = pltpu.SemaphoreType.DMA
    return pl.pallas_call(
        functools.partial(gather_kernel, head_size, seq_size),
        in_specs=[
            pl.BlockSpec(memory_space=smem),
            pl.BlockSpec(memory_space=vmem),
            pl.BlockSpec(memory_space=vmem),
        ],
        out_specs=[pl.BlockSpec(memory_space=vmem)] * 3,
        out_shape=[
            jax.ShapeDtypeStruct((heads, 2, blocks, BLOCK, HEAD_SIZE), jnp.bfloat16),
            jax.ShapeDtypeStruct((2, BLOCK, width), jnp.bfloat16),
            jax.ShapeDtypeStruct((2, BLOCK, width), jnp.bfloat16),
        ],
        scratch_shapes=[
            *[pltpu.VMEM((3 * slots, BLOCK, HEAD_SIZE), jnp.bfloat16)] * pieces,
            pltpu.VMEM((pieces, slots, BLOCK, HEAD_SIZE), jnp.bfloat16),
            dma((head_size, pieces)), dma((head_size, pieces)),
            dma((pieces,)), dma((pieces,)), dma((pieces,)), dma((pieces,)),
            dma((head_size, pieces)), dma((head_size, pieces)),
            dma((2,)), dma((2,)), dma((events,)), dma((events,)),
        ],
        compiler_params=pltpu.CompilerParams(
            collective_id=0, has_side_effects=True, vmem_limit_bytes=40 * 1024 * 1024
        ),
        name="gather",
    )(chosen, key_rows, value_rows)


def scatter_kernel(
    head_size, seq_size, links, g_rand, g_edge, g_root, acc, k_out, v_out,
    slots_in, chain, sections, near_in, far_in, back, edge_in, root, root_total, root_box,
    a_send, a_recv, near_send, near_recv, far_send, far_recv,
    b_send, b_recv, edge_send, edge_recv, root_send, root_recv,
):
    shard, part = lax.axis_index("seq"), lax.axis_index("head")
    tokens, width = k_out.shape
    blocks = tokens // BLOCK
    slots = blocks * head_size
    each = width // HEAD_SIZE // head_size
    pieces = 2 * each
    outputs = (k_out, v_out)
    seq_steps = tree_steps(seq_size)[::-1]
    before = jnp.maximum(shard - 1, 0)
    has_after, has_before = shard + 1 < seq_size, shard > 0

    def columns(p, c):
        return pl.ds(pl.multiple_of((p * each + c // 2) * HEAD_SIZE, HEAD_SIZE), HEAD_SIZE)

    greet(head_size, seq_size)

    def slice_out(d, c):
        other = lax.rem(part + d, head_size)
        return send(
            g_rand.at[other * each + c // 2, c % 2],
            slots_in.at[c, rows_of(part * blocks, blocks)],
            a_send.at[d, c], a_recv.at[d, c], (shard, other),
        )

    def far_copy(c):
        return send(
            sections.at[c, rows_of(0, slots)], far_in.at[c],
            far_send.at[c], far_recv.at[c], (before, part),
        )

    def near_copy(c):
        return send(
            sections.at[c, rows_of(slots, slots)], near_in.at[c],
            near_send.at[c], near_recv.at[c], (before, part),
        )

    def slice_back(d, c):
        other = lax.rem(part + d, head_size)
        return send(
            sections.at[c, rows_of(2 * slots + other * blocks, blocks)], back.at[c, part],
            b_send.at[d, c], b_recv.at[d, c], (shard, other),
        )

    def edge_copy():
        other = (
            jnp.where(part == 0, before, shard),
            jnp.where(part == 0, head_size - 1, part - 1),
        )
        return send(g_edge, edge_in, edge_send.at[0], edge_recv.at[0], other)

    gives_edge = jnp.logical_or(part > 0, has_before)
    gets_edge = jnp.logical_or(part < head_size - 1, has_after)

    def root_over_seq(e):
        step = seq_steps[e]
        other = jnp.maximum(shard - step, 0)
        at = head_size - 1 + e
        copy = send(root, root_box.at[at], root_send.at[at], root_recv.at[at], (other, part))
        gives = jnp.logical_and(shard >= step, shard < 2 * step)
        gets = jnp.logical_and(shard < step, shard + step < seq_size)
        return copy, gives, gets

    def root_over_head(z):
        return send(root, root_box.at[z - 1], root_send.at[z - 1], root_recv.at[z - 1], (shard, 0))

    gives_last = jnp.logical_and(shard == 0, part > 0)

    def root_event(e):
        if 0 < e <= len(seq_steps):
            copy, _, gets = root_over_seq(e - 1)

            @pl.when(gets)
            def _():
                copy.wait_recv()
                root[...] += root_box[head_size - 1 + e - 1]

        if e < len(seq_steps):
            copy, gives, _ = root_over_seq(e)
            pl.when(gives)(copy.start)
        elif e == len(seq_steps):

            @pl.when(gives_last)
            def _():
                root_over_head(jnp.maximum(part, 1)).start()

    def start_slices(c):
        for d in range(1, head_size):
            slice_out(d, c).start()

    start_slices(0)
    if pieces > 1:
        start_slices(1)
    root[...] = g_root[...]
    root_event(0)
    done = 1
    for c in range(pieces):
        slots_in[c, rows_of(part * blocks, blocks)] = g_rand[part * each + c // 2, c % 2]

    def section(c, t):
        at = links[slots + t]
        found = chain[jnp.maximum(at, 0)]
        return jnp.where(at >= 0, found, 0.0)

    for at in range(pieces + 2):
        if 0 <= at - 2:
            c = at - 2

            @pl.when(has_after)
            def _(c=c):
                near_copy(c).wait_recv()
                where = rows_of(2 * slots, slots)
                sections[c, where] = (
                    sections[c, where].astype(jnp.float32) + near_in[c].astype(jnp.float32)
                ).astype(jnp.bfloat16)

            for d in range(1, head_size):
                slice_back(d, c).start()
        if 0 <= at - 1 < pieces:
            c = at - 1

            @pl.when(jnp.logical_and(has_before, has_after))
            def _(c=c):
                far_copy(c).wait_recv()
                where = rows_of(slots, slots)
                sections[c, where] = (
                    sections[c, where].astype(jnp.float32) + far_in[c].astype(jnp.float32)
                ).astype(jnp.bfloat16)

            pl.when(has_before)(near_copy(c).start)
        if at < pieces:
            c = at
            for d in range(1, head_size):
                slice_out(d, c).wait_recv()
            if c + 2 < pieces:
                start_slices(c + 2)
            for n in range(slots):
                term = slots_in[c, n].astype(jnp.float32)
                if n > 0:
                    same = links[n]
                    found = chain[jnp.maximum(same, 0)]
                    term = term + jnp.where(same >= 0, found, 0.0)
                chain[n] = term
            for t in range(3 * slots):
                sections[c, t] = section(c, t).astype(jnp.bfloat16)
                if t == slots - 1:
                    pl.when(shard > 1)(far_copy(c).start)
            if c == pieces - 1:
                pl.when(gives_edge)(edge_copy().start)
        root_event(done)
        done += 1
    while done <= len(seq_steps):
        root_event(done)
        done += 1

    root_total[...] = jnp.zeros_like(root_total)

    @pl.when(gets_edge)
    def _():
        edge_copy().wait_recv()

    @pl.when(jnp.logical_not(gets_edge))
    def _():
        edge_in[...] = jnp.zeros_like(edge_in)

    @pl.when(jnp.logical_and(shard == 0, part == 0))
    def _():
        for z in range(1, head_size):
            root_over_head(z).wait_recv()
        total = root[...]
        for z in range(1, head_size):
            total += root_box[z - 1]
        root_total[...] = total

    def finish(c, p, came):
        where = columns(p, c)
        for n in range(blocks):
            here = pl.ds(n * BLOCK, BLOCK)
            total = acc[c % 2, here, where] + came[n].astype(jnp.float32)
            if n == 0:
                total += root_total[c % 2, :, where]
            if n == blocks - 1:
                total += edge_in[c % 2, :, where].astype(jnp.float32)
            outputs[c % 2][here, where] = total.astype(jnp.bfloat16)

    for c in range(pieces):
        finish(c, part, sections.at[c, rows_of(2 * slots + part * blocks, blocks)])
        for d in range(1, head_size):
            came = lax.rem(part + head_size - d, head_size)
            slice_back(d, c).wait_recv()
            finish(c, came, back.at[c, came])
    for c in range(pieces):
        for d in range(1, head_size):
            slice_out(d, c).wait_send()
            slice_back(d, c).wait_send()
        pl.when(shard > 1)(far_copy(c).wait_send)
        pl.when(has_before)(near_copy(c).wait_send)
    pl.when(gives_edge)(edge_copy().wait_send)
    for e in range(len(seq_steps)):
        copy, gives, _ = root_over_seq(e)
        pl.when(gives)(copy.wait_send)

    @pl.when(gives_last)
    def _():
        root_over_head(jnp.maximum(part, 1)).wait_send()


def scatter(links, g_rand, g_edge, g_root, acc, head_size, seq_size):
    heads, _, blocks, _, _ = g_rand.shape
    tokens, width = blocks * BLOCK, heads * HEAD_SIZE
    pieces = 2 * heads // head_size
    slots = blocks * head_size
    events = head_size - 1 + len(tree_steps(seq_size))
    vmem, smem = pltpu.MemorySpace.VMEM, pltpu.MemorySpace.SMEM
    dma = pltpu.SemaphoreType.DMA
    return pl.pallas_call(
        functools.partial(scatter_kernel, head_size, seq_size),
        in_specs=[pl.BlockSpec(memory_space=smem)] + [pl.BlockSpec(memory_space=vmem)] * 3
        + [pl.BlockSpec(memory_space=vmem)],
        out_specs=[pl.BlockSpec(memory_space=vmem)] * 2,
        out_shape=[jax.ShapeDtypeStruct((tokens, width), jnp.bfloat16)] * 2,
        scratch_shapes=[
            pltpu.VMEM((pieces, slots, BLOCK, HEAD_SIZE), jnp.bfloat16),
            pltpu.VMEM((slots, BLOCK, HEAD_SIZE), jnp.float32),
            pltpu.VMEM((pieces, 3 * slots, BLOCK, HEAD_SIZE), jnp.bfloat16),
            pltpu.VMEM((pieces, slots, BLOCK, HEAD_SIZE), jnp.bfloat16),
            pltpu.VMEM((pieces, slots, BLOCK, HEAD_SIZE), jnp.bfloat16),
            pltpu.VMEM((pieces, head_size, blocks, BLOCK, HEAD_SIZE), jnp.bfloat16),
            pltpu.VMEM((2, BLOCK, width), jnp.bfloat16),
            pltpu.VMEM((2, BLOCK, width), jnp.float32),
            pltpu.VMEM((2, BLOCK, width), jnp.float32),
            pltpu.VMEM((events, 2, BLOCK, width), jnp.float32),
            dma((head_size, pieces)), dma((head_size, pieces)),
            dma((pieces,)), dma((pieces,)), dma((pieces,)), dma((pieces,)),
            dma((head_size, pieces)), dma((head_size, pieces)),
            dma((1,)), dma((1,)), dma((events,)), dma((events,)),
        ],
        compiler_params=pltpu.CompilerParams(
            collective_id=1, has_side_effects=True, vmem_limit_bytes=48 * 1024 * 1024
        ),
        name="scatter",
    )(links, g_rand, g_edge, g_root, acc)


def local(queries, key_rows, value_rows, upstream, ancestors):
    tokens, _ = key_rows.shape
    blocks = tokens // BLOCK
    slots = ancestors.shape[0]
    head_size, seq_size = lax.axis_size("head"), lax.axis_size("seq")
    shard, part = lax.axis_index("seq"), lax.axis_index("head")
    first_entry, last_entry = ancestors[:, 0], ancestors[:, 1]
    use_prev = first_entry >= 0
    use_rand = (last_entry >= 0) & (last_entry != first_entry)
    uses = jnp.stack([use_prev, use_rand], 1).astype(jnp.int32)
    info = jnp.concatenate(
        [
            (shard * slots + part * blocks)[None].astype(jnp.int32),
            lax.dynamic_slice_in_dim(uses, part * blocks, blocks, 0).reshape(-1),
        ]
    )
    place = jnp.where(last_entry >= 0, last_entry - (shard - 2) * slots, -1)
    chosen = jnp.where(place >= 0, place, 2 * slots).astype(jnp.int32)
    order = jnp.arange(slots, dtype=jnp.int32)
    earlier = (place[None, :] == place[:, None]) & (order[None, :] < order[:, None])
    same = jnp.max(jnp.where(earlier, order[None, :], -1), axis=1)
    window = jnp.arange(3 * slots, dtype=jnp.int32)
    last = jnp.max(jnp.where(place[None, :] == window[:, None], order[None, :], -1), axis=1)
    links = jnp.concatenate([same, last]).astype(jnp.int32)

    blocked = (blocks, BLOCK, key_rows.shape[1])
    rand, edge, root = gather(
        chosen, key_rows.reshape(blocked), value_rows.reshape(blocked), head_size, seq_size
    )
    attended, query_grad, acc, g_edge, g_rand, g_root = attention(
        info, queries, upstream, key_rows, value_rows, edge, root, rand
    )
    key_grad, value_grad = scatter(links, g_rand, g_edge, g_root, acc, head_size, seq_size)
    return attended, query_grad, key_grad, value_grad


def solution(mesh):
    tokens = P(("seq", "head"), None)
    return jax.shard_map(
        local,
        mesh=mesh,
        in_specs=(tokens, tokens, tokens, tokens, P("seq", None)),
        out_specs=(tokens, tokens, tokens, tokens),
        check_vma=False,
    )
```

```python
import functools
import math

import jax
import jax.numpy as jnp
from jax import lax
from jax.experimental import pallas as pl
from jax.experimental.pallas import tpu as pltpu
from jax.sharding import PartitionSpec as P

HEAD_SIZE = 128
BLOCK = 64
NEGATIVE = -1e30
MESH = pl.DeviceIdType.MESH


def attend(first, use_prev, use_rand, q_tile, up_tile, keys, values, groups):
    scale = HEAD_SIZE ** (-0.5)
    rows = groups * BLOCK
    q = jnp.concatenate(
        [q_tile[:, r * HEAD_SIZE : (r + 1) * HEAD_SIZE] for r in range(groups)], axis=0
    )
    up = jnp.concatenate(
        [up_tile[:, r * HEAD_SIZE : (r + 1) * HEAD_SIZE] for r in range(groups)], axis=0
    )
    up_t = up.T
    scores = lax.dot_general(
        keys, q, (((1,), (1,)), ((), ())), preferred_element_type=jnp.float32
    ) * (scale * math.log2(math.e))
    key_at = lax.broadcasted_iota(jnp.int32, (BLOCK, rows), 0)
    query_at = lax.broadcasted_iota(jnp.int32, (BLOCK, rows), 1) & (BLOCK - 1)
    causal = key_at <= query_at
    never = jnp.float32(NEGATIVE)
    zero = jnp.float32(0.0)
    root_off = jnp.where(causal, zero, jnp.where(first, never, zero))
    own_off = jnp.where(causal, jnp.where(first, never, zero), never)
    prev_off = jnp.where(use_prev, zero, never)
    rand_off = jnp.where(use_rand, zero, never)
    scores = jnp.concatenate(
        [
            scores[:BLOCK] + root_off,
            scores[BLOCK : 2 * BLOCK] + own_off,
            scores[2 * BLOCK : 3 * BLOCK] + prev_off,
            scores[3 * BLOCK :] + rand_off,
        ],
        axis=0,
    )
    top = jnp.max(scores, axis=0, keepdims=True)
    weights = jnp.exp2(scores - top)
    total = jnp.sum(weights, axis=0, keepdims=True)
    probs = (weights * (1.0 / total)).astype(jnp.bfloat16)
    att_t = lax.dot_general(
        values, probs, (((0,), (0,)), ((), ())), preferred_element_type=jnp.float32
    ).astype(jnp.bfloat16)
    delta = jnp.sum(
        att_t.astype(jnp.float32) * up_t.astype(jnp.float32), axis=0, keepdims=True
    )
    dprob = lax.dot_general(
        values, up_t, (((1,), (0,)), ((), ())), preferred_element_type=jnp.float32
    )
    dscore = (probs.astype(jnp.float32) * (dprob - delta)).astype(jnp.bfloat16)
    dq_t = lax.dot_general(
        keys, dscore, (((0,), (0,)), ((), ())), preferred_element_type=jnp.float32
    )
    dq = (dq_t * scale).astype(jnp.bfloat16).T
    grads = (
        scale * jnp.dot(dscore, q, preferred_element_type=jnp.float32),
        jnp.dot(probs, up, preferred_element_type=jnp.float32),
    )
    return att_t.T, dq, grads


def chunk_head(i, h, head_size, each):
    z = lax.rem(lax.axis_index("head") + 1 + i, head_size)
    return z, z * each + h


class Chunk:
    def __init__(self, h, each, head_size, info, wide, tokens, kvx, root, rand, grads, scratch):
        self.h, self.each, self.head_size, self.info = h, each, head_size, info
        self.wide, self.tokens, self.kvx, self.root, self.rand = wide, tokens, kvx, root, rand
        self.acc, self.g_edge, self.g_rand, self.g_root = grads
        self.buffers, self.load_sem, self.store_sem = scratch[:4], scratch[4], scratch[5]
        self.blocks = wide[0].shape[0]
        self.width = self.buffers[0].shape[-1]

    def columns(self, i):
        _, g = chunk_head(i, self.h, self.head_size, self.each)
        return pl.ds(pl.multiple_of(g * self.width, self.width), self.width)

    def load(self, i, which):
        return pltpu.make_async_copy(
            self.wide[which].at[:, :, self.columns(i)],
            self.buffers[which].at[i],
            self.load_sem.at[i, which],
        )

    def store(self, i, which):
        return pltpu.make_async_copy(
            self.buffers[2 + which].at[i],
            self.tokens[which].at[:, :, self.columns(i)],
            self.store_sem.at[i, which],
        )

    def start_loads(self):
        for i in range(self.head_size):
            for which in range(2):
                self.load(i, which).start()

    def wait_stores(self):
        for i in range(self.head_size):
            for which in range(2):
                self.store(i, which).wait()

    def run(self, events, after_head):
        blocks = self.blocks
        steps = self.head_size * blocks
        shard, part = lax.axis_index("seq"), lax.axis_index("head")
        at_first = jnp.logical_and(shard == 0, part == 0)
        q_buf, up_buf, att_buf, dq_buf = self.buffers
        groups = self.width // HEAD_SIZE

        def step(t, carry):
            i, j = t // blocks, t % blocks
            z, g = chunk_head(i, self.h, self.head_size, self.each)

            @pl.when(j == 0)
            def _():
                for which in range(2):
                    self.load(i, which).wait()

            here = pl.ds(pl.multiple_of(g * HEAD_SIZE, HEAD_SIZE), HEAD_SIZE)
            keys, values = (
                jnp.concatenate(
                    [
                        self.root[kv, :, here],
                        self.kvx[kv, j + 1, :, here],
                        self.kvx[kv, j, :, here],
                        self.rand[z, kv, j],
                    ],
                    axis=0,
                )
                for kv in range(2)
            )
            att, dq, grads = attend(
                jnp.logical_and(at_first, j == 0),
                self.info[2 * j] > 0,
                self.info[2 * j + 1] > 0,
                q_buf[i, j], up_buf[i, j], keys, values, groups,
            )
            for r in range(groups):
                where = slice(r * HEAD_SIZE, (r + 1) * HEAD_SIZE)
                att_buf[i, j, :, where] = att[r * BLOCK : (r + 1) * BLOCK]
                dq_buf[i, j, :, where] = dq[r * BLOCK : (r + 1) * BLOCK]
            for kv, grad in enumerate(grads):
                self.acc[z, kv, j] = grad[BLOCK : 2 * BLOCK]
                self.g_rand[z, kv, j] = grad[3 * BLOCK :].astype(jnp.bfloat16)

            @pl.when(j == 0)
            def _():
                for kv, grad in enumerate(grads):
                    self.g_root[z, kv] = grad[:BLOCK]
                    self.g_edge[z, kv] = grad[2 * BLOCK : 3 * BLOCK].astype(jnp.bfloat16)

            @pl.when(j > 0)
            def _():
                for kv, grad in enumerate(grads):
                    self.g_root[z, kv] += grad[:BLOCK]
                    self.acc[z, kv, j - 1] += grad[2 * BLOCK : 3 * BLOCK]

            @pl.when(j == blocks - 1)
            def _():
                for which in range(2):
                    self.store(i, which).start()
                after_head(i)

            for at, event in events:
                pl.when(t == at * steps // 16)(event)
            return carry

        lax.fori_loop(0, steps, step, 0)


def grad_shapes(head_size, blocks):
    block = (BLOCK, HEAD_SIZE)
    return [
        ((head_size, 2, blocks) + block, jnp.float32),
        ((head_size, 2) + block, jnp.bfloat16),
        ((head_size, 2, blocks) + block, jnp.bfloat16),
        ((head_size, 2) + block, jnp.float32),
    ]


def chunk_scratch(head_size, blocks, wide):
    return [pltpu.VMEM((head_size, blocks, BLOCK, wide), jnp.bfloat16)] * 4 + [
        pltpu.SemaphoreType.DMA((head_size, 2)),
        pltpu.SemaphoreType.DMA((head_size, 2)),
    ]


def tree_steps(length):
    steps, step = [], 1
    while step < length:
        steps.append(step)
        step *= 2
    return steps


def greet(head_size, seq_size):
    shard, part = lax.axis_index("seq"), lax.axis_index("head")
    barrier = pltpu.get_barrier_semaphore()
    count = 0

    def signal(other):
        pl.semaphore_signal(barrier, inc=1, device_id=other, device_id_type=MESH)

    for d in range(1, head_size):
        signal((shard, lax.rem(part + d, head_size)))
        count += 1
    for step in tree_steps(seq_size):
        signal((lax.rem(shard + step, seq_size), part))
        signal((lax.rem(shard + seq_size - step, seq_size), part))
        count += 2
    after, before = lax.rem(shard + 1, seq_size), lax.rem(shard + seq_size - 1, seq_size)

    @pl.when(part == head_size - 1)
    def _():
        signal((after, 0))

    @pl.when(part == 0)
    def _():
        signal((before, head_size - 1))

    at_end = jnp.logical_or(part == 0, part == head_size - 1)
    pl.semaphore_wait(barrier, count + jnp.where(at_end, 1, 0))


def send(source, target, send_sem, recv_sem, other):
    return pltpu.make_async_remote_copy(
        src_ref=source,
        dst_ref=target,
        send_sem=send_sem,
        recv_sem=recv_sem,
        device_id=other,
        device_id_type=MESH,
    )


def rows_of(at, count):
    return pl.ds(at, count)


def gather_kernel(head_size, seq_size, early, each, chosen, info, k_ref, v_ref, q_ref, up_ref, *rest):
    shard, part = lax.axis_index("seq"), lax.axis_index("head")
    blocks, _, width = k_ref.shape
    slots = blocks * head_size
    pieces = 2 * each
    rest = list(rest)

    def take(count):
        taken = rest[:count]
        del rest[:count]
        return taken

    kvx, root = take(2)
    late_rand = take(each - early)
    tokens = take(2 if early else 0)
    grads = [take(4) for _ in range(early)]
    window = take(pieces)
    rand = take(early) + late_rand
    work = take(6 if early else 0)
    (stage, kv_sem, a_send, a_recv, near_send, near_recv, far_send, far_recv,
     b_send, b_recv, edge_send, edge_recv, root_send, root_recv) = rest
    inputs = (k_ref, v_ref)
    seq_steps = tree_steps(seq_size)[::-1]
    after = jnp.minimum(shard + 1, seq_size - 1)
    has_after, has_before = shard + 1 < seq_size, shard > 0
    at_first = jnp.logical_and(shard == 0, part == 0)
    chunks = [
        Chunk(h, each, head_size, info, (q_ref, up_ref), tokens, kvx, root, rand[h], grads[h], work)
        for h in range(early)
    ]

    def columns(p, c):
        return pl.ds(pl.multiple_of((p * each + c // 2) * HEAD_SIZE, HEAD_SIZE), HEAD_SIZE)

    def kv_load(kv):
        return pltpu.make_async_copy(inputs[kv], kvx.at[kv, pl.ds(1, blocks)], kv_sem.at[kv])

    for kv in range(2):
        kv_load(kv).start()
    greet(head_size, seq_size)

    def slice_out(d, c):
        other = lax.rem(part + d, head_size)
        return send(
            inputs[c % 2].at[:, :, columns(other, c)],
            window[c].at[rows_of(2 * slots + part * blocks, blocks)],
            a_send.at[d, c], a_recv.at[d, c], (shard, other),
        )

    def near_copy(c):
        return send(
            window[c].at[rows_of(2 * slots, slots)], window[c].at[rows_of(slots, slots)],
            near_send.at[c], near_recv.at[c], (after, part),
        )

    def far_copy(c):
        return send(
            window[c].at[rows_of(slots, slots)], window[c].at[rows_of(0, slots)],
            far_send.at[c], far_recv.at[c], (after, part),
        )

    def slice_back(d, c):
        other = lax.rem(part + d, head_size)
        return send(
            stage.at[c, rows_of(other * blocks, blocks)], rand[c // 2].at[part, c % 2],
            b_send.at[d, c], b_recv.at[d, c], (shard, other),
        )

    def edge_copy(kv):
        last = part == head_size - 1
        other = (jnp.where(last, after, shard), jnp.where(last, 0, part + 1))
        return send(
            inputs[kv].at[blocks - 1], kvx.at[kv, 0], edge_send.at[kv], edge_recv.at[kv], other
        )

    gives_edge = jnp.logical_or(part < head_size - 1, has_after)
    gets_edge = jnp.logical_or(part > 0, has_before)

    def root_over_head(z):
        return send(root, root, root_send.at[z - 1], root_recv.at[z - 1], (shard, z))

    def root_over_seq(e):
        step = seq_steps[e]
        other = jnp.minimum(shard + step, seq_size - 1)
        at = head_size - 1 + e
        copy = send(root, root, root_send.at[at], root_recv.at[at], (other, part))
        turn = lax.rem(shard, 2 * step)
        gives = jnp.logical_and(turn == 0, shard + step < seq_size)
        return copy, gives, turn == step

    def root_event(e):
        if e == 0:

            @pl.when(jnp.logical_and(shard == 0, part > 0))
            def _():
                root_over_head(jnp.maximum(part, 1)).wait_recv()

        elif e <= len(seq_steps):
            copy, _, gets = root_over_seq(e - 1)
            pl.when(gets)(copy.wait_recv)
        if e < len(seq_steps):
            copy, gives, _ = root_over_seq(e)
            pl.when(gives)(copy.start)

    def start_slices(c):
        for d in range(1, head_size):
            slice_out(d, c).start()

    for c in range(2):
        start_slices(c)
    for kv in range(2):
        pl.when(gives_edge)(edge_copy(kv).start)
        kv_load(kv).wait()

    @pl.when(at_first)
    def _():
        for kv in range(2):
            root[kv] = kvx[kv, 1]
        for z in range(1, head_size):
            root_over_head(z).start()

    for chunk in chunks[:1]:
        chunk.start_loads()
    for c in range(pieces):
        window[c][rows_of(2 * slots + part * blocks, blocks)] = kvx[
            c % 2, 1:, :, columns(part, c)
        ]

    @pl.when(jnp.logical_not(gets_edge))
    def _():
        for kv in range(2):
            kvx[kv, 0] = kvx[kv, 1]

    def pass_on(c):
        for d in range(1, head_size):
            slice_out(d, c).wait_recv()
        if c + 2 < pieces:
            start_slices(c + 2)
        pl.when(has_after)(near_copy(c).start)

    def relay(c):
        pl.when(has_before)(near_copy(c).wait_recv)
        pl.when(jnp.logical_and(has_before, has_after))(far_copy(c).start)

    def pick(c):
        pl.when(shard > 1)(far_copy(c).wait_recv)
        for d in range(1, head_size):
            other = lax.rem(part + d, head_size)
            for n in range(blocks):
                stage[c, other * blocks + n] = window[c][chosen[other * blocks + n]]
            slice_back(d, c).start()
        for n in range(blocks):
            rand[c // 2][part, c % 2, n] = window[c][chosen[part * blocks + n]]

    def arrive(c):
        for d in range(1, head_size):
            slice_back(d, c).wait_recv()

    done = 0
    for at in range(pieces + 1):
        if at >= 2:
            pick(at - 2)
        if at >= 1:
            relay(at - 1)
        if at < pieces:
            pass_on(at)
        if at >= 1:
            root_event(done)
            done += 1
    while done <= len(seq_steps):
        root_event(done)
        done += 1
    for kv in range(2):
        pl.when(gets_edge)(edge_copy(kv).wait_recv)
    arrived = 0
    for h, chunk in enumerate(chunks):
        for c in range(arrived, 2 * h + 2):
            arrive(c)
        arrived = 2 * h + 2
        if h > 0:
            chunks[h - 1].wait_stores()
            chunk.start_loads()
        chunk.run([(2, functools.partial(pick, pieces - 1))] if h == 0 else [], lambda i: None)
    if not chunks:
        pick(pieces - 1)
    for c in range(arrived, pieces):
        arrive(c)
    for chunk in chunks[-1:]:
        chunk.wait_stores()
    for c in range(pieces):
        for d in range(1, head_size):
            slice_out(d, c).wait_send()
            slice_back(d, c).wait_send()
        pl.when(has_after)(near_copy(c).wait_send)
        pl.when(jnp.logical_and(has_before, has_after))(far_copy(c).wait_send)
    for kv in range(2):
        pl.when(gives_edge)(edge_copy(kv).wait_send)
    for e in range(len(seq_steps)):
        copy, gives, _ = root_over_seq(e)
        pl.when(gives)(copy.wait_send)

    @pl.when(at_first)
    def _():
        for z in range(1, head_size):
            root_over_head(z).wait_send()


def gather(chosen, info, key_rows, value_rows, queries, upstream, head_size, seq_size, early):
    blocks, _, width = key_rows.shape
    heads = width // HEAD_SIZE
    each = heads // head_size
    pieces = 2 * each
    slots = blocks * head_size
    events = head_size - 1 + len(tree_steps(seq_size))
    vmem, smem = pltpu.MemorySpace.VMEM, pltpu.MemorySpace.SMEM
    dma = pltpu.SemaphoreType.DMA
    picked = (head_size, 2, blocks, BLOCK, HEAD_SIZE)
    outs = [((2, blocks + 1, BLOCK, width), jnp.bfloat16), ((2, BLOCK, width), jnp.bfloat16)]
    outs += [(picked, jnp.bfloat16)] * (each - early)
    kinds = [vmem] * len(outs)
    if early:
        outs += [(queries.shape, jnp.bfloat16)] * 2
        kinds += [pl.ANY] * 2
        outs += grad_shapes(head_size, blocks) * early
        kinds += [vmem] * 4 * early
    return pl.pallas_call(
        functools.partial(gather_kernel, head_size, seq_size, early, each),
        in_specs=[pl.BlockSpec(memory_space=smem)] * 2 + [pl.BlockSpec(memory_space=pl.ANY)] * 4,
        out_specs=[pl.BlockSpec(memory_space=kind) for kind in kinds],
        out_shape=[jax.ShapeDtypeStruct(*out) for out in outs],
        scratch_shapes=[
            *[pltpu.VMEM((3 * slots, BLOCK, HEAD_SIZE), jnp.bfloat16)] * pieces,
            *[pltpu.VMEM(picked, jnp.bfloat16)] * early,
            *(chunk_scratch(head_size, blocks, queries.shape[-1] // heads) if early else []),
            pltpu.VMEM((pieces, slots, BLOCK, HEAD_SIZE), jnp.bfloat16),
            dma((2,)),
            dma((head_size, pieces)), dma((head_size, pieces)),
            dma((pieces,)), dma((pieces,)), dma((pieces,)), dma((pieces,)),
            dma((head_size, pieces)), dma((head_size, pieces)),
            dma((2,)), dma((2,)), dma((events,)), dma((events,)),
        ],
        compiler_params=pltpu.CompilerParams(
            collective_id=0, has_side_effects=True, vmem_limit_bytes=32 * 1024 * 1024
        ),
        name="gather",
    )(chosen, info, key_rows, value_rows, queries, upstream)


def scatter_kernel(head_size, seq_size, early, each, links, info, q_ref, up_ref, *rest):
    shard, part = lax.axis_index("seq"), lax.axis_index("head")
    rest = list(rest)

    def take(count):
        taken = rest[:count]
        del rest[:count]
        return taken

    late = each - early
    take(2 if early else 0)
    kvx, root_block = take(2)
    rand = take(late)
    grads = [take(4) for _ in range(early)]
    tokens = take(2)
    outputs = take(2)
    grads += [take(4) for _ in range(late)]
    work = take(6)
    (slots_in, chain, sections, near_in, far_in, back, edge_in, root, root_total, root_box,
     a_send, a_recv, near_send, near_recv, far_send, far_recv,
     b_send, b_recv, edge_send, edge_recv, root_send, root_recv) = rest
    blocks = q_ref.shape[0]
    slots = blocks * head_size
    pieces = 2 * each
    seq_steps = tree_steps(seq_size)
    before = jnp.maximum(shard - 1, 0)
    has_after, has_before = shard + 1 < seq_size, shard > 0
    chunks = [
        Chunk(
            early + n, each, head_size, info, (q_ref, up_ref), tokens, kvx, root_block, rand[n],
            grads[early + n], work,
        )
        for n in range(late)
    ]
    chunks[0].start_loads()
    greet(head_size, seq_size)

    def slice_out(d, c):
        other = lax.rem(part + d, head_size)
        return send(
            grads[c // 2][2].at[other, c % 2],
            slots_in.at[c, rows_of(part * blocks, blocks)],
            a_send.at[d, c], a_recv.at[d, c], (shard, other),
        )

    def far_copy(c):
        return send(
            sections.at[c, rows_of(0, slots)], far_in.at[c],
            far_send.at[c], far_recv.at[c], (before, part),
        )

    def near_copy(c):
        return send(
            sections.at[c, rows_of(slots, slots)], near_in.at[c],
            near_send.at[c], near_recv.at[c], (before, part),
        )

    def slice_back(d, c):
        other = lax.rem(part + d, head_size)
        return send(
            sections.at[c, rows_of(2 * slots + other * blocks, blocks)], back.at[c, part],
            b_send.at[d, c], b_recv.at[d, c], (shard, other),
        )

    def edge_copy(h):
        other = (
            jnp.where(part == 0, before, shard),
            jnp.where(part == 0, head_size - 1, part - 1),
        )
        return send(grads[h][1], edge_in.at[h], edge_send.at[h], edge_recv.at[h], other)

    gives_edge = jnp.logical_or(part > 0, has_before)
    gets_edge = jnp.logical_or(part < head_size - 1, has_after)

    def root_over_seq(h, e):
        step = seq_steps[e]
        other = jnp.maximum(shard - step, 0)
        at = head_size - 1 + e
        copy = send(
            root.at[h], root_box.at[h, at], root_send.at[h, at], root_recv.at[h, at], (other, part)
        )
        turn = lax.rem(shard, 2 * step)
        return copy, turn == step, jnp.logical_and(turn == 0, shard + step < seq_size)

    def root_over_head(h, z):
        return send(
            root.at[h], root_box.at[h, z - 1], root_send.at[h, z - 1], root_recv.at[h, z - 1],
            (shard, 0),
        )

    gives_last = jnp.logical_and(shard == 0, part > 0)

    def root_event(h, e):
        if e == 0:
            root[h] = grads[h][3][...]
        else:
            copy, _, gets = root_over_seq(h, e - 1)

            @pl.when(gets)
            def _():
                copy.wait_recv()
                root[h] += root_box[h, head_size - 1 + e - 1]

        if e < len(seq_steps):
            copy, gives, _ = root_over_seq(h, e)
            pl.when(gives)(copy.start)
        elif e == len(seq_steps):

            @pl.when(gives_last)
            def _():
                root_over_head(h, jnp.maximum(part, 1)).start()

    def keep(c):
        slots_in[c, rows_of(part * blocks, blocks)] = grads[c // 2][2][part, c % 2]

    def section(t):
        at = links[slots + t]
        found = chain[jnp.maximum(at, 0)]
        return jnp.where(at >= 0, found, 0.0).astype(jnp.bfloat16)

    def collect(c):
        for d in range(1, head_size):
            slice_out(d, c).wait_recv()
        for n in range(slots):
            term = slots_in[c, n].astype(jnp.float32)
            if n > 0:
                same = links[n]
                found = chain[jnp.maximum(same, 0)]
                term = term + jnp.where(same >= 0, found, 0.0)
            chain[n] = term
        for t in range(slots):
            sections[c, t] = section(t)
        pl.when(shard > 1)(far_copy(c).start)
        for t in range(slots, 3 * slots):
            sections[c, t] = section(t)

    def add_to(c, where, came):
        sections[c, where] = (
            sections[c, where].astype(jnp.float32) + came[c].astype(jnp.float32)
        ).astype(jnp.bfloat16)

    def relay(c):
        @pl.when(jnp.logical_and(has_before, has_after))
        def _():
            far_copy(c).wait_recv()
            add_to(c, rows_of(slots, slots), far_in)

        pl.when(has_before)(near_copy(c).start)

    def give_back(c):
        @pl.when(has_after)
        def _():
            near_copy(c).wait_recv()
            add_to(c, rows_of(2 * slots, slots), near_in)

        for d in range(1, head_size):
            slice_back(d, c).start()

    part_of = functools.partial
    events, steps = [], len(seq_steps)
    for h in range(early):
        for c in (2 * h, 2 * h + 1):
            for d in range(1, head_size):
                slice_out(d, c).start()
        pl.when(gives_edge)(edge_copy(h).start)
    for h in range(early):
        root_event(h, 0)
        for c in (2 * h, 2 * h + 1):
            keep(c)
        for e in range(1, steps + 1):
            events.append((2 * e + 1, part_of(root_event, h, e)))
        events += [
            (5, part_of(collect, 2 * h)),
            (8, part_of(collect, 2 * h + 1)),
            (9, part_of(relay, 2 * h)),
            (11, part_of(relay, 2 * h + 1)),
            (12, part_of(give_back, 2 * h)),
            (14, part_of(give_back, 2 * h + 1)),
        ]
    events.sort(key=lambda event: event[0])

    for n, chunk in enumerate(chunks):
        h = early + n
        if n > 0:
            chunks[n - 1].wait_stores()
            chunk.start_loads()

        def after_head(i, h=h):
            @pl.when(i < head_size - 1)
            def _():
                for kv in range(2):
                    slice_out(i + 1, 2 * h + kv).start()

        chunk.run(events if n == 0 else [], after_head)
        root_event(h, 0)
        pl.when(gives_edge)(edge_copy(h).start)
        for c in (2 * h, 2 * h + 1):
            keep(c)
    first = 2 * early
    done = 1
    for at in range(first, pieces + 2):
        if first <= at - 2:
            give_back(at - 2)
        if first <= at - 1 < pieces:
            relay(at - 1)
        if at < pieces:
            collect(at)
        if done <= steps:
            for h in range(early, each):
                root_event(h, done)
            done += 1
    while done <= steps:
        for h in range(early, each):
            root_event(h, done)
        done += 1

    root_total[...] = jnp.zeros_like(root_total)
    for h in range(each):
        pl.when(gets_edge)(edge_copy(h).wait_recv)

    @pl.when(jnp.logical_not(gets_edge))
    def _():
        edge_in[...] = jnp.zeros_like(edge_in)

    @pl.when(jnp.logical_and(shard == 0, part == 0))
    def _():
        for h in range(each):
            total = root[h]
            for z in range(1, head_size):
                root_over_head(h, z).wait_recv()
                total += root_box[h, z - 1]
            root_total[h] = total

    def finish(c, z, came):
        h, kv = c // 2, c % 2
        where = pl.ds(pl.multiple_of((z * each + h) * HEAD_SIZE, HEAD_SIZE), HEAD_SIZE)
        for n in range(blocks):
            total = grads[h][0][z, kv, n] + came[n].astype(jnp.float32)
            if n == 0:
                total += root_total[h, z, kv]
            if n == blocks - 1:
                total += edge_in[h, z, kv].astype(jnp.float32)
            outputs[kv][pl.ds(n * BLOCK, BLOCK), where] = total.astype(jnp.bfloat16)

    for c in range(pieces):
        finish(c, part, sections.at[c, rows_of(2 * slots + part * blocks, blocks)])
        for d in range(1, head_size):
            came = lax.rem(part + head_size - d, head_size)
            slice_back(d, c).wait_recv()
            finish(c, came, back.at[c, came])
    chunks[-1].wait_stores()
    for c in range(pieces):
        for d in range(1, head_size):
            slice_out(d, c).wait_send()
            slice_back(d, c).wait_send()
        pl.when(shard > 1)(far_copy(c).wait_send)
        pl.when(has_before)(near_copy(c).wait_send)
    for h in range(each):
        pl.when(gives_edge)(edge_copy(h).wait_send)
        for e in range(steps):
            copy, gives, _ = root_over_seq(h, e)
            pl.when(gives)(copy.wait_send)

    @pl.when(gives_last)
    def _():
        for h in range(each):
            root_over_head(h, jnp.maximum(part, 1)).wait_send()


def scatter(links, info, queries, upstream, gathered, head_size, seq_size, early):
    kvx, root = gathered[:2]
    blocks = queries.shape[0]
    width = root.shape[-1]
    heads = width // HEAD_SIZE
    each = heads // head_size
    late = each - early
    rand, gathered = gathered[2 : 2 + late], gathered[2 + late :]
    pieces = 2 * each
    slots = blocks * head_size
    events = head_size - 1 + len(tree_steps(seq_size))
    vmem, smem = pltpu.MemorySpace.VMEM, pltpu.MemorySpace.SMEM
    dma = pltpu.SemaphoreType.DMA
    box = pltpu.VMEM((pieces, slots, BLOCK, HEAD_SIZE), jnp.bfloat16)
    edge = (head_size, 2, BLOCK, HEAD_SIZE)
    operands = [links, info, queries, upstream]
    kinds = [smem, smem, pl.ANY, pl.ANY]
    aliases = {}
    if early:
        aliases = {4: 0, 5: 1}
        operands += gathered[:2]
        kinds += [pl.ANY] * 2
        gathered = gathered[2:]
    rest = [kvx, root, *rand, *gathered]
    operands += rest
    kinds += [vmem] * len(rest)
    return pl.pallas_call(
        functools.partial(scatter_kernel, head_size, seq_size, early, each),
        in_specs=[pl.BlockSpec(memory_space=kind) for kind in kinds],
        out_specs=[pl.BlockSpec(memory_space=pl.ANY)] * 2 + [pl.BlockSpec(memory_space=vmem)] * 2,
        out_shape=[jax.ShapeDtypeStruct(queries.shape, jnp.bfloat16)] * 2
        + [jax.ShapeDtypeStruct((blocks * BLOCK, width), jnp.bfloat16)] * 2,
        input_output_aliases=aliases,
        scratch_shapes=[
            *[pltpu.VMEM(*shape) for shape in grad_shapes(head_size, blocks) * late],
            *chunk_scratch(head_size, blocks, queries.shape[-1] // heads),
            box,
            pltpu.VMEM((slots, BLOCK, HEAD_SIZE), jnp.float32),
            pltpu.VMEM((pieces, 3 * slots, BLOCK, HEAD_SIZE), jnp.bfloat16),
            box,
            box,
            pltpu.VMEM((pieces, head_size, blocks, BLOCK, HEAD_SIZE), jnp.bfloat16),
            pltpu.VMEM((each,) + edge, jnp.bfloat16),
            pltpu.VMEM((each,) + edge, jnp.float32),
            pltpu.VMEM((each,) + edge, jnp.float32),
            pltpu.VMEM((each, events) + edge, jnp.float32),
            dma((head_size, pieces)), dma((head_size, pieces)),
            dma((pieces,)), dma((pieces,)), dma((pieces,)), dma((pieces,)),
            dma((head_size, pieces)), dma((head_size, pieces)),
            dma((each,)), dma((each,)), dma((each, events)), dma((each, events)),
        ],
        compiler_params=pltpu.CompilerParams(
            collective_id=1, has_side_effects=True, vmem_limit_bytes=40 * 1024 * 1024
        ),
        name="scatter",
    )(*operands)


def local(queries, key_rows, value_rows, upstream, ancestors):
    tokens, _ = key_rows.shape
    blocks = tokens // BLOCK
    slots = ancestors.shape[0]
    head_size, seq_size = lax.axis_size("head"), lax.axis_size("seq")
    shard, part = lax.axis_index("seq"), lax.axis_index("head")
    first_entry, last_entry = ancestors[:, 0], ancestors[:, 1]
    use_prev = first_entry >= 0
    use_rand = (last_entry >= 0) & (last_entry != first_entry)
    uses = jnp.stack([use_prev, use_rand], 1).astype(jnp.int32)
    info = lax.dynamic_slice_in_dim(uses, part * blocks, blocks, 0).reshape(-1)
    place = jnp.where(last_entry >= 0, last_entry - (shard - 2) * slots, -1)
    chosen = jnp.where(place >= 0, place, 2 * slots).astype(jnp.int32)
    order = jnp.arange(slots, dtype=jnp.int32)
    earlier = (place[None, :] == place[:, None]) & (order[None, :] < order[:, None])
    same = jnp.max(jnp.where(earlier, order[None, :], -1), axis=1)
    window = jnp.arange(3 * slots, dtype=jnp.int32)
    last = jnp.max(jnp.where(place[None, :] == window[:, None], order[None, :], -1), axis=1)
    links = jnp.concatenate([same, last]).astype(jnp.int32)

    def blocked(x):
        return x.reshape(blocks, BLOCK, x.shape[1])

    queries, upstream = blocked(queries), blocked(upstream)
    early = key_rows.shape[1] // HEAD_SIZE // head_size // 2
    gathered = gather(
        chosen, info, blocked(key_rows), blocked(value_rows), queries, upstream,
        head_size, seq_size, early,
    )
    attended, query_grad, key_grad, value_grad = scatter(
        links, info, queries, upstream, gathered, head_size, seq_size, early
    )
    wide = queries.shape[-1]
    return attended.reshape(tokens, wide), query_grad.reshape(tokens, wide), key_grad, value_grad


def solution(mesh):
    tokens = P(("seq", "head"), None)
    return jax.shard_map(
        local,
        mesh=mesh,
        in_specs=(tokens, tokens, tokens, tokens, P("seq", None)),
        out_specs=(tokens, tokens, tokens, tokens),
        check_vma=False,
    )
```

```python
import functools
import math

import jax
import jax.numpy as jnp
from jax import lax
from jax.experimental import pallas as pl
from jax.experimental.pallas import tpu as pltpu
from jax.sharding import PartitionSpec as P

HEAD_SIZE = 128
BLOCK = 64
NEGATIVE = -1e30
MESH = pl.DeviceIdType.MESH


def attend(first, use_prev, use_rand, q_tile, up_tile, keys, values, groups):
    scale = HEAD_SIZE ** (-0.5)
    rows = groups * BLOCK
    q = jnp.concatenate(
        [q_tile[:, r * HEAD_SIZE : (r + 1) * HEAD_SIZE] for r in range(groups)], axis=0
    )
    up = jnp.concatenate(
        [up_tile[:, r * HEAD_SIZE : (r + 1) * HEAD_SIZE] for r in range(groups)], axis=0
    )
    up_t = up.T
    scores = lax.dot_general(
        keys, q, (((1,), (1,)), ((), ())), preferred_element_type=jnp.float32
    ) * (scale * math.log2(math.e))
    key_at = lax.broadcasted_iota(jnp.int32, (BLOCK, rows), 0)
    query_at = lax.broadcasted_iota(jnp.int32, (BLOCK, rows), 1) & (BLOCK - 1)
    causal = key_at <= query_at
    never = jnp.float32(NEGATIVE)
    zero = jnp.float32(0.0)
    root_off = jnp.where(causal, zero, jnp.where(first, never, zero))
    own_off = jnp.where(causal, jnp.where(first, never, zero), never)
    prev_off = jnp.where(use_prev, zero, never)
    rand_off = jnp.where(use_rand, zero, never)
    scores = jnp.concatenate(
        [
            scores[:BLOCK] + root_off,
            scores[BLOCK : 2 * BLOCK] + own_off,
            scores[2 * BLOCK : 3 * BLOCK] + prev_off,
            scores[3 * BLOCK :] + rand_off,
        ],
        axis=0,
    )
    top = jnp.max(scores, axis=0, keepdims=True)
    weights = jnp.exp2(scores - top)
    total = jnp.sum(weights, axis=0, keepdims=True)
    probs = (weights * (1.0 / total)).astype(jnp.bfloat16)
    att_t = lax.dot_general(
        values, probs, (((0,), (0,)), ((), ())), preferred_element_type=jnp.float32
    ).astype(jnp.bfloat16)
    delta = jnp.sum(
        att_t.astype(jnp.float32) * up_t.astype(jnp.float32), axis=0, keepdims=True
    )
    dprob = lax.dot_general(
        values, up_t, (((1,), (0,)), ((), ())), preferred_element_type=jnp.float32
    )
    dscore = (probs.astype(jnp.float32) * (dprob - delta)).astype(jnp.bfloat16)
    dq_t = lax.dot_general(
        keys, dscore, (((0,), (0,)), ((), ())), preferred_element_type=jnp.float32
    )
    dq = (dq_t * scale).astype(jnp.bfloat16).T
    grads = (
        scale * jnp.dot(dscore, q, preferred_element_type=jnp.float32),
        jnp.dot(probs, up, preferred_element_type=jnp.float32),
    )
    return att_t.T, dq, grads


def chunk_head(i, h, head_size, each):
    z = lax.rem(lax.axis_index("head") + 1 + i, head_size)
    return z, z * each + h


class Chunk:
    def __init__(self, h, each, head_size, info, wide, tokens, kvx, root, rand, grads, scratch):
        self.h, self.each, self.head_size, self.info = h, each, head_size, info
        self.wide, self.tokens, self.kvx, self.root, self.rand = wide, tokens, kvx, root, rand
        self.acc, self.g_edge, self.g_rand, self.g_root = grads
        self.buffers, self.load_sem, self.store_sem = scratch[:4], scratch[4], scratch[5]
        self.blocks = wide[0].shape[0]
        self.width = self.buffers[0].shape[-1]

    def columns(self, i):
        _, g = chunk_head(i, self.h, self.head_size, self.each)
        return pl.ds(pl.multiple_of(g * self.width, self.width), self.width)

    def load(self, i, which):
        return pltpu.make_async_copy(
            self.wide[which].at[:, :, self.columns(i)],
            self.buffers[which].at[i],
            self.load_sem.at[i, which],
        )

    def store(self, i, which):
        return pltpu.make_async_copy(
            self.buffers[2 + which].at[i],
            self.tokens[which].at[:, :, self.columns(i)],
            self.store_sem.at[i, which],
        )

    def start_loads(self):
        for i in range(self.head_size):
            for which in range(2):
                self.load(i, which).start()

    def wait_stores(self):
        for i in range(self.head_size):
            for which in range(2):
                self.store(i, which).wait()

    def run(self, events, after_head):
        blocks = self.blocks
        steps = self.head_size * blocks
        shard, part = lax.axis_index("seq"), lax.axis_index("head")
        at_first = jnp.logical_and(shard == 0, part == 0)
        q_buf, up_buf, att_buf, dq_buf = self.buffers
        groups = self.width // HEAD_SIZE

        def step(t, carry):
            i, j = t // blocks, t % blocks
            z, g = chunk_head(i, self.h, self.head_size, self.each)

            @pl.when(j == 0)
            def _():
                for which in range(2):
                    self.load(i, which).wait()

            here = pl.ds(pl.multiple_of(g * HEAD_SIZE, HEAD_SIZE), HEAD_SIZE)
            keys, values = (
                jnp.concatenate(
                    [
                        self.root[kv, :, here],
                        self.kvx[kv, j + 1, :, here],
                        self.kvx[kv, j, :, here],
                        self.rand[z, kv, j],
                    ],
                    axis=0,
                )
                for kv in range(2)
            )
            att, dq, grads = attend(
                jnp.logical_and(at_first, j == 0),
                self.info[2 * j] > 0,
                self.info[2 * j + 1] > 0,
                q_buf[i, j], up_buf[i, j], keys, values, groups,
            )
            for r in range(groups):
                where = slice(r * HEAD_SIZE, (r + 1) * HEAD_SIZE)
                att_buf[i, j, :, where] = att[r * BLOCK : (r + 1) * BLOCK]
                dq_buf[i, j, :, where] = dq[r * BLOCK : (r + 1) * BLOCK]
            for kv, grad in enumerate(grads):
                self.acc[z, kv, j] = grad[BLOCK : 2 * BLOCK]
                self.g_rand[z, kv, j] = grad[3 * BLOCK :].astype(jnp.bfloat16)

            @pl.when(j == 0)
            def _():
                for kv, grad in enumerate(grads):
                    self.g_root[z, kv] = grad[:BLOCK]
                    self.g_edge[z, kv] = grad[2 * BLOCK : 3 * BLOCK].astype(jnp.bfloat16)

            @pl.when(j > 0)
            def _():
                for kv, grad in enumerate(grads):
                    self.g_root[z, kv] += grad[:BLOCK]
                    self.acc[z, kv, j - 1] += grad[2 * BLOCK : 3 * BLOCK]

            @pl.when(j == blocks - 1)
            def _():
                for which in range(2):
                    self.store(i, which).start()
                after_head(i)

            for at, event in events:
                pl.when(t == at * steps // 16)(event)
            return carry

        lax.fori_loop(0, steps, step, 0)


def grad_shapes(head_size, blocks):
    block = (BLOCK, HEAD_SIZE)
    return [
        ((head_size, 2, blocks) + block, jnp.float32),
        ((head_size, 2) + block, jnp.bfloat16),
        ((head_size, 2, blocks) + block, jnp.bfloat16),
        ((head_size, 2) + block, jnp.float32),
    ]


def chunk_scratch(head_size, blocks, wide):
    return [pltpu.VMEM((head_size, blocks, BLOCK, wide), jnp.bfloat16)] * 4 + [
        pltpu.SemaphoreType.DMA((head_size, 2)),
        pltpu.SemaphoreType.DMA((head_size, 2)),
    ]


def tree_steps(length):
    steps, step = [], 1
    while step < length:
        steps.append(step)
        step *= 2
    return steps


def greet(head_size, seq_size):
    shard, part = lax.axis_index("seq"), lax.axis_index("head")
    barrier = pltpu.get_barrier_semaphore()
    count = 0

    def signal(other):
        pl.semaphore_signal(barrier, inc=1, device_id=other, device_id_type=MESH)

    for d in range(1, head_size):
        signal((shard, lax.rem(part + d, head_size)))
        count += 1
    for step in tree_steps(seq_size):
        signal((lax.rem(shard + step, seq_size), part))
        signal((lax.rem(shard + seq_size - step, seq_size), part))
        count += 2
    after, before = lax.rem(shard + 1, seq_size), lax.rem(shard + seq_size - 1, seq_size)

    @pl.when(part == head_size - 1)
    def _():
        signal((after, 0))

    @pl.when(part == 0)
    def _():
        signal((before, head_size - 1))

    at_end = jnp.logical_or(part == 0, part == head_size - 1)
    pl.semaphore_wait(barrier, count + jnp.where(at_end, 1, 0))


def send(source, target, send_sem, recv_sem, other):
    return pltpu.make_async_remote_copy(
        src_ref=source,
        dst_ref=target,
        send_sem=send_sem,
        recv_sem=recv_sem,
        device_id=other,
        device_id_type=MESH,
    )


def rows_of(at, count):
    return pl.ds(at, count)


def fetch_steps(head_size, seq_size, each, chosen, inputs, window, rand, kvx, root, kv_load, scratch):
    shard, part = lax.axis_index("seq"), lax.axis_index("head")
    blocks = inputs[0].shape[0]
    slots = blocks * head_size
    pieces = 2 * each
    (stage, a_send, a_recv, near_send, near_recv, far_send, far_recv,
     b_send, b_recv, edge_send, edge_recv, root_send, root_recv) = scratch
    seq_steps = tree_steps(seq_size)[::-1]
    after = jnp.minimum(shard + 1, seq_size - 1)
    has_after, has_before = shard + 1 < seq_size, shard > 0
    at_first = jnp.logical_and(shard == 0, part == 0)

    def columns(p, c):
        return pl.ds(pl.multiple_of((p * each + c // 2) * HEAD_SIZE, HEAD_SIZE), HEAD_SIZE)

    def slice_out(d, c):
        other = lax.rem(part + d, head_size)
        return send(
            inputs[c % 2].at[:, :, columns(other, c)],
            window[c].at[rows_of(2 * slots + part * blocks, blocks)],
            a_send.at[d, c], a_recv.at[d, c], (shard, other),
        )

    def near_copy(c):
        return send(
            window[c].at[rows_of(2 * slots, slots)], window[c].at[rows_of(slots, slots)],
            near_send.at[c], near_recv.at[c], (after, part),
        )

    def far_copy(c):
        return send(
            window[c].at[rows_of(slots, slots)], window[c].at[rows_of(0, slots)],
            far_send.at[c], far_recv.at[c], (after, part),
        )

    def slice_back(d, c):
        other = lax.rem(part + d, head_size)
        return send(
            stage.at[c, rows_of(other * blocks, blocks)], rand[c // 2].at[part, c % 2],
            b_send.at[d, c], b_recv.at[d, c], (shard, other),
        )

    def edge_copy(kv):
        last = part == head_size - 1
        other = (jnp.where(last, after, shard), jnp.where(last, 0, part + 1))
        return send(
            inputs[kv].at[blocks - 1], kvx.at[kv, 0], edge_send.at[kv], edge_recv.at[kv], other
        )

    gives_edge = jnp.logical_or(part < head_size - 1, has_after)
    gets_edge = jnp.logical_or(part > 0, has_before)

    def root_over_head(z):
        return send(root, root, root_send.at[z - 1], root_recv.at[z - 1], (shard, z))

    def root_over_seq(e):
        step = seq_steps[e]
        other = jnp.minimum(shard + step, seq_size - 1)
        at = head_size - 1 + e
        copy = send(root, root, root_send.at[at], root_recv.at[at], (other, part))
        turn = lax.rem(shard, 2 * step)
        gives = jnp.logical_and(turn == 0, shard + step < seq_size)
        return copy, gives, turn == step

    def root_event(e):
        if e == 0:

            @pl.when(jnp.logical_and(shard == 0, part > 0))
            def _():
                root_over_head(jnp.maximum(part, 1)).wait_recv()

        elif e <= len(seq_steps):
            copy, _, gets = root_over_seq(e - 1)
            pl.when(gets)(copy.wait_recv)
        if e < len(seq_steps):
            copy, gives, _ = root_over_seq(e)
            pl.when(gives)(copy.start)

    def start_slices(c):
        for d in range(1, head_size):
            slice_out(d, c).start()

    def begin():
        for c in range(2):
            start_slices(c)
        for kv in range(2):
            pl.when(gives_edge)(edge_copy(kv).start)
            kv_load(kv).wait()

        @pl.when(at_first)
        def _():
            for kv in range(2):
                root[kv] = kvx[kv, 1]
            for z in range(1, head_size):
                root_over_head(z).start()

        for c in range(pieces):
            window[c][rows_of(2 * slots + part * blocks, blocks)] = kvx[
                c % 2, 1:, :, columns(part, c)
            ]

        @pl.when(jnp.logical_not(gets_edge))
        def _():
            for kv in range(2):
                kvx[kv, 0] = kvx[kv, 1]

    def pass_on(c):
        for d in range(1, head_size):
            slice_out(d, c).wait_recv()
        if c + 2 < pieces:
            start_slices(c + 2)
        pl.when(has_after)(near_copy(c).start)

    def relay(c):
        pl.when(has_before)(near_copy(c).wait_recv)
        pl.when(jnp.logical_and(has_before, has_after))(far_copy(c).start)

    def pick(c):
        pl.when(shard > 1)(far_copy(c).wait_recv)
        for d in range(1, head_size):
            other = lax.rem(part + d, head_size)
            for n in range(blocks):
                stage[c, other * blocks + n] = window[c][chosen[other * blocks + n]]
            slice_back(d, c).start()
        for n in range(blocks):
            rand[c // 2][part, c % 2, n] = window[c][chosen[part * blocks + n]]

    def arrive(c):
        for d in range(1, head_size):
            slice_back(d, c).wait_recv()

    def finish_edge():
        for kv in range(2):
            pl.when(gets_edge)(edge_copy(kv).wait_recv)

    def drain():
        for c in range(pieces):
            for d in range(1, head_size):
                slice_out(d, c).wait_send()
                slice_back(d, c).wait_send()
            pl.when(has_after)(near_copy(c).wait_send)
            pl.when(jnp.logical_and(has_before, has_after))(far_copy(c).wait_send)
        for kv in range(2):
            pl.when(gives_edge)(edge_copy(kv).wait_send)
        for e in range(len(seq_steps)):
            copy, gives, _ = root_over_seq(e)
            pl.when(gives)(copy.wait_send)

        @pl.when(at_first)
        def _():
            for z in range(1, head_size):
                root_over_head(z).wait_send()

    return begin, pass_on, relay, pick, arrive, root_event, finish_edge, drain


def give_steps(head_size, seq_size, each, links, grads, outputs, scratch):
    shard, part = lax.axis_index("seq"), lax.axis_index("head")
    (slots_in, chain, sections, near_in, far_in, back, edge_in, root, root_total, root_box,
     a_send, a_recv, near_send, near_recv, far_send, far_recv,
     b_send, b_recv, edge_send, edge_recv, root_send, root_recv) = scratch
    blocks = grads[0][0].shape[2]
    slots = blocks * head_size
    pieces = 2 * each
    seq_steps = tree_steps(seq_size)
    steps = len(seq_steps)
    before = jnp.maximum(shard - 1, 0)
    has_after, has_before = shard + 1 < seq_size, shard > 0

    def slice_out(d, c):
        other = lax.rem(part + d, head_size)
        return send(
            grads[c // 2][2].at[other, c % 2],
            slots_in.at[c, rows_of(part * blocks, blocks)],
            a_send.at[d, c], a_recv.at[d, c], (shard, other),
        )

    def far_copy(c):
        return send(
            sections.at[c, rows_of(0, slots)], far_in.at[c],
            far_send.at[c], far_recv.at[c], (before, part),
        )

    def near_copy(c):
        return send(
            sections.at[c, rows_of(slots, slots)], near_in.at[c],
            near_send.at[c], near_recv.at[c], (before, part),
        )

    def slice_back(d, c):
        other = lax.rem(part + d, head_size)
        return send(
            sections.at[c, rows_of(2 * slots + other * blocks, blocks)], back.at[c, part],
            b_send.at[d, c], b_recv.at[d, c], (shard, other),
        )

    def edge_copy(h):
        other = (
            jnp.where(part == 0, before, shard),
            jnp.where(part == 0, head_size - 1, part - 1),
        )
        return send(grads[h][1], edge_in.at[h], edge_send.at[h], edge_recv.at[h], other)

    gives_edge = jnp.logical_or(part > 0, has_before)
    gets_edge = jnp.logical_or(part < head_size - 1, has_after)

    def root_over_seq(h, e):
        step = seq_steps[e]
        other = jnp.maximum(shard - step, 0)
        at = head_size - 1 + e
        copy = send(
            root.at[h], root_box.at[h, at], root_send.at[h, at], root_recv.at[h, at], (other, part)
        )
        turn = lax.rem(shard, 2 * step)
        return copy, turn == step, jnp.logical_and(turn == 0, shard + step < seq_size)

    def root_over_head(h, z):
        return send(
            root.at[h], root_box.at[h, z - 1], root_send.at[h, z - 1], root_recv.at[h, z - 1],
            (shard, 0),
        )

    gives_last = jnp.logical_and(shard == 0, part > 0)

    def root_event(h, e):
        if e == 0:
            root[h] = grads[h][3][...]
        else:
            copy, _, gets = root_over_seq(h, e - 1)

            @pl.when(gets)
            def _():
                copy.wait_recv()
                root[h] += root_box[h, head_size - 1 + e - 1]

        if e < len(seq_steps):
            copy, gives, _ = root_over_seq(h, e)
            pl.when(gives)(copy.start)
        elif e == len(seq_steps):

            @pl.when(gives_last)
            def _():
                root_over_head(h, jnp.maximum(part, 1)).start()

    def keep(c):
        slots_in[c, rows_of(part * blocks, blocks)] = grads[c // 2][2][part, c % 2]

    def section(t):
        at = links[slots + t]
        found = chain[jnp.maximum(at, 0)]
        return jnp.where(at >= 0, found, 0.0).astype(jnp.bfloat16)

    def collect(c):
        for d in range(1, head_size):
            slice_out(d, c).wait_recv()
        for n in range(slots):
            term = slots_in[c, n].astype(jnp.float32)
            if n > 0:
                same = links[n]
                found = chain[jnp.maximum(same, 0)]
                term = term + jnp.where(same >= 0, found, 0.0)
            chain[n] = term
        for t in range(slots):
            sections[c, t] = section(t)
        pl.when(shard > 1)(far_copy(c).start)
        for t in range(slots, 3 * slots):
            sections[c, t] = section(t)

    def add_to(c, where, came):
        sections[c, where] = (
            sections[c, where].astype(jnp.float32) + came[c].astype(jnp.float32)
        ).astype(jnp.bfloat16)

    def relay(c):
        @pl.when(jnp.logical_and(has_before, has_after))
        def _():
            far_copy(c).wait_recv()
            add_to(c, rows_of(slots, slots), far_in)

        pl.when(has_before)(near_copy(c).start)

    def give_back(c):
        @pl.when(has_after)
        def _():
            near_copy(c).wait_recv()
            add_to(c, rows_of(2 * slots, slots), near_in)

        for d in range(1, head_size):
            slice_back(d, c).start()

    def after_head(h, i):
        @pl.when(i < head_size - 1)
        def _():
            for kv in range(2):
                slice_out(i + 1, 2 * h + kv).start()

    def after_chunk(h):
        root_event(h, 0)
        pl.when(gives_edge)(edge_copy(h).start)
        for c in (2 * h, 2 * h + 1):
            keep(c)

    def finish(c, z, came):
        h, kv = c // 2, c % 2
        where = pl.ds(pl.multiple_of((z * each + h) * HEAD_SIZE, HEAD_SIZE), HEAD_SIZE)
        for n in range(blocks):
            total = grads[h][0][z, kv, n] + came[n].astype(jnp.float32)
            if n == 0:
                total += root_total[h, z, kv]
            if n == blocks - 1:
                total += edge_in[h, z, kv].astype(jnp.float32)
            outputs[kv][pl.ds(n * BLOCK, BLOCK), where] = total.astype(jnp.bfloat16)

    def finish_all():
        root_total[...] = jnp.zeros_like(root_total)
        for h in range(each):
            pl.when(gets_edge)(edge_copy(h).wait_recv)

        @pl.when(jnp.logical_not(gets_edge))
        def _():
            edge_in[...] = jnp.zeros_like(edge_in)

        @pl.when(jnp.logical_and(shard == 0, part == 0))
        def _():
            for h in range(each):
                total = root[h]
                for z in range(1, head_size):
                    root_over_head(h, z).wait_recv()
                    total += root_box[h, z - 1]
                root_total[h] = total

        for c in range(pieces):
            finish(c, part, sections.at[c, rows_of(2 * slots + part * blocks, blocks)])
            for d in range(1, head_size):
                came = lax.rem(part + head_size - d, head_size)
                slice_back(d, c).wait_recv()
                finish(c, came, back.at[c, came])

    def drain():
        for c in range(pieces):
            for d in range(1, head_size):
                slice_out(d, c).wait_send()
                slice_back(d, c).wait_send()
            pl.when(shard > 1)(far_copy(c).wait_send)
            pl.when(has_before)(near_copy(c).wait_send)
        for h in range(each):
            pl.when(gives_edge)(edge_copy(h).wait_send)
            for e in range(steps):
                copy, gives, _ = root_over_seq(h, e)
                pl.when(gives)(copy.wait_send)

        @pl.when(gives_last)
        def _():
            for h in range(each):
                root_over_head(h, jnp.maximum(part, 1)).wait_send()

    return after_head, after_chunk, collect, relay, give_back, root_event, finish_all, drain


def kernel(
    head_size, seq_size, each, chosen, links, info, k_ref, v_ref, q_ref, up_ref,
    att_ref, dq_ref, k_out, v_out, *rest,
):
    shard, part = lax.axis_index("seq"), lax.axis_index("head")
    blocks, _, width = k_ref.shape
    slots = blocks * head_size
    pieces = 2 * each
    rest = list(rest)

    def take(count):
        taken = rest[:count]
        del rest[:count]
        return taken

    window = take(pieces)
    rand = take(each)
    grads = [take(4) for _ in range(each)]
    work = [take(6) for _ in range(each)]
    kvx, root_block, stage = take(3)
    (slots_in, chain, sections, near_in, far_in, back, edge_in, root, root_total,
     root_box) = take(10)
    (kv_sem,) = take(1)
    fetch_sems = take(12)
    inputs, outputs = (k_ref, v_ref), (k_out, v_out)
    chunks = [
        Chunk(
            h, each, head_size, info, (q_ref, up_ref), (att_ref, dq_ref), kvx, root_block, rand[h],
            grads[h], work[h],
        )
        for h in range(each)
    ]

    def kv_load(kv):
        return pltpu.make_async_copy(inputs[kv], kvx.at[kv, pl.ds(1, blocks)], kv_sem.at[kv])

    for kv in range(2):
        kv_load(kv).start()
    greet(head_size, seq_size)
    begin, pass_on, relay, pick, arrive, root_event, finish_edge, drain = fetch_steps(
        head_size, seq_size, each, chosen, inputs, window, rand, kvx, root_block, kv_load,
        [stage, *fetch_sems],
    )
    after_head, after_chunk, collect, give_on, give_back, root_sum, finish_all, drain_grads = (
        give_steps(
            head_size, seq_size, each, links, grads, outputs,
            [slots_in, chain, sections, near_in, far_in, back, edge_in, root, root_total,
             root_box, *rest],
        )
    )
    begin()
    for chunk in chunks:
        chunk.start_loads()
    steps = len(tree_steps(seq_size))
    for at in range(pieces + 1):
        if at >= 2:
            pick(at - 2)
        if at >= 1:
            relay(at - 1)
            root_event(at - 1)
        if at < pieces:
            pass_on(at)
    for e in range(pieces, steps + 1):
        root_event(e)
    finish_edge()
    last = pieces - 1
    if each == 1:
        pick(last)
    do = functools.partial
    for h, chunk in enumerate(chunks):
        for c in (2 * h, 2 * h + 1):
            arrive(c)
        if h == 0:
            events = [(3, do(pick, last))] if each > 1 else []
        else:
            events = [(2 * e + 3, do(root_sum, h - 1, e)) for e in range(2, steps + 1)]
            for n, c in enumerate((2 * h - 2, 2 * h - 1)):
                events += [(2 + 2 * n, do(give_on, c)), (6 + 2 * n, do(give_back, c))]
            events.sort(key=lambda event: event[0])
        chunk.run(events, do(after_head, h))
        after_chunk(h)
        if h < each - 1:
            collect(2 * h)
            root_sum(h, 1)
            collect(2 * h + 1)
    h = each - 1
    collect(2 * h)
    root_sum(h, 1)
    give_on(2 * h)
    collect(2 * h + 1)
    root_sum(h, 2)
    give_back(2 * h)
    give_on(2 * h + 1)
    root_sum(h, 3)
    give_back(2 * h + 1)
    for e in range(4, steps + 1):
        root_sum(h, e)
    finish_all()
    for chunk in chunks:
        chunk.wait_stores()
    drain()
    drain_grads()


def attention(chosen, links, info, key_rows, value_rows, queries, upstream, head_size, seq_size):
    blocks, _, width = key_rows.shape
    heads = width // HEAD_SIZE
    each = heads // head_size
    pieces = 2 * each
    slots = blocks * head_size
    events = head_size - 1 + len(tree_steps(seq_size))
    vmem, smem = pltpu.MemorySpace.VMEM, pltpu.MemorySpace.SMEM
    dma = pltpu.SemaphoreType.DMA
    picked = pltpu.VMEM((head_size, 2, blocks, BLOCK, HEAD_SIZE), jnp.bfloat16)
    box = pltpu.VMEM((pieces, slots, BLOCK, HEAD_SIZE), jnp.bfloat16)
    edge = (head_size, 2, BLOCK, HEAD_SIZE)
    outs = [(queries.shape, jnp.bfloat16)] * 2 + [((blocks * BLOCK, width), jnp.bfloat16)] * 2
    hops = [
        dma((head_size, pieces)), dma((head_size, pieces)),
        dma((pieces,)), dma((pieces,)), dma((pieces,)), dma((pieces,)),
        dma((head_size, pieces)), dma((head_size, pieces)),
    ]
    return pl.pallas_call(
        functools.partial(kernel, head_size, seq_size, each),
        in_specs=[pl.BlockSpec(memory_space=smem)] * 3 + [pl.BlockSpec(memory_space=pl.ANY)] * 4,
        out_specs=[pl.BlockSpec(memory_space=pl.ANY)] * 2 + [pl.BlockSpec(memory_space=vmem)] * 2,
        out_shape=[jax.ShapeDtypeStruct(*out) for out in outs],
        scratch_shapes=[
            *[pltpu.VMEM((3 * slots, BLOCK, HEAD_SIZE), jnp.bfloat16)] * pieces,
            *[picked] * each,
            *[pltpu.VMEM(*shape) for shape in grad_shapes(head_size, blocks) * each],
            *chunk_scratch(head_size, blocks, queries.shape[-1] // heads) * each,
            pltpu.VMEM((2, blocks + 1, BLOCK, width), jnp.bfloat16),
            pltpu.VMEM((2, BLOCK, width), jnp.bfloat16),
            box,
            box,
            pltpu.VMEM((slots, BLOCK, HEAD_SIZE), jnp.float32),
            pltpu.VMEM((pieces, 3 * slots, BLOCK, HEAD_SIZE), jnp.bfloat16),
            box,
            box,
            pltpu.VMEM((pieces, head_size, blocks, BLOCK, HEAD_SIZE), jnp.bfloat16),
            pltpu.VMEM((each,) + edge, jnp.bfloat16),
            pltpu.VMEM((each,) + edge, jnp.float32),
            pltpu.VMEM((each,) + edge, jnp.float32),
            pltpu.VMEM((each, events) + edge, jnp.float32),
            dma((2,)),
            *hops, dma((2,)), dma((2,)), dma((events,)), dma((events,)),
            *hops, dma((each,)), dma((each,)), dma((each, events)), dma((each, events)),
        ],
        compiler_params=pltpu.CompilerParams(
            collective_id=0, has_side_effects=True, vmem_limit_bytes=56 * 1024 * 1024
        ),
        name="attention",
    )(chosen, links, info, key_rows, value_rows, queries, upstream)


def local(queries, key_rows, value_rows, upstream, ancestors):
    tokens, _ = key_rows.shape
    blocks = tokens // BLOCK
    slots = ancestors.shape[0]
    head_size, seq_size = lax.axis_size("head"), lax.axis_size("seq")
    shard, part = lax.axis_index("seq"), lax.axis_index("head")
    first_entry, last_entry = ancestors[:, 0], ancestors[:, 1]
    use_prev = first_entry >= 0
    use_rand = (last_entry >= 0) & (last_entry != first_entry)
    uses = jnp.stack([use_prev, use_rand], 1).astype(jnp.int32)
    info = lax.dynamic_slice_in_dim(uses, part * blocks, blocks, 0).reshape(-1)
    place = jnp.where(last_entry >= 0, last_entry - (shard - 2) * slots, -1)
    chosen = jnp.where(place >= 0, place, 2 * slots).astype(jnp.int32)
    order = jnp.arange(slots, dtype=jnp.int32)
    earlier = (place[None, :] == place[:, None]) & (order[None, :] < order[:, None])
    same = jnp.max(jnp.where(earlier, order[None, :], -1), axis=1)
    window = jnp.arange(3 * slots, dtype=jnp.int32)
    last = jnp.max(jnp.where(place[None, :] == window[:, None], order[None, :], -1), axis=1)
    links = jnp.concatenate([same, last]).astype(jnp.int32)

    def blocked(x):
        return x.reshape(blocks, BLOCK, x.shape[1])

    attended, query_grad, key_grad, value_grad = attention(
        chosen, links, info, blocked(key_rows), blocked(value_rows), blocked(queries),
        blocked(upstream), head_size, seq_size,
    )
    wide = queries.shape[-1]
    return attended.reshape(tokens, wide), query_grad.reshape(tokens, wide), key_grad, value_grad


def solution(mesh):
    tokens = P(("seq", "head"), None)
    return jax.shard_map(
        local,
        mesh=mesh,
        in_specs=(tokens, tokens, tokens, tokens, P("seq", None)),
        out_specs=(tokens, tokens, tokens, tokens),
        check_vma=False,
    )
```

```python
import functools
import math

import jax
import jax.numpy as jnp
from jax import lax
from jax.experimental import pallas as pl
from jax.experimental.pallas import tpu as pltpu
from jax.sharding import PartitionSpec as P

HEAD_SIZE = 128
BLOCK = 64
NEGATIVE = -1e30
MESH = pl.DeviceIdType.MESH


def attend(first, use_prev, use_rand, q_tile, up_tile, keys, values, groups):
    scale = HEAD_SIZE ** (-0.5)
    rows = groups * BLOCK
    q = jnp.concatenate(
        [q_tile[:, r * HEAD_SIZE : (r + 1) * HEAD_SIZE] for r in range(groups)], axis=0
    )
    up = jnp.concatenate(
        [up_tile[:, r * HEAD_SIZE : (r + 1) * HEAD_SIZE] for r in range(groups)], axis=0
    )
    up_t = up.T
    scores = lax.dot_general(
        keys, q, (((1,), (1,)), ((), ())), preferred_element_type=jnp.float32
    ) * (scale * math.log2(math.e))
    key_at = lax.broadcasted_iota(jnp.int32, (BLOCK, rows), 0)
    query_at = lax.broadcasted_iota(jnp.int32, (BLOCK, rows), 1) & (BLOCK - 1)
    causal = key_at <= query_at
    never = jnp.float32(NEGATIVE)
    zero = jnp.float32(0.0)
    root_off = jnp.where(causal, zero, jnp.where(first, never, zero))
    own_off = jnp.where(causal, jnp.where(first, never, zero), never)
    prev_off = jnp.where(use_prev, zero, never)
    rand_off = jnp.where(use_rand, zero, never)
    scores = jnp.concatenate(
        [
            scores[:BLOCK] + root_off,
            scores[BLOCK : 2 * BLOCK] + own_off,
            scores[2 * BLOCK : 3 * BLOCK] + prev_off,
            scores[3 * BLOCK :] + rand_off,
        ],
        axis=0,
    )
    top = jnp.max(scores, axis=0, keepdims=True)
    weights = jnp.exp2(scores - top)
    total = jnp.sum(weights, axis=0, keepdims=True)
    probs = (weights * (1.0 / total)).astype(jnp.bfloat16)
    att_t = lax.dot_general(
        values, probs, (((0,), (0,)), ((), ())), preferred_element_type=jnp.float32
    ).astype(jnp.bfloat16)
    delta = jnp.sum(
        att_t.astype(jnp.float32) * up_t.astype(jnp.float32), axis=0, keepdims=True
    )
    dprob = lax.dot_general(
        values, up_t, (((1,), (0,)), ((), ())), preferred_element_type=jnp.float32
    )
    dscore = (probs.astype(jnp.float32) * (dprob - delta)).astype(jnp.bfloat16)
    dq_t = lax.dot_general(
        keys, dscore, (((0,), (0,)), ((), ())), preferred_element_type=jnp.float32
    )
    dq = (dq_t * scale).astype(jnp.bfloat16).T
    grads = (
        scale * jnp.dot(dscore, q, preferred_element_type=jnp.float32),
        jnp.dot(probs, up, preferred_element_type=jnp.float32),
    )
    return att_t.T, dq, grads


def chunk_head(i, h, head_size, each):
    z = lax.rem(lax.axis_index("head") + 1 + i, head_size)
    return z, z * each + h


class Chunk:
    def __init__(self, h, each, head_size, uses, wide, tokens, kvx, root, rand, grads, scratch):
        self.h, self.each, self.head_size, self.uses = h, each, head_size, uses
        self.wide, self.tokens, self.kvx, self.root, self.rand = wide, tokens, kvx, root, rand
        self.acc, self.g_edge, self.g_rand, self.g_root = grads
        self.buffers, self.load_sem = scratch[:2], scratch[2]
        self.blocks = wide[0].shape[0]
        self.width = self.buffers[0].shape[-1]

    def columns(self, i):
        _, g = chunk_head(i, self.h, self.head_size, self.each)
        return pl.ds(pl.multiple_of(g * self.width, self.width), self.width)

    def load(self, i, which):
        return pltpu.make_async_copy(
            self.wide[which].at[:, :, self.columns(i)],
            self.buffers[which].at[i],
            self.load_sem.at[i, which],
        )

    def start_loads(self):
        for i in range(self.head_size):
            for which in range(2):
                self.load(i, which).start()

    def run(self, events, after_head):
        blocks = self.blocks
        steps = self.head_size * blocks
        shard, part = lax.axis_index("seq"), lax.axis_index("head")
        at_first = jnp.logical_and(shard == 0, part == 0)
        q_buf, up_buf = self.buffers
        att_ref, dq_ref = self.tokens
        groups = self.width // HEAD_SIZE

        def step(t, carry):
            i, j = t // blocks, t % blocks
            z, g = chunk_head(i, self.h, self.head_size, self.each)

            @pl.when(j == 0)
            def _():
                for which in range(2):
                    self.load(i, which).wait()

            here = pl.ds(pl.multiple_of(g * HEAD_SIZE, HEAD_SIZE), HEAD_SIZE)
            mine = slice(self.h * HEAD_SIZE, (self.h + 1) * HEAD_SIZE)
            keys, values = (
                jnp.concatenate(
                    [
                        self.root[z, kv, :, mine],
                        self.kvx[kv, j + 1, :, here],
                        self.kvx[kv, j, :, here],
                        self.rand[z, kv, j],
                    ],
                    axis=0,
                )
                for kv in range(2)
            )
            att, dq, grads = attend(
                jnp.logical_and(at_first, j == 0),
                *self.uses(j),
                q_buf[i, j], up_buf[i, j], keys, values, groups,
            )
            for r in range(groups):
                at = pl.multiple_of((g * groups + r) * HEAD_SIZE, HEAD_SIZE)
                att_ref[j, :, pl.ds(at, HEAD_SIZE)] = att[r * BLOCK : (r + 1) * BLOCK]
                dq_ref[j, :, pl.ds(at, HEAD_SIZE)] = dq[r * BLOCK : (r + 1) * BLOCK]
            for kv, grad in enumerate(grads):
                self.acc[z, kv, j] = grad[BLOCK : 2 * BLOCK]
                self.g_rand[z, kv, j] = grad[3 * BLOCK :].astype(jnp.bfloat16)

            @pl.when(j == 0)
            def _():
                for kv, grad in enumerate(grads):
                    self.g_root[z, kv] = grad[:BLOCK]
                    self.g_edge[z, kv] = grad[2 * BLOCK : 3 * BLOCK].astype(jnp.bfloat16)

            @pl.when(j > 0)
            def _():
                for kv, grad in enumerate(grads):
                    self.g_root[z, kv] += grad[:BLOCK]
                    self.acc[z, kv, j - 1] += grad[2 * BLOCK : 3 * BLOCK]

            @pl.when(j == blocks - 1)
            def _():
                after_head(i)

            for at, event in events:
                pl.when(t == at * steps // 16)(event)
            return carry

        lax.fori_loop(0, steps, step, 0)


def grad_shapes(head_size, blocks):
    block = (BLOCK, HEAD_SIZE)
    return [
        ((head_size, 2, blocks) + block, jnp.float32),
        ((head_size, 2) + block, jnp.bfloat16),
        ((head_size, 2, blocks) + block, jnp.bfloat16),
        ((head_size, 2) + block, jnp.float32),
    ]


def chunk_scratch(head_size, blocks, wide):
    return [pltpu.VMEM((head_size, blocks, BLOCK, wide), jnp.bfloat16)] * 2 + [
        pltpu.SemaphoreType.DMA((head_size, 2)),
    ]


def carrier(q, head_size, seq_size):
    return q * seq_size // head_size


def greet(head_size, seq_size):
    shard, part = lax.axis_index("seq"), lax.axis_index("head")
    barrier = pltpu.get_barrier_semaphore()
    count = 0

    def signal(other):
        pl.semaphore_signal(barrier, inc=1, device_id=other, device_id_type=MESH)

    for d in range(1, head_size):
        signal((shard, lax.rem(part + d, head_size)))
        count += 1
    for d in range(1, seq_size):
        signal((lax.rem(shard + d, seq_size), part))
        count += 1
    after, before = lax.rem(shard + 1, seq_size), lax.rem(shard + seq_size - 1, seq_size)

    @pl.when(part == head_size - 1)
    def _():
        signal((after, 0))

    @pl.when(part == 0)
    def _():
        signal((before, head_size - 1))

    at_end = jnp.logical_or(part == 0, part == head_size - 1)
    pl.semaphore_wait(barrier, count + jnp.where(at_end, 1, 0))


def send(source, target, send_sem, recv_sem, other):
    return pltpu.make_async_remote_copy(
        src_ref=source,
        dst_ref=target,
        send_sem=send_sem,
        recv_sem=recv_sem,
        device_id=other,
        device_id_type=MESH,
    )


def rows_of(at, count):
    return pl.ds(at, count)


def fetch_steps(
    head_size, seq_size, each, chosen, inputs, window, rand, kvx, root, kv_load, scratch
):
    shard, part = lax.axis_index("seq"), lax.axis_index("head")
    blocks = inputs[0].shape[0]
    slots = blocks * head_size
    pieces = 2 * each
    (stage, a_send, a_recv, near_send, near_recv, far_send, far_recv,
     b_send, b_recv, edge_send, edge_recv, out_send, out_recv, up_send, up_recv,
     over_send, over_recv) = scratch
    shares = [carrier(q, head_size, seq_size) for q in range(head_size)]
    stride = seq_size // head_size
    share = shard // stride
    carries = lax.rem(shard, stride) == 0
    after = jnp.minimum(shard + 1, seq_size - 1)
    has_after, has_before = shard + 1 < seq_size, shard > 0
    at_first = jnp.logical_and(shard == 0, part == 0)

    def columns(p, c):
        return pl.ds(pl.multiple_of((p * each + c // 2) * HEAD_SIZE, HEAD_SIZE), HEAD_SIZE)

    def slice_out(d, c):
        other = lax.rem(part + d, head_size)
        return send(
            inputs[c % 2].at[:, :, columns(other, c)],
            window[c].at[rows_of(2 * slots + part * blocks, blocks)],
            a_send.at[d, c], a_recv.at[d, c], (shard, other),
        )

    def near_copy(c):
        return send(
            window[c].at[rows_of(2 * slots, slots)], window[c].at[rows_of(slots, slots)],
            near_send.at[c], near_recv.at[c], (after, part),
        )

    def far_copy(c):
        return send(
            window[c].at[rows_of(slots, slots)], window[c].at[rows_of(0, slots)],
            far_send.at[c], far_recv.at[c], (after, part),
        )

    def slice_back(d, c):
        other = lax.rem(part + d, head_size)
        return send(
            stage.at[c, rows_of(other * blocks, blocks)], rand[c // 2].at[part, c % 2],
            b_send.at[d, c], b_recv.at[d, c], (shard, other),
        )

    def edge_copy(kv):
        last = part == head_size - 1
        other = (jnp.where(last, after, shard), jnp.where(last, 0, part + 1))
        return send(
            inputs[kv].at[blocks - 1], kvx.at[kv, 0], edge_send.at[kv], edge_recv.at[kv], other
        )

    gives_edge = jnp.logical_or(part < head_size - 1, has_after)
    gets_edge = jnp.logical_or(part > 0, has_before)

    def root_out(q):
        return send(
            root.at[q], root.at[q], out_send.at[q], out_recv.at[0], (jnp.int32(shares[q]), part)
        )

    def root_up(z):
        return send(root.at[share], root.at[share], up_send.at[z], up_recv.at[0], (shard, z))

    def root_over(d):
        other = lax.rem(shard + d, seq_size)
        copy = send(
            root.at[share], root.at[share], over_send.at[d], over_recv.at[share], (other, part)
        )
        return copy, jnp.logical_or(part > 0, other > 0)

    def spread():
        for d in range(1, seq_size):
            copy, wanted = root_over(d)
            pl.when(wanted)(copy.start)

    def root_event(e):
        if e == 0:

            @pl.when(jnp.logical_and(carries, part == 0))
            def _():
                pl.when(shard > 0)(root_out(0).wait_recv)
                for z in range(1, head_size):
                    root_up(z).start()
                spread()

        elif e == 1:

            @pl.when(jnp.logical_and(carries, part > 0))
            def _():
                root_up(0).wait_recv()
                spread()

        else:

            @pl.when(jnp.logical_not(at_first))
            def _():
                for q in range(head_size):
                    copy = send(root.at[q], root.at[q], over_send.at[0], over_recv.at[q], (shard, part))
                    pl.when(shard != shares[q])(copy.wait_recv)

    def start_slices(c):
        for d in range(1, head_size):
            slice_out(d, c).start()

    def begin():
        for c in range(2):
            start_slices(c)
        for kv in range(2):
            pl.when(gives_edge)(edge_copy(kv).start)
            kv_load(kv).wait()

        @pl.when(at_first)
        def _():
            for q in range(head_size):
                for kv in range(2):
                    root[q, kv] = kvx[kv, 1, :, q * each * HEAD_SIZE : (q + 1) * each * HEAD_SIZE]
            for q in range(1, head_size):
                root_out(q).start()

        for c in range(pieces):
            window[c][rows_of(2 * slots + part * blocks, blocks)] = kvx[
                c % 2, 1:, :, columns(part, c)
            ]

        @pl.when(jnp.logical_not(gets_edge))
        def _():
            for kv in range(2):
                kvx[kv, 0] = kvx[kv, 1]

    def pass_on(c):
        for d in range(1, head_size):
            slice_out(d, c).wait_recv()
        if c + 2 < pieces:
            start_slices(c + 2)
        pl.when(has_after)(near_copy(c).start)

    def relay(c):
        pl.when(has_before)(near_copy(c).wait_recv)
        pl.when(jnp.logical_and(has_before, has_after))(far_copy(c).start)

    def pick(c):
        pl.when(shard > 1)(far_copy(c).wait_recv)
        for d in range(1, head_size):
            other = lax.rem(part + d, head_size)
            for n in range(blocks):
                stage[c, other * blocks + n] = window[c][chosen(other * blocks + n)]
            slice_back(d, c).start()
        for n in range(blocks):
            rand[c // 2][part, c % 2, n] = window[c][chosen(part * blocks + n)]

    def arrive(c):
        for d in range(1, head_size):
            slice_back(d, c).wait_recv()

    def finish_edge():
        for kv in range(2):
            pl.when(gets_edge)(edge_copy(kv).wait_recv)

    def drain():
        for c in range(pieces):
            for d in range(1, head_size):
                slice_out(d, c).wait_send()
                slice_back(d, c).wait_send()
            pl.when(has_after)(near_copy(c).wait_send)
            pl.when(jnp.logical_and(has_before, has_after))(far_copy(c).wait_send)
        for kv in range(2):
            pl.when(gives_edge)(edge_copy(kv).wait_send)

        @pl.when(at_first)
        def _():
            for q in range(1, head_size):
                root_out(q).wait_send()

        @pl.when(carries)
        def _():
            @pl.when(part == 0)
            def _():
                for z in range(1, head_size):
                    root_up(z).wait_send()

            for d in range(1, seq_size):
                copy, wanted = root_over(d)
                pl.when(wanted)(copy.wait_send)

    return begin, pass_on, relay, pick, arrive, root_event, finish_edge, drain


def give_steps(head_size, seq_size, each, earlier, last, grads, outputs, scratch):
    shard, part = lax.axis_index("seq"), lax.axis_index("head")
    (slots_in, chain, sections, near_in, far_in, back, edge_in, root, root_box, up_box, last_box,
     a_send, a_recv, near_send, near_recv, far_send, far_recv,
     b_send, b_recv, edge_send, edge_recv, over_send, over_recv, up_send, up_recv,
     out_send, out_recv) = scratch
    blocks = grads[0][0].shape[2]
    slots = blocks * head_size
    pieces = 2 * each
    shares = [carrier(q, head_size, seq_size) for q in range(head_size)]
    stride = seq_size // head_size
    share = shard // stride
    carries = lax.rem(shard, stride) == 0
    before = jnp.maximum(shard - 1, 0)
    has_after, has_before = shard + 1 < seq_size, shard > 0

    def slice_out(d, c):
        other = lax.rem(part + d, head_size)
        return send(
            grads[c // 2][2].at[other, c % 2],
            slots_in.at[c, rows_of(part * blocks, blocks)],
            a_send.at[d, c], a_recv.at[d, c], (shard, other),
        )

    def far_copy(c):
        return send(
            sections.at[c, rows_of(0, slots)], far_in.at[c],
            far_send.at[c], far_recv.at[c], (before, part),
        )

    def near_copy(c):
        return send(
            sections.at[c, rows_of(slots, slots)], near_in.at[c],
            near_send.at[c], near_recv.at[c], (before, part),
        )

    def slice_back(d, c):
        other = lax.rem(part + d, head_size)
        return send(
            sections.at[c, rows_of(2 * slots + other * blocks, blocks)], back.at[c, part],
            b_send.at[d, c], b_recv.at[d, c], (shard, other),
        )

    def edge_copy(h):
        other = (
            jnp.where(part == 0, before, shard),
            jnp.where(part == 0, head_size - 1, part - 1),
        )
        return send(grads[h][1], edge_in.at[h], edge_send.at[h], edge_recv.at[h], other)

    gives_edge = jnp.logical_or(part > 0, has_before)
    gets_edge = jnp.logical_or(part < head_size - 1, has_after)

    def root_over(h, q):
        return send(
            grads[h][3].at[q], root_box.at[h, shard], over_send.at[h, q], over_recv.at[h, shard],
            (jnp.int32(shares[q]), part),
        )

    def root_up(h):
        return send(
            root.at[h, share], up_box.at[h, part], up_send.at[h], up_recv.at[h, part], (shard, 0)
        )

    def root_out(h):
        return send(
            root.at[h, share], last_box.at[h, share], out_send.at[h], out_recv.at[h, share], (0, part)
        )

    sends_up = jnp.logical_and(carries, part > 0)
    sends_out = jnp.logical_and(jnp.logical_and(carries, part == 0), shard > 0)

    def landed(box, sem):
        send(box, box, sem, sem, (shard, part)).wait_recv()

    def root_event(h, e):
        if e == 0:
            for q in range(head_size):
                pl.when(shard != shares[q])(root_over(h, q).start)
        elif e == 1:

            @pl.when(carries)
            def _():
                total = grads[h][3][share]
                for d in range(1, seq_size):
                    other = lax.rem(shard + d, seq_size)
                    landed(root_box.at[h, other], over_recv.at[h, other])
                    total += root_box[h, other]
                root[h, share] = total

            pl.when(sends_up)(root_up(h).start)
        else:

            @pl.when(jnp.logical_and(carries, part == 0))
            def _():
                total = root[h, share]
                for z in range(1, head_size):
                    landed(up_box.at[h, z], up_recv.at[h, z])
                    total += up_box[h, z]
                root[h, share] = total

            pl.when(sends_out)(root_out(h).start)

    def keep(c):
        slots_in[c, rows_of(part * blocks, blocks)] = grads[c // 2][2][part, c % 2]

    def section(t):
        at = last[t]
        found = chain[jnp.maximum(at, 0)]
        return jnp.where(at >= 0, found, 0.0).astype(jnp.bfloat16)

    def collect(c):
        for d in range(1, head_size):
            slice_out(d, c).wait_recv()
        for n in range(slots):
            term = slots_in[c, n].astype(jnp.float32)
            if n > 0:
                same = earlier[n]
                found = chain[jnp.maximum(same, 0)]
                term = term + jnp.where(same >= 0, found, 0.0)
            chain[n] = term
        for t in range(slots):
            sections[c, t] = section(t)
        pl.when(shard > 1)(far_copy(c).start)
        for t in range(slots, 3 * slots):
            sections[c, t] = section(t)

    def add_to(c, where, came):
        sections[c, where] = (
            sections[c, where].astype(jnp.float32) + came[c].astype(jnp.float32)
        ).astype(jnp.bfloat16)

    def relay(c):
        @pl.when(jnp.logical_and(has_before, has_after))
        def _():
            far_copy(c).wait_recv()
            add_to(c, rows_of(slots, slots), far_in)

        pl.when(has_before)(near_copy(c).start)

    def give_back(c):
        @pl.when(has_after)
        def _():
            near_copy(c).wait_recv()
            add_to(c, rows_of(2 * slots, slots), near_in)

        for d in range(1, head_size):
            slice_back(d, c).start()

    def after_head(h, i):
        @pl.when(i < head_size - 1)
        def _():
            for kv in range(2):
                slice_out(i + 1, 2 * h + kv).start()

    def after_chunk(h):
        root_event(h, 0)
        pl.when(gives_edge)(edge_copy(h).start)
        for c in (2 * h, 2 * h + 1):
            keep(c)

    def finish(c, z, came):
        h, kv = c // 2, c % 2
        where = pl.ds(pl.multiple_of((z * each + h) * HEAD_SIZE, HEAD_SIZE), HEAD_SIZE)
        for n in range(blocks):
            total = grads[h][0][z, kv, n] + came[n].astype(jnp.float32)
            if n == 0:
                total += root[h, z, kv]
            if n == blocks - 1:
                total += edge_in[h, z, kv].astype(jnp.float32)
            outputs[kv][pl.ds(n * BLOCK, BLOCK), where] = total.astype(jnp.bfloat16)

    def finish_all():
        for h in range(each):
            pl.when(gets_edge)(edge_copy(h).wait_recv)

        @pl.when(jnp.logical_not(gets_edge))
        def _():
            edge_in[...] = jnp.zeros_like(edge_in)

        first = jnp.logical_and(shard == 0, part == 0)

        @pl.when(first)
        def _():
            for h in range(each):
                for q in range(1, head_size):
                    landed(last_box.at[h, q], out_recv.at[h, q])
                    root[h, q] = last_box[h, q]

        @pl.when(jnp.logical_not(first))
        def _():
            for h in range(each):
                pl.when(sends_up)(root_up(h).wait_send)
                pl.when(sends_out)(root_out(h).wait_send)
            root[...] = jnp.zeros_like(root)

        for c in range(pieces):
            finish(c, part, sections.at[c, rows_of(2 * slots + part * blocks, blocks)])
            for d in range(1, head_size):
                came = lax.rem(part + head_size - d, head_size)
                slice_back(d, c).wait_recv()
                finish(c, came, back.at[c, came])

    def drain():
        for c in range(pieces):
            for d in range(1, head_size):
                slice_out(d, c).wait_send()
                slice_back(d, c).wait_send()
            pl.when(shard > 1)(far_copy(c).wait_send)
            pl.when(has_before)(near_copy(c).wait_send)
        for h in range(each):
            pl.when(gives_edge)(edge_copy(h).wait_send)
            for q in range(head_size):
                pl.when(shard != shares[q])(root_over(h, q).wait_send)

    return after_head, after_chunk, collect, relay, give_back, root_event, finish_all, drain


def kernel(
    head_size, seq_size, each, ancestors, k_ref, v_ref, q_ref, up_ref,
    att_ref, dq_ref, k_out, v_out, *rest,
):
    shard, part = lax.axis_index("seq"), lax.axis_index("head")
    blocks, _, width = k_ref.shape
    slots = blocks * head_size
    pieces = 2 * each
    rest = list(rest)

    def take(count):
        taken = rest[:count]
        del rest[:count]
        return taken

    window = take(pieces)
    rand = take(each)
    grads = [take(4) for _ in range(each)]
    work = [take(3) for _ in range(each)]
    kvx, root_block, stage = take(3)
    given = take(11)
    earlier, last = take(2)
    (kv_sem,) = take(1)
    fetch_sems = take(16)
    inputs, outputs = (k_ref, v_ref), (k_out, v_out)
    shard, part = lax.axis_index("seq"), lax.axis_index("head")
    origin = (shard - 2) * slots

    def place(n):
        entry = ancestors[n, 1]
        return jnp.where(entry >= 0, entry - origin, -1)

    def chosen(n):
        at = place(n)
        return jnp.where(at >= 0, at, 2 * slots)

    def uses(j):
        n = part * blocks + j
        first_entry, last_entry = ancestors[n, 0], ancestors[n, 1]
        return first_entry >= 0, jnp.logical_and(last_entry >= 0, last_entry != first_entry)

    def write_links():
        places = [place(n) for n in range(slots)]
        for n in range(slots):
            found = jnp.int32(-1)
            for m in range(n):
                found = jnp.where(places[m] == places[n], m, found)
            earlier[n] = found

        def one(t, carry):
            found = jnp.int32(-1)
            for n in range(slots):
                found = jnp.where(places[n] == t, n, found)
            last[t] = found
            return carry

        lax.fori_loop(0, 3 * slots, one, 0)

    chunks = [
        Chunk(
            h, each, head_size, uses, (q_ref, up_ref), (att_ref, dq_ref), kvx, root_block, rand[h],
            grads[h], work[h],
        )
        for h in range(each)
    ]

    def kv_load(kv):
        return pltpu.make_async_copy(inputs[kv], kvx.at[kv, pl.ds(1, blocks)], kv_sem.at[kv])

    for kv in range(2):
        kv_load(kv).start()
    greet(head_size, seq_size)
    begin, pass_on, relay, pick, arrive, root_event, finish_edge, drain = fetch_steps(
        head_size, seq_size, each, chosen, inputs, window, rand, kvx, root_block, kv_load,
        [stage, *fetch_sems],
    )
    after_head, after_chunk, collect, give_on, give_back, root_sum, finish_all, drain_grads = (
        give_steps(
            head_size, seq_size, each, earlier, last, grads, outputs, [*given, *rest],
        )
    )
    begin()
    for chunk in chunks:
        chunk.start_loads()
    write_links()
    for at in range(pieces + 1):
        if at >= 2:
            pick(at - 2)
        if at >= 1:
            relay(at - 1)
        if at < pieces:
            pass_on(at)
        if at < 2:
            root_event(at)
    root_event(2)
    finish_edge()
    final = pieces - 1
    if each == 1:
        pick(final)
    do = functools.partial
    for h, chunk in enumerate(chunks):
        for c in (2 * h, 2 * h + 1):
            arrive(c)
        if h == 0:
            events = [(3, do(pick, final))] if each > 1 else []
        else:
            events = [(5, do(root_sum, h - 1, 2))]
            for n, c in enumerate((2 * h - 2, 2 * h - 1)):
                events += [(2 + 2 * n, do(give_on, c)), (6 + 2 * n, do(give_back, c))]
            events.sort(key=lambda event: event[0])
        chunk.run(events, do(after_head, h))
        after_chunk(h)
        if h < each - 1:
            collect(2 * h)
            root_sum(h, 1)
            collect(2 * h + 1)
    h = each - 1
    collect(2 * h)
    root_sum(h, 1)
    give_on(2 * h)
    collect(2 * h + 1)
    root_sum(h, 2)
    give_back(2 * h)
    give_on(2 * h + 1)
    give_back(2 * h + 1)
    finish_all()
    drain()
    drain_grads()


def attention(ancestors, key_rows, value_rows, queries, upstream, head_size, seq_size):
    blocks, _, width = key_rows.shape
    heads = width // HEAD_SIZE
    each = heads // head_size
    pieces = 2 * each
    slots = blocks * head_size
    vmem, smem = pltpu.MemorySpace.VMEM, pltpu.MemorySpace.SMEM
    dma = pltpu.SemaphoreType.DMA
    picked = pltpu.VMEM((head_size, 2, blocks, BLOCK, HEAD_SIZE), jnp.bfloat16)
    box = pltpu.VMEM((pieces, slots, BLOCK, HEAD_SIZE), jnp.bfloat16)
    edge = (head_size, 2, BLOCK, HEAD_SIZE)
    outs = [(queries.shape, jnp.bfloat16)] * 2 + [((blocks * BLOCK, width), jnp.bfloat16)] * 2
    hops = [
        dma((head_size, pieces)), dma((head_size, pieces)),
        dma((pieces,)), dma((pieces,)), dma((pieces,)), dma((pieces,)),
        dma((head_size, pieces)), dma((head_size, pieces)),
    ]
    return pl.pallas_call(
        functools.partial(kernel, head_size, seq_size, each),
        in_specs=[pl.BlockSpec(memory_space=smem)] + [pl.BlockSpec(memory_space=pl.ANY)] * 4,
        out_specs=[pl.BlockSpec(memory_space=vmem)] * 4,
        out_shape=[jax.ShapeDtypeStruct(*out) for out in outs],
        scratch_shapes=[
            *[pltpu.VMEM((3 * slots, BLOCK, HEAD_SIZE), jnp.bfloat16)] * pieces,
            *[picked] * each,
            *[pltpu.VMEM(*shape) for shape in grad_shapes(head_size, blocks) * each],
            *chunk_scratch(head_size, blocks, queries.shape[-1] // heads) * each,
            pltpu.VMEM((2, blocks + 1, BLOCK, width), jnp.bfloat16),
            pltpu.VMEM((head_size, 2, BLOCK, each * HEAD_SIZE), jnp.bfloat16),
            box,
            box,
            pltpu.VMEM((slots, BLOCK, HEAD_SIZE), jnp.float32),
            pltpu.VMEM((pieces, 3 * slots, BLOCK, HEAD_SIZE), jnp.bfloat16),
            box,
            box,
            pltpu.VMEM((pieces, head_size, blocks, BLOCK, HEAD_SIZE), jnp.bfloat16),
            pltpu.VMEM((each,) + edge, jnp.bfloat16),
            pltpu.VMEM((each,) + edge, jnp.float32),
            pltpu.VMEM((each, seq_size) + edge[1:], jnp.float32),
            pltpu.VMEM((each,) + edge, jnp.float32),
            pltpu.VMEM((each,) + edge, jnp.float32),
            pltpu.SMEM((slots,), jnp.int32),
            pltpu.SMEM((3 * slots,), jnp.int32),
            dma((2,)),
            *hops, dma((2,)), dma((2,)),
            dma((head_size,)), dma((1,)), dma((head_size,)), dma((1,)),
            dma((seq_size,)), dma((head_size,)),
            *hops, dma((each,)), dma((each,)),
            dma((each, head_size)), dma((each, seq_size)), dma((each,)), dma((each, head_size)),
            dma((each,)), dma((each, head_size)),
        ],
        compiler_params=pltpu.CompilerParams(
            collective_id=0, has_side_effects=True, vmem_limit_bytes=56 * 1024 * 1024
        ),
        name="attention",
    )(ancestors, key_rows, value_rows, queries, upstream)


def deliver_kernel(*refs):
    count = len(refs) // 2
    sems = refs[-1]
    copies = [
        pltpu.make_async_copy(refs[n], refs[count + n], sems.at[n]) for n in range(count)
    ]
    for copy in copies:
        copy.start()
    for copy in copies:
        copy.wait()


def deliver(arrays):
    return pl.pallas_call(
        deliver_kernel,
        in_specs=[pl.BlockSpec(memory_space=pltpu.MemorySpace.VMEM)] * len(arrays),
        out_specs=[pl.BlockSpec(memory_space=pl.ANY)] * len(arrays),
        out_shape=[jax.ShapeDtypeStruct(x.shape, x.dtype) for x in arrays],
        scratch_shapes=[pltpu.SemaphoreType.DMA((len(arrays),))],
        name="deliver",
    )(*arrays)


def local(queries, key_rows, value_rows, upstream, ancestors):
    tokens, _ = key_rows.shape
    blocks = tokens // BLOCK
    head_size, seq_size = lax.axis_size("head"), lax.axis_size("seq")

    def blocked(x):
        return x.reshape(blocks, BLOCK, x.shape[1])

    attended, query_grad, key_grad, value_grad = deliver(
        attention(
            ancestors, blocked(key_rows), blocked(value_rows), blocked(queries),
            blocked(upstream), head_size, seq_size,
        )
    )
    wide = queries.shape[-1]
    return attended.reshape(tokens, wide), query_grad.reshape(tokens, wide), key_grad, value_grad


def solution(mesh):
    tokens = P(("seq", "head"), None)
    return jax.shard_map(
        local,
        mesh=mesh,
        in_specs=(tokens, tokens, tokens, tokens, P("seq", None)),
        out_specs=(tokens, tokens, tokens, tokens),
        check_vma=False,
    )
```

```python
import functools
import math

import jax
import jax.numpy as jnp
from jax import lax
from jax.experimental import pallas as pl
from jax.experimental.pallas import tpu as pltpu
from jax.sharding import PartitionSpec as P

HEAD_SIZE = 128
BLOCK = 64
NEGATIVE = -1e30
MESH = pl.DeviceIdType.MESH


def attend(first, use_prev, use_rand, q_tile, up_tile, keys, values, groups):
    scale = HEAD_SIZE ** (-0.5)
    rows = groups * BLOCK
    q = jnp.concatenate(
        [q_tile[:, r * HEAD_SIZE : (r + 1) * HEAD_SIZE] for r in range(groups)], axis=0
    )
    up = jnp.concatenate(
        [up_tile[:, r * HEAD_SIZE : (r + 1) * HEAD_SIZE] for r in range(groups)], axis=0
    )
    up_t = up.T
    scores = lax.dot_general(
        keys, q, (((1,), (1,)), ((), ())), preferred_element_type=jnp.float32
    ) * (scale * math.log2(math.e))
    key_at = lax.broadcasted_iota(jnp.int32, (BLOCK, rows), 0)
    query_at = lax.broadcasted_iota(jnp.int32, (BLOCK, rows), 1) & (BLOCK - 1)
    causal = key_at <= query_at
    never = jnp.float32(NEGATIVE)
    zero = jnp.float32(0.0)
    root_off = jnp.where(causal, zero, jnp.where(first, never, zero))
    own_off = jnp.where(causal, jnp.where(first, never, zero), never)
    prev_off = jnp.where(use_prev, zero, never)
    rand_off = jnp.where(use_rand, zero, never)
    scores = jnp.concatenate(
        [
            scores[:BLOCK] + root_off,
            scores[BLOCK : 2 * BLOCK] + own_off,
            scores[2 * BLOCK : 3 * BLOCK] + prev_off,
            scores[3 * BLOCK :] + rand_off,
        ],
        axis=0,
    )
    top = jnp.max(scores, axis=0, keepdims=True)
    weights = jnp.exp2(scores - top)
    total = jnp.sum(weights, axis=0, keepdims=True)
    probs = (weights * (1.0 / total)).astype(jnp.bfloat16)
    att_t = lax.dot_general(
        values, probs, (((0,), (0,)), ((), ())), preferred_element_type=jnp.float32
    ).astype(jnp.bfloat16)
    delta = jnp.sum(
        att_t.astype(jnp.float32) * up_t.astype(jnp.float32), axis=0, keepdims=True
    )
    dprob = lax.dot_general(
        values, up_t, (((1,), (0,)), ((), ())), preferred_element_type=jnp.float32
    )
    dscore = (probs.astype(jnp.float32) * (dprob - delta)).astype(jnp.bfloat16)
    dq_t = lax.dot_general(
        keys, dscore, (((0,), (0,)), ((), ())), preferred_element_type=jnp.float32
    )
    dq = (dq_t * scale).astype(jnp.bfloat16).T
    grads = (
        scale * jnp.dot(dscore, q, preferred_element_type=jnp.float32),
        jnp.dot(probs, up, preferred_element_type=jnp.float32),
    )
    return att_t.T, dq, grads


def chunk_head(i, h, head_size, each):
    z = lax.rem(lax.axis_index("head") + 1 + i, head_size)
    return z, z * each + h


class Chunk:
    def __init__(self, h, each, head_size, uses, wide, tokens, kvx, root, rand, grads, scratch):
        self.h, self.each, self.head_size, self.uses = h, each, head_size, uses
        self.wide, self.tokens, self.kvx, self.root, self.rand = wide, tokens, kvx, root, rand
        self.acc, self.g_edge, self.g_rand, self.g_root = grads
        self.buffers, self.load_sem, self.store_sem = scratch[:4], scratch[4], scratch[5]
        self.blocks = wide[0].shape[0]
        self.width = self.buffers[0].shape[-1]

    def columns(self, i):
        _, g = chunk_head(i, self.h, self.head_size, self.each)
        return pl.ds(pl.multiple_of(g * self.width, self.width), self.width)

    def load(self, i, which):
        return pltpu.make_async_copy(
            self.wide[which].at[:, :, self.columns(i)],
            self.buffers[which].at[i],
            self.load_sem.at[i, which],
        )

    def store(self, i, which):
        return pltpu.make_async_copy(
            self.buffers[2 + which].at[i],
            self.tokens[which].at[:, :, self.columns(i)],
            self.store_sem.at[i, which],
        )

    def wait_stores(self):
        for i in range(self.head_size):
            for which in range(2):
                self.store(i, which).wait()

    def start_loads(self):
        for i in range(self.head_size):
            for which in range(2):
                self.load(i, which).start()

    def run(self, events, after_head):
        blocks = self.blocks
        steps = self.head_size * blocks
        shard, part = lax.axis_index("seq"), lax.axis_index("head")
        at_first = jnp.logical_and(shard == 0, part == 0)
        q_buf, up_buf, att_buf, dq_buf = self.buffers
        groups = self.width // HEAD_SIZE

        def step(t, carry):
            i, j = t // blocks, t % blocks
            z, g = chunk_head(i, self.h, self.head_size, self.each)

            @pl.when(j == 0)
            def _():
                for which in range(2):
                    self.load(i, which).wait()

            here = pl.ds(pl.multiple_of(g * HEAD_SIZE, HEAD_SIZE), HEAD_SIZE)
            mine = slice(self.h * HEAD_SIZE, (self.h + 1) * HEAD_SIZE)
            keys, values = (
                jnp.concatenate(
                    [
                        self.root[z, kv, :, mine],
                        self.kvx[kv, j + 1, :, here],
                        self.kvx[kv, j, :, here],
                        self.rand[z, kv, j],
                    ],
                    axis=0,
                )
                for kv in range(2)
            )
            att, dq, grads = attend(
                jnp.logical_and(at_first, j == 0),
                *self.uses(j),
                q_buf[i, j], up_buf[i, j], keys, values, groups,
            )
            for r in range(groups):
                where = slice(r * HEAD_SIZE, (r + 1) * HEAD_SIZE)
                att_buf[i, j, :, where] = att[r * BLOCK : (r + 1) * BLOCK]
                dq_buf[i, j, :, where] = dq[r * BLOCK : (r + 1) * BLOCK]
            for kv, grad in enumerate(grads):
                self.acc[z, kv, j] = grad[BLOCK : 2 * BLOCK]
                self.g_rand[z, kv, j] = grad[3 * BLOCK :].astype(jnp.bfloat16)

            @pl.when(j == 0)
            def _():
                for kv, grad in enumerate(grads):
                    self.g_root[z, kv] = grad[:BLOCK]
                    self.g_edge[z, kv] = grad[2 * BLOCK : 3 * BLOCK].astype(jnp.bfloat16)

            @pl.when(j > 0)
            def _():
                for kv, grad in enumerate(grads):
                    self.g_root[z, kv] += grad[:BLOCK]
                    self.acc[z, kv, j - 1] += grad[2 * BLOCK : 3 * BLOCK]

            @pl.when(j == blocks - 1)
            def _():
                for which in range(2):
                    self.store(i, which).start()
                after_head(i)

            for at, event in events:
                pl.when(t == at * steps // 16)(event)
            return carry

        lax.fori_loop(0, steps, step, 0)


def grad_shapes(head_size, blocks):
    block = (BLOCK, HEAD_SIZE)
    return [
        ((head_size, 2, blocks) + block, jnp.float32),
        ((head_size, 2) + block, jnp.bfloat16),
        ((head_size, 2, blocks) + block, jnp.bfloat16),
        ((head_size, 2) + block, jnp.float32),
    ]


def chunk_scratch(head_size, blocks, wide):
    return [pltpu.VMEM((head_size, blocks, BLOCK, wide), jnp.bfloat16)] * 4 + [
        pltpu.SemaphoreType.DMA((head_size, 2)),
        pltpu.SemaphoreType.DMA((head_size, 2)),
    ]


def carrier(q, head_size, seq_size):
    return q * seq_size // head_size


def greet(head_size, seq_size):
    shard, part = lax.axis_index("seq"), lax.axis_index("head")
    barrier = pltpu.get_barrier_semaphore()
    count = 0

    def signal(other):
        pl.semaphore_signal(barrier, inc=1, device_id=other, device_id_type=MESH)

    for d in range(1, head_size):
        signal((shard, lax.rem(part + d, head_size)))
        count += 1
    for d in range(1, seq_size):
        signal((lax.rem(shard + d, seq_size), part))
        count += 1
    after, before = lax.rem(shard + 1, seq_size), lax.rem(shard + seq_size - 1, seq_size)

    @pl.when(part == head_size - 1)
    def _():
        signal((after, 0))

    @pl.when(part == 0)
    def _():
        signal((before, head_size - 1))

    at_end = jnp.logical_or(part == 0, part == head_size - 1)
    pl.semaphore_wait(barrier, count + jnp.where(at_end, 1, 0))


def send(source, target, send_sem, recv_sem, other):
    return pltpu.make_async_remote_copy(
        src_ref=source,
        dst_ref=target,
        send_sem=send_sem,
        recv_sem=recv_sem,
        device_id=other,
        device_id_type=MESH,
    )


def rows_of(at, count):
    return pl.ds(at, count)


def fetch_steps(
    head_size, seq_size, each, chosen, inputs, window, rand, kvx, root, kv_load, scratch
):
    shard, part = lax.axis_index("seq"), lax.axis_index("head")
    blocks = inputs[0].shape[0]
    slots = blocks * head_size
    pieces = 2 * each
    (stage, a_send, a_recv, near_send, near_recv, far_send, far_recv,
     b_send, b_recv, edge_send, edge_recv, out_send, out_recv, up_send, up_recv,
     over_send, over_recv) = scratch
    shares = [carrier(q, head_size, seq_size) for q in range(head_size)]
    stride = seq_size // head_size
    share = shard // stride
    carries = lax.rem(shard, stride) == 0
    after = jnp.minimum(shard + 1, seq_size - 1)
    has_after, has_before = shard + 1 < seq_size, shard > 0
    at_first = jnp.logical_and(shard == 0, part == 0)

    def columns(p, c):
        return pl.ds(pl.multiple_of((p * each + c // 2) * HEAD_SIZE, HEAD_SIZE), HEAD_SIZE)

    def slice_out(d, c):
        other = lax.rem(part + d, head_size)
        return send(
            inputs[c % 2].at[:, :, columns(other, c)],
            window[c].at[rows_of(2 * slots + part * blocks, blocks)],
            a_send.at[d, c], a_recv.at[d, c], (shard, other),
        )

    def near_copy(c):
        return send(
            window[c].at[rows_of(2 * slots, slots)], window[c].at[rows_of(slots, slots)],
            near_send.at[c], near_recv.at[c], (after, part),
        )

    def far_copy(c):
        return send(
            window[c].at[rows_of(slots, slots)], window[c].at[rows_of(0, slots)],
            far_send.at[c], far_recv.at[c], (after, part),
        )

    def slice_back(d, c):
        other = lax.rem(part + d, head_size)
        return send(
            stage.at[c, rows_of(other * blocks, blocks)], rand[c // 2].at[part, c % 2],
            b_send.at[d, c], b_recv.at[d, c], (shard, other),
        )

    def edge_copy(kv):
        last = part == head_size - 1
        other = (jnp.where(last, after, shard), jnp.where(last, 0, part + 1))
        return send(
            inputs[kv].at[blocks - 1], kvx.at[kv, 0], edge_send.at[kv], edge_recv.at[kv], other
        )

    gives_edge = jnp.logical_or(part < head_size - 1, has_after)
    gets_edge = jnp.logical_or(part > 0, has_before)

    def root_out(q):
        return send(
            root.at[q], root.at[q], out_send.at[q], out_recv.at[0], (jnp.int32(shares[q]), part)
        )

    def root_up(z):
        return send(root.at[share], root.at[share], up_send.at[z], up_recv.at[0], (shard, z))

    def root_over(d):
        other = lax.rem(shard + d, seq_size)
        copy = send(
            root.at[share], root.at[share], over_send.at[d], over_recv.at[share], (other, part)
        )
        return copy, jnp.logical_or(part > 0, other > 0)

    def spread():
        for d in range(1, seq_size):
            copy, wanted = root_over(d)
            pl.when(wanted)(copy.start)

    def root_event(e):
        if e == 0:

            @pl.when(jnp.logical_and(carries, part == 0))
            def _():
                pl.when(shard > 0)(root_out(0).wait_recv)
                for z in range(1, head_size):
                    root_up(z).start()
                spread()

        elif e == 1:

            @pl.when(jnp.logical_and(carries, part > 0))
            def _():
                root_up(0).wait_recv()
                spread()

        else:

            @pl.when(jnp.logical_not(at_first))
            def _():
                for q in range(head_size):
                    copy = send(root.at[q], root.at[q], over_send.at[0], over_recv.at[q], (shard, part))
                    pl.when(shard != shares[q])(copy.wait_recv)

    def start_slices(c):
        for d in range(1, head_size):
            slice_out(d, c).start()

    def begin():
        for c in range(2):
            start_slices(c)
        for kv in range(2):
            pl.when(gives_edge)(edge_copy(kv).start)
            kv_load(kv).wait()

        @pl.when(at_first)
        def _():
            for q in range(head_size):
                for kv in range(2):
                    root[q, kv] = kvx[kv, 1, :, q * each * HEAD_SIZE : (q + 1) * each * HEAD_SIZE]
            for q in range(1, head_size):
                root_out(q).start()

        for c in range(pieces):
            window[c][rows_of(2 * slots + part * blocks, blocks)] = kvx[
                c % 2, 1:, :, columns(part, c)
            ]

        @pl.when(jnp.logical_not(gets_edge))
        def _():
            for kv in range(2):
                kvx[kv, 0] = kvx[kv, 1]

    def pass_on(c):
        for d in range(1, head_size):
            slice_out(d, c).wait_recv()
        if c + 2 < pieces:
            start_slices(c + 2)
        pl.when(has_after)(near_copy(c).start)

    def relay(c):
        pl.when(has_before)(near_copy(c).wait_recv)
        pl.when(jnp.logical_and(has_before, has_after))(far_copy(c).start)

    def pick(c):
        pl.when(shard > 1)(far_copy(c).wait_recv)
        for d in range(1, head_size):
            other = lax.rem(part + d, head_size)
            for n in range(blocks):
                stage[c, other * blocks + n] = window[c][chosen(other * blocks + n)]
            slice_back(d, c).start()
        for n in range(blocks):
            rand[c // 2][part, c % 2, n] = window[c][chosen(part * blocks + n)]

    def arrive(c):
        for d in range(1, head_size):
            slice_back(d, c).wait_recv()

    def finish_edge():
        for kv in range(2):
            pl.when(gets_edge)(edge_copy(kv).wait_recv)

    def drain():
        for c in range(pieces):
            for d in range(1, head_size):
                slice_out(d, c).wait_send()
                slice_back(d, c).wait_send()
            pl.when(has_after)(near_copy(c).wait_send)
            pl.when(jnp.logical_and(has_before, has_after))(far_copy(c).wait_send)
        for kv in range(2):
            pl.when(gives_edge)(edge_copy(kv).wait_send)

        @pl.when(at_first)
        def _():
            for q in range(1, head_size):
                root_out(q).wait_send()

        @pl.when(carries)
        def _():
            @pl.when(part == 0)
            def _():
                for z in range(1, head_size):
                    root_up(z).wait_send()

            for d in range(1, seq_size):
                copy, wanted = root_over(d)
                pl.when(wanted)(copy.wait_send)

    return begin, pass_on, relay, pick, arrive, root_event, finish_edge, drain


def give_steps(head_size, seq_size, each, earlier, last, grads, outputs, scratch):
    shard, part = lax.axis_index("seq"), lax.axis_index("head")
    (slots_in, chain, sections, near_in, far_in, back, edge_in, root, root_box, up_box, last_box,
     a_send, a_recv, near_send, near_recv, far_send, far_recv,
     b_send, b_recv, edge_send, edge_recv, over_send, over_recv, up_send, up_recv,
     out_send, out_recv) = scratch
    blocks = grads[0][0].shape[2]
    slots = blocks * head_size
    pieces = 2 * each
    shares = [carrier(q, head_size, seq_size) for q in range(head_size)]
    stride = seq_size // head_size
    share = shard // stride
    carries = lax.rem(shard, stride) == 0
    before = jnp.maximum(shard - 1, 0)
    has_after, has_before = shard + 1 < seq_size, shard > 0

    def slice_out(d, c):
        other = lax.rem(part + d, head_size)
        return send(
            grads[c // 2][2].at[other, c % 2],
            slots_in.at[c, rows_of(part * blocks, blocks)],
            a_send.at[d, c], a_recv.at[d, c], (shard, other),
        )

    def far_copy(c):
        return send(
            sections.at[c, rows_of(0, slots)], far_in.at[c],
            far_send.at[c], far_recv.at[c], (before, part),
        )

    def near_copy(c):
        return send(
            sections.at[c, rows_of(slots, slots)], near_in.at[c],
            near_send.at[c], near_recv.at[c], (before, part),
        )

    def slice_back(d, c):
        other = lax.rem(part + d, head_size)
        return send(
            sections.at[c, rows_of(2 * slots + other * blocks, blocks)], back.at[c, part],
            b_send.at[d, c], b_recv.at[d, c], (shard, other),
        )

    def edge_copy(h):
        other = (
            jnp.where(part == 0, before, shard),
            jnp.where(part == 0, head_size - 1, part - 1),
        )
        return send(grads[h][1], edge_in.at[h], edge_send.at[h], edge_recv.at[h], other)

    gives_edge = jnp.logical_or(part > 0, has_before)
    gets_edge = jnp.logical_or(part < head_size - 1, has_after)

    def root_over(h, q):
        return send(
            grads[h][3].at[q], root_box.at[h, shard], over_send.at[h, q], over_recv.at[h, shard],
            (jnp.int32(carrier(q, head_size, seq_size)), part),
        )

    def root_up(h):
        return send(
            root.at[h, share], up_box.at[h, part], up_send.at[h], up_recv.at[h, part], (shard, 0)
        )

    def root_out(h):
        return send(
            root.at[h, share], last_box.at[h, share], out_send.at[h], out_recv.at[h, share], (0, part)
        )

    sends_up = jnp.logical_and(carries, part > 0)
    sends_out = jnp.logical_and(jnp.logical_and(carries, part == 0), shard > 0)

    def landed(box, sem):
        send(box, box, sem, sem, (shard, part)).wait_recv()

    def root_event(h, e):
        if e == 1:

            @pl.when(carries)
            def _():
                total = grads[h][3][share]
                for d in range(1, seq_size):
                    other = lax.rem(shard + d, seq_size)
                    landed(root_box.at[h, other], over_recv.at[h, other])
                    total += root_box[h, other]
                root[h, share] = total

            pl.when(sends_up)(root_up(h).start)
        else:

            @pl.when(jnp.logical_and(carries, part == 0))
            def _():
                total = root[h, share]
                for z in range(1, head_size):
                    landed(up_box.at[h, z], up_recv.at[h, z])
                    total += up_box[h, z]
                root[h, share] = total

            pl.when(sends_out)(root_out(h).start)

    def keep(c):
        slots_in[c, rows_of(part * blocks, blocks)] = grads[c // 2][2][part, c % 2]

    def section(t):
        at = last[t]
        found = chain[jnp.maximum(at, 0)]
        return jnp.where(at >= 0, found, 0.0).astype(jnp.bfloat16)

    def collect(c):
        for d in range(1, head_size):
            slice_out(d, c).wait_recv()
        for n in range(slots):
            term = slots_in[c, n].astype(jnp.float32)
            if n > 0:
                same = earlier[n]
                found = chain[jnp.maximum(same, 0)]
                term = term + jnp.where(same >= 0, found, 0.0)
            chain[n] = term
        for t in range(slots):
            sections[c, t] = section(t)
        pl.when(shard > 1)(far_copy(c).start)
        for t in range(slots, 3 * slots):
            sections[c, t] = section(t)

    def add_to(c, where, came):
        sections[c, where] = (
            sections[c, where].astype(jnp.float32) + came[c].astype(jnp.float32)
        ).astype(jnp.bfloat16)

    def relay(c):
        @pl.when(jnp.logical_and(has_before, has_after))
        def _():
            far_copy(c).wait_recv()
            add_to(c, rows_of(slots, slots), far_in)

        pl.when(has_before)(near_copy(c).start)

    def give_back(c):
        @pl.when(has_after)
        def _():
            near_copy(c).wait_recv()
            add_to(c, rows_of(2 * slots, slots), near_in)

        for d in range(1, head_size):
            slice_back(d, c).start()

    def after_head(h, i):
        z, _ = chunk_head(i, h, head_size, each)
        pl.when(shard != carrier(z, head_size, seq_size))(root_over(h, z).start)

        @pl.when(i < head_size - 1)
        def _():
            for kv in range(2):
                slice_out(i + 1, 2 * h + kv).start()

    def after_chunk(h):
        pl.when(gives_edge)(edge_copy(h).start)
        for c in (2 * h, 2 * h + 1):
            keep(c)

    def finish(c, z, came):
        h, kv = c // 2, c % 2
        where = pl.ds(pl.multiple_of((z * each + h) * HEAD_SIZE, HEAD_SIZE), HEAD_SIZE)
        for n in range(blocks):
            total = grads[h][0][z, kv, n] + came[n].astype(jnp.float32)
            if n == 0:
                total += root[h, z, kv]
            if n == blocks - 1:
                total += edge_in[h, z, kv].astype(jnp.float32)
            outputs[kv][pl.ds(n * BLOCK, BLOCK), where] = total.astype(jnp.bfloat16)

    def finish_all():
        for h in range(each):
            pl.when(gets_edge)(edge_copy(h).wait_recv)

        @pl.when(jnp.logical_not(gets_edge))
        def _():
            edge_in[...] = jnp.zeros_like(edge_in)

        first = jnp.logical_and(shard == 0, part == 0)

        @pl.when(first)
        def _():
            for h in range(each):
                for q in range(1, head_size):
                    landed(last_box.at[h, q], out_recv.at[h, q])
                    root[h, q] = last_box[h, q]

        @pl.when(jnp.logical_not(first))
        def _():
            for h in range(each):
                pl.when(sends_up)(root_up(h).wait_send)
                pl.when(sends_out)(root_out(h).wait_send)
            root[...] = jnp.zeros_like(root)

        for c in range(pieces):
            finish(c, part, sections.at[c, rows_of(2 * slots + part * blocks, blocks)])
            for d in range(1, head_size):
                came = lax.rem(part + head_size - d, head_size)
                slice_back(d, c).wait_recv()
                finish(c, came, back.at[c, came])

    def drain():
        for c in range(pieces):
            for d in range(1, head_size):
                slice_out(d, c).wait_send()
                slice_back(d, c).wait_send()
            pl.when(shard > 1)(far_copy(c).wait_send)
            pl.when(has_before)(near_copy(c).wait_send)
        for h in range(each):
            pl.when(gives_edge)(edge_copy(h).wait_send)
            for q in range(head_size):
                pl.when(shard != shares[q])(root_over(h, q).wait_send)

    return after_head, after_chunk, collect, relay, give_back, root_event, finish_all, drain


def kernel(
    head_size, seq_size, each, ancestors, k_ref, v_ref, q_ref, up_ref,
    att_ref, dq_ref, k_out, v_out, *rest,
):
    shard, part = lax.axis_index("seq"), lax.axis_index("head")
    blocks, _, width = k_ref.shape
    slots = blocks * head_size
    pieces = 2 * each
    rest = list(rest)

    def take(count):
        taken = rest[:count]
        del rest[:count]
        return taken

    window = take(pieces)
    rand = take(each)
    grads = [take(4) for _ in range(each)]
    work = [take(6) for _ in range(each)]
    kvx, root_block, stage = take(3)
    given = take(11)
    earlier, last = take(2)
    (kv_sem,) = take(1)
    fetch_sems = take(16)
    inputs, outputs = (k_ref, v_ref), (k_out, v_out)
    shard, part = lax.axis_index("seq"), lax.axis_index("head")
    origin = (shard - 2) * slots

    def place(n):
        entry = ancestors[n, 1]
        return jnp.where(entry >= 0, entry - origin, -1)

    def chosen(n):
        at = place(n)
        return jnp.where(at >= 0, at, 2 * slots)

    def uses(j):
        n = part * blocks + j
        first_entry, last_entry = ancestors[n, 0], ancestors[n, 1]
        return first_entry >= 0, jnp.logical_and(last_entry >= 0, last_entry != first_entry)

    def write_links():
        places = [place(n) for n in range(slots)]
        for n in range(slots):
            found = jnp.int32(-1)
            for m in range(n):
                found = jnp.where(places[m] == places[n], m, found)
            earlier[n] = found

        def one(t, carry):
            found = jnp.int32(-1)
            for n in range(slots):
                found = jnp.where(places[n] == t, n, found)
            last[t] = found
            return carry

        lax.fori_loop(0, 3 * slots, one, 0)

    chunks = [
        Chunk(
            h, each, head_size, uses, (q_ref, up_ref), (att_ref, dq_ref), kvx, root_block, rand[h],
            grads[h], work[h],
        )
        for h in range(each)
    ]

    def kv_load(kv):
        return pltpu.make_async_copy(inputs[kv], kvx.at[kv, pl.ds(1, blocks)], kv_sem.at[kv])

    for kv in range(2):
        kv_load(kv).start()
    greet(head_size, seq_size)
    begin, pass_on, relay, pick, arrive, root_event, finish_edge, drain = fetch_steps(
        head_size, seq_size, each, chosen, inputs, window, rand, kvx, root_block, kv_load,
        [stage, *fetch_sems],
    )
    after_head, after_chunk, collect, give_on, give_back, root_sum, finish_all, drain_grads = (
        give_steps(
            head_size, seq_size, each, earlier, last, grads, outputs, [*given, *rest],
        )
    )
    begin()
    for chunk in chunks:
        chunk.start_loads()
    write_links()
    for at in range(pieces + 1):
        if at >= 2:
            pick(at - 2)
        if at >= 1:
            relay(at - 1)
        if at < pieces:
            pass_on(at)
        if at < 2:
            root_event(at)
    root_event(2)
    finish_edge()
    final = pieces - 1
    if each == 1:
        pick(final)
    do = functools.partial
    for h, chunk in enumerate(chunks):
        for c in (2 * h, 2 * h + 1):
            arrive(c)
        if h == 0:
            events = [(3, do(pick, final))] if each > 1 else []
        else:
            events = [
                (2, do(give_on, 2 * h - 2)),
                (4, do(give_on, 2 * h - 1)),
                (9, do(root_sum, h - 1, 1)),
                (11, do(give_back, 2 * h - 2)),
                (13, do(root_sum, h - 1, 2)),
                (15, do(give_back, 2 * h - 1)),
            ]
        chunk.run(events, do(after_head, h))
        after_chunk(h)
        if h < each - 1:
            collect(2 * h)
            collect(2 * h + 1)
    h = each - 1
    collect(2 * h)
    collect(2 * h + 1)
    give_on(2 * h)
    give_on(2 * h + 1)
    root_sum(h, 1)
    give_back(2 * h)
    give_back(2 * h + 1)
    root_sum(h, 2)
    finish_all()
    for chunk in chunks:
        chunk.wait_stores()
    drain()
    drain_grads()


def attention(ancestors, key_rows, value_rows, queries, upstream, head_size, seq_size):
    blocks, _, width = key_rows.shape
    heads = width // HEAD_SIZE
    each = heads // head_size
    pieces = 2 * each
    slots = blocks * head_size
    vmem, smem = pltpu.MemorySpace.VMEM, pltpu.MemorySpace.SMEM
    dma = pltpu.SemaphoreType.DMA
    picked = pltpu.VMEM((head_size, 2, blocks, BLOCK, HEAD_SIZE), jnp.bfloat16)
    box = pltpu.VMEM((pieces, slots, BLOCK, HEAD_SIZE), jnp.bfloat16)
    edge = (head_size, 2, BLOCK, HEAD_SIZE)
    outs = [(queries.shape, jnp.bfloat16)] * 2 + [((blocks * BLOCK, width), jnp.bfloat16)] * 2
    hops = [
        dma((head_size, pieces)), dma((head_size, pieces)),
        dma((pieces,)), dma((pieces,)), dma((pieces,)), dma((pieces,)),
        dma((head_size, pieces)), dma((head_size, pieces)),
    ]
    return pl.pallas_call(
        functools.partial(kernel, head_size, seq_size, each),
        in_specs=[pl.BlockSpec(memory_space=smem)] + [pl.BlockSpec(memory_space=pl.ANY)] * 4,
        out_specs=[pl.BlockSpec(memory_space=pl.ANY)] * 2 + [pl.BlockSpec(memory_space=vmem)] * 2,
        out_shape=[jax.ShapeDtypeStruct(*out) for out in outs],
        scratch_shapes=[
            *[pltpu.VMEM((3 * slots, BLOCK, HEAD_SIZE), jnp.bfloat16)] * pieces,
            *[picked] * each,
            *[pltpu.VMEM(*shape) for shape in grad_shapes(head_size, blocks) * each],
            *chunk_scratch(head_size, blocks, queries.shape[-1] // heads) * each,
            pltpu.VMEM((2, blocks + 1, BLOCK, width), jnp.bfloat16),
            pltpu.VMEM((head_size, 2, BLOCK, each * HEAD_SIZE), jnp.bfloat16),
            box,
            box,
            pltpu.VMEM((slots, BLOCK, HEAD_SIZE), jnp.float32),
            pltpu.VMEM((pieces, 3 * slots, BLOCK, HEAD_SIZE), jnp.bfloat16),
            box,
            box,
            pltpu.VMEM((pieces, head_size, blocks, BLOCK, HEAD_SIZE), jnp.bfloat16),
            pltpu.VMEM((each,) + edge, jnp.bfloat16),
            pltpu.VMEM((each,) + edge, jnp.float32),
            pltpu.VMEM((each, seq_size) + edge[1:], jnp.float32),
            pltpu.VMEM((each,) + edge, jnp.float32),
            pltpu.VMEM((each,) + edge, jnp.float32),
            pltpu.SMEM((slots,), jnp.int32),
            pltpu.SMEM((3 * slots,), jnp.int32),
            dma((2,)),
            *hops, dma((2,)), dma((2,)),
            dma((head_size,)), dma((1,)), dma((head_size,)), dma((1,)),
            dma((seq_size,)), dma((head_size,)),
            *hops, dma((each,)), dma((each,)),
            dma((each, head_size)), dma((each, seq_size)), dma((each,)), dma((each, head_size)),
            dma((each,)), dma((each, head_size)),
        ],
        compiler_params=pltpu.CompilerParams(
            collective_id=0, has_side_effects=True, vmem_limit_bytes=42 * 1024 * 1024
        ),
        name="attention",
    )(ancestors, key_rows, value_rows, queries, upstream)


def local(queries, key_rows, value_rows, upstream, ancestors):
    tokens, _ = key_rows.shape
    blocks = tokens // BLOCK
    head_size, seq_size = lax.axis_size("head"), lax.axis_size("seq")

    def blocked(x):
        return x.reshape(blocks, BLOCK, x.shape[1])

    attended, query_grad, key_grad, value_grad = attention(
        ancestors, blocked(key_rows), blocked(value_rows), blocked(queries),
        blocked(upstream), head_size, seq_size,
    )
    wide = queries.shape[-1]
    return attended.reshape(tokens, wide), query_grad.reshape(tokens, wide), key_grad, value_grad


def solution(mesh):
    tokens = P(("seq", "head"), None)
    return jax.shard_map(
        local,
        mesh=mesh,
        in_specs=(tokens, tokens, tokens, tokens, P("seq", None)),
        out_specs=(tokens, tokens, tokens, tokens),
        check_vma=False,
    )
```

```python
import functools
import math

import jax
import jax.numpy as jnp
from jax import lax
from jax.experimental import pallas as pl
from jax.experimental.pallas import tpu as pltpu
from jax.sharding import PartitionSpec as P

HEAD_SIZE = 128
BLOCK = 64
NEGATIVE = -1e30
MESH = pl.DeviceIdType.MESH


def attend(first, use_prev, use_rand, q_tile, up_tile, keys, values, groups):
    scale = HEAD_SIZE ** (-0.5)
    rows = groups * BLOCK
    q = jnp.concatenate(
        [q_tile[:, r * HEAD_SIZE : (r + 1) * HEAD_SIZE] for r in range(groups)], axis=0
    )
    up = jnp.concatenate(
        [up_tile[:, r * HEAD_SIZE : (r + 1) * HEAD_SIZE] for r in range(groups)], axis=0
    )
    up_t = up.T
    scores = lax.dot_general(
        keys, q, (((1,), (1,)), ((), ())), preferred_element_type=jnp.float32
    ) * (scale * math.log2(math.e))
    key_at = lax.broadcasted_iota(jnp.int32, (BLOCK, rows), 0)
    query_at = lax.broadcasted_iota(jnp.int32, (BLOCK, rows), 1) & (BLOCK - 1)
    causal = key_at <= query_at
    never = jnp.float32(NEGATIVE)
    zero = jnp.float32(0.0)
    root_off = jnp.where(causal, zero, jnp.where(first, never, zero))
    own_off = jnp.where(causal, jnp.where(first, never, zero), never)
    prev_off = jnp.where(use_prev, zero, never)
    rand_off = jnp.where(use_rand, zero, never)
    scores = jnp.concatenate(
        [
            scores[:BLOCK] + root_off,
            scores[BLOCK : 2 * BLOCK] + own_off,
            scores[2 * BLOCK : 3 * BLOCK] + prev_off,
            scores[3 * BLOCK :] + rand_off,
        ],
        axis=0,
    )
    top = jnp.max(scores, axis=0, keepdims=True)
    weights = jnp.exp2(scores - top)
    total = jnp.sum(weights, axis=0, keepdims=True)
    probs = (weights * (1.0 / total)).astype(jnp.bfloat16)
    att_t = lax.dot_general(
        values, probs, (((0,), (0,)), ((), ())), preferred_element_type=jnp.float32
    ).astype(jnp.bfloat16)
    delta = jnp.sum(
        att_t.astype(jnp.float32) * up_t.astype(jnp.float32), axis=0, keepdims=True
    )
    dprob = lax.dot_general(
        values, up_t, (((1,), (0,)), ((), ())), preferred_element_type=jnp.float32
    )
    dscore = (probs.astype(jnp.float32) * (dprob - delta)).astype(jnp.bfloat16)
    dq_t = lax.dot_general(
        keys, dscore, (((0,), (0,)), ((), ())), preferred_element_type=jnp.float32
    )
    dq = (dq_t * scale).astype(jnp.bfloat16).T
    grads = (
        scale * jnp.dot(dscore, q, preferred_element_type=jnp.float32),
        jnp.dot(probs, up, preferred_element_type=jnp.float32),
    )
    return att_t.T, dq, grads


def chunk_head(i, h, head_size, each):
    z = lax.rem(lax.axis_index("head") + 1 + i, head_size)
    return z, z * each + h


class Chunk:
    def __init__(self, h, each, head_size, uses, wide, tokens, kvx, root, rand, grads, scratch):
        self.h, self.each, self.head_size, self.uses = h, each, head_size, uses
        self.wide, self.tokens, self.kvx, self.root, self.rand = wide, tokens, kvx, root, rand
        self.acc, self.g_edge, self.g_rand, self.g_root = grads
        self.buffers, self.load_sem, self.store_sem = scratch[:4], scratch[4], scratch[5]
        self.blocks = wide[0].shape[0]
        self.width = self.buffers[0].shape[-1]

    def columns(self, i):
        _, g = chunk_head(i, self.h, self.head_size, self.each)
        return pl.ds(pl.multiple_of(g * self.width, self.width), self.width)

    def load(self, i, which):
        return pltpu.make_async_copy(
            self.wide[which].at[:, :, self.columns(i)],
            self.buffers[which].at[i],
            self.load_sem.at[i, which],
        )

    def store(self, i, which):
        return pltpu.make_async_copy(
            self.buffers[2 + which].at[i],
            self.tokens[which].at[:, :, self.columns(i)],
            self.store_sem.at[i, which],
        )

    def wait_stores(self):
        for i in range(self.head_size):
            for which in range(2):
                self.store(i, which).wait()

    def start_loads(self):
        for i in range(self.head_size):
            for which in range(2):
                self.load(i, which).start()

    def run(self, events, after_head):
        blocks = self.blocks
        steps = self.head_size * blocks
        shard, part = lax.axis_index("seq"), lax.axis_index("head")
        at_first = jnp.logical_and(shard == 0, part == 0)
        q_buf, up_buf, att_buf, dq_buf = self.buffers
        groups = self.width // HEAD_SIZE

        def step(t, carry):
            i, j = t // blocks, t % blocks
            z, g = chunk_head(i, self.h, self.head_size, self.each)

            @pl.when(j == 0)
            def _():
                for which in range(2):
                    self.load(i, which).wait()

            here = pl.ds(pl.multiple_of(g * HEAD_SIZE, HEAD_SIZE), HEAD_SIZE)
            mine = slice(self.h * HEAD_SIZE, (self.h + 1) * HEAD_SIZE)
            keys, values = (
                jnp.concatenate(
                    [
                        self.root[z, kv, :, mine],
                        self.kvx[kv, j + 1, :, here],
                        self.kvx[kv, j, :, here],
                        self.rand[z, kv, j],
                    ],
                    axis=0,
                )
                for kv in range(2)
            )
            att, dq, grads = attend(
                jnp.logical_and(at_first, j == 0),
                *self.uses(j),
                q_buf[i, j], up_buf[i, j], keys, values, groups,
            )
            for r in range(groups):
                where = slice(r * HEAD_SIZE, (r + 1) * HEAD_SIZE)
                att_buf[i, j, :, where] = att[r * BLOCK : (r + 1) * BLOCK]
                dq_buf[i, j, :, where] = dq[r * BLOCK : (r + 1) * BLOCK]
            for kv, grad in enumerate(grads):
                self.acc[z, kv, j] = grad[BLOCK : 2 * BLOCK]
                self.g_rand[z, kv, j] = grad[3 * BLOCK :].astype(jnp.bfloat16)

            @pl.when(j == 0)
            def _():
                for kv, grad in enumerate(grads):
                    self.g_root[z, kv] = grad[:BLOCK]
                    self.g_edge[z, kv] = grad[2 * BLOCK : 3 * BLOCK].astype(jnp.bfloat16)

            @pl.when(j > 0)
            def _():
                for kv, grad in enumerate(grads):
                    self.g_root[z, kv] += grad[:BLOCK]
                    self.acc[z, kv, j - 1] += grad[2 * BLOCK : 3 * BLOCK]

            @pl.when(j == blocks - 1)
            def _():
                for which in range(2):
                    self.store(i, which).start()
                after_head(i)

            for at, event in events:
                pl.when(t == at * steps // 16)(event)
            return carry

        lax.fori_loop(0, steps, step, 0)


def grad_shapes(head_size, blocks):
    block = (BLOCK, HEAD_SIZE)
    return [
        ((head_size, 2, blocks) + block, jnp.float32),
        ((head_size, 2) + block, jnp.bfloat16),
        ((head_size, 2, blocks) + block, jnp.bfloat16),
        ((head_size, 2) + block, jnp.float32),
    ]


def chunk_scratch(head_size, blocks, wide):
    return [pltpu.VMEM((head_size, blocks, BLOCK, wide), jnp.bfloat16)] * 4 + [
        pltpu.SemaphoreType.DMA((head_size, 2)),
        pltpu.SemaphoreType.DMA((head_size, 2)),
    ]


def carrier(q, head_size, seq_size):
    return q * seq_size // head_size


def greet(head_size, seq_size):
    shard, part = lax.axis_index("seq"), lax.axis_index("head")
    barrier = pltpu.get_barrier_semaphore()
    count = 0

    def signal(other):
        pl.semaphore_signal(barrier, inc=1, device_id=other, device_id_type=MESH)

    for d in range(1, head_size):
        signal((shard, lax.rem(part + d, head_size)))
        count += 1
    for d in range(1, seq_size):
        signal((lax.rem(shard + d, seq_size), part))
        count += 1
    after, before = lax.rem(shard + 1, seq_size), lax.rem(shard + seq_size - 1, seq_size)

    @pl.when(part == head_size - 1)
    def _():
        signal((after, 0))

    @pl.when(part == 0)
    def _():
        signal((before, head_size - 1))

    at_end = jnp.logical_or(part == 0, part == head_size - 1)
    pl.semaphore_wait(barrier, count + jnp.where(at_end, 1, 0))


def send(source, target, send_sem, recv_sem, other):
    return pltpu.make_async_remote_copy(
        src_ref=source,
        dst_ref=target,
        send_sem=send_sem,
        recv_sem=recv_sem,
        device_id=other,
        device_id_type=MESH,
    )


def rows_of(at, count):
    return pl.ds(at, count)


def fetch_steps(
    head_size, seq_size, each, chosen, inputs, window, rand, kvx, root, kv_load, scratch
):
    shard, part = lax.axis_index("seq"), lax.axis_index("head")
    blocks = inputs[0].shape[0]
    slots = blocks * head_size
    pieces = 2 * each
    (stage, a_send, a_recv, near_send, near_recv, far_send, far_recv,
     b_send, b_recv, edge_send, edge_recv, inner_send, inner_recv, out_send, out_recv,
     up_send, up_recv, over_send, over_recv) = scratch
    middle = head_size // 2
    half = inputs[0].shape[-1] // 2
    shares = [carrier(q, head_size, seq_size) for q in range(head_size)]
    stride = seq_size // head_size
    share = shard // stride
    carries = lax.rem(shard, stride) == 0
    after = jnp.minimum(shard + 1, seq_size - 1)
    has_after, has_before = shard + 1 < seq_size, shard > 0
    at_first = jnp.logical_and(shard == 0, part == 0)

    def columns(p, c):
        return pl.ds(pl.multiple_of((p * each + c // 2) * HEAD_SIZE, HEAD_SIZE), HEAD_SIZE)

    def slice_out(d, c):
        other = lax.rem(part + d, head_size)
        return send(
            inputs[c % 2].at[:, :, columns(other, c)],
            window[c].at[rows_of(2 * slots + part * blocks, blocks)],
            a_send.at[d, c], a_recv.at[d, c], (shard, other),
        )

    def near_copy(c):
        return send(
            window[c].at[rows_of(2 * slots, slots)], window[c].at[rows_of(slots, slots)],
            near_send.at[c], near_recv.at[c], (after, part),
        )

    def far_copy(c):
        return send(
            window[c].at[rows_of(slots, slots)], window[c].at[rows_of(0, slots)],
            far_send.at[c], far_recv.at[c], (after, part),
        )

    def slice_back(d, c):
        other = lax.rem(part + d, head_size)
        return send(
            stage.at[c, rows_of(other * blocks, blocks)], rand[c // 2].at[part, c % 2],
            b_send.at[d, c], b_recv.at[d, c], (shard, other),
        )

    def edge_copy(kv, side):
        last = part == head_size - 1
        other = (jnp.where(last, after, shard), jnp.where(last, 0, part + 1))
        columns = slice(side * half, (side + 1) * half)
        return send(
            inputs[kv].at[blocks - 1, :, columns], kvx.at[kv, 0, :, columns],
            edge_send.at[kv, side], edge_recv.at[kv, side], other,
        )

    gives_edge = jnp.logical_or(part < head_size - 1, has_after)
    gets_edge = jnp.logical_or(part > 0, has_before)
    gives_side = (
        jnp.logical_and(gives_edge, part != head_size - 1),
        jnp.logical_and(gives_edge, part != middle - 1),
    )
    gets_side = (
        jnp.logical_and(gets_edge, part != 0),
        jnp.logical_and(gets_edge, part != middle),
    )
    lower = part < middle
    near_end = 2 * slots - 1
    inner_at = jnp.where(lower, near_end, near_end + middle * blocks)
    inner_to = jnp.where(lower, 0, middle)
    has_inner = jnp.logical_or(part >= middle, has_before)

    def inner_copy(q, c):
        return send(
            window[c].at[inner_at], kvx.at[c % 2, 0, :, columns(q, c)],
            inner_send.at[c], inner_recv.at[q, c], (shard, inner_to),
        )

    gives_inner = jnp.logical_and(has_inner, part != inner_to)

    def inner(c):
        pl.when(gives_inner)(inner_copy(part, c).start)

        @pl.when(jnp.logical_and(has_inner, part == inner_to))
        def _():
            kvx[c % 2, 0, :, columns(part, c)] = window[c][inner_at]

    def root_out(q):
        return send(
            root.at[q], root.at[q], out_send.at[q], out_recv.at[0], (jnp.int32(shares[q]), part)
        )

    def root_up(z):
        return send(root.at[share], root.at[share], up_send.at[z], up_recv.at[0], (shard, z))

    def root_over(d):
        other = lax.rem(shard + d, seq_size)
        copy = send(
            root.at[share], root.at[share], over_send.at[d], over_recv.at[share], (other, part)
        )
        return copy, jnp.logical_or(part > 0, other > 0)

    def spread():
        for d in range(1, seq_size):
            copy, wanted = root_over(d)
            pl.when(wanted)(copy.start)

    def root_event(e):
        if e == 0:

            @pl.when(jnp.logical_and(carries, part == 0))
            def _():
                pl.when(shard > 0)(root_out(0).wait_recv)
                for z in range(1, head_size):
                    root_up(z).start()
                spread()

        elif e == 1:

            @pl.when(jnp.logical_and(carries, part > 0))
            def _():
                root_up(0).wait_recv()
                spread()

        else:

            @pl.when(jnp.logical_not(at_first))
            def _():
                for q in range(head_size):
                    copy = send(root.at[q], root.at[q], over_send.at[0], over_recv.at[q], (shard, part))
                    pl.when(shard != shares[q])(copy.wait_recv)

    def start_slices(c):
        for d in range(1, head_size):
            slice_out(d, c).start()

    def begin():
        for c in range(2):
            start_slices(c)
        for kv in range(2):
            for side in range(2):
                pl.when(gives_side[side])(edge_copy(kv, side).start)
            kv_load(kv).wait()

        @pl.when(at_first)
        def _():
            for q in range(head_size):
                for kv in range(2):
                    root[q, kv] = kvx[kv, 1, :, q * each * HEAD_SIZE : (q + 1) * each * HEAD_SIZE]
            for q in range(1, head_size):
                root_out(q).start()

        for c in range(pieces):
            window[c][rows_of(2 * slots + part * blocks, blocks)] = kvx[
                c % 2, 1:, :, columns(part, c)
            ]

        @pl.when(jnp.logical_not(gets_edge))
        def _():
            for kv in range(2):
                kvx[kv, 0] = kvx[kv, 1]

    def pass_on(c):
        for d in range(1, head_size):
            slice_out(d, c).wait_recv()
        if c + 2 < pieces:
            start_slices(c + 2)
        pl.when(has_after)(near_copy(c).start)

    def relay(c):
        pl.when(has_before)(near_copy(c).wait_recv)
        pl.when(jnp.logical_and(has_before, has_after))(far_copy(c).start)
        inner(c)

    def pick(c):
        pl.when(shard > 1)(far_copy(c).wait_recv)
        for d in range(1, head_size):
            other = lax.rem(part + d, head_size)
            for n in range(blocks):
                stage[c, other * blocks + n] = window[c][chosen(other * blocks + n)]
            slice_back(d, c).start()
        for n in range(blocks):
            rand[c // 2][part, c % 2, n] = window[c][chosen(part * blocks + n)]

    def arrive(c):
        for d in range(1, head_size):
            slice_back(d, c).wait_recv()

    def finish_edge():
        for kv in range(2):
            for side in range(2):
                pl.when(gets_side[side])(edge_copy(kv, side).wait_recv)

        @pl.when(jnp.logical_and(has_inner, part == inner_to))
        def _():
            for d in range(1, middle):
                for c in range(pieces):
                    inner_copy(part + d, c).wait_recv()

    def drain():
        for c in range(pieces):
            for d in range(1, head_size):
                slice_out(d, c).wait_send()
                slice_back(d, c).wait_send()
            pl.when(has_after)(near_copy(c).wait_send)
            pl.when(jnp.logical_and(has_before, has_after))(far_copy(c).wait_send)
        for c in range(pieces):
            pl.when(gives_inner)(inner_copy(part, c).wait_send)
        for kv in range(2):
            for side in range(2):
                pl.when(gives_side[side])(edge_copy(kv, side).wait_send)

        @pl.when(at_first)
        def _():
            for q in range(1, head_size):
                root_out(q).wait_send()

        @pl.when(carries)
        def _():
            @pl.when(part == 0)
            def _():
                for z in range(1, head_size):
                    root_up(z).wait_send()

            for d in range(1, seq_size):
                copy, wanted = root_over(d)
                pl.when(wanted)(copy.wait_send)

    return begin, pass_on, relay, pick, arrive, root_event, finish_edge, drain


def give_steps(head_size, seq_size, each, earlier, last, grads, outputs, scratch):
    shard, part = lax.axis_index("seq"), lax.axis_index("head")
    (slots_in, chain, sections, near_in, far_in, back, edge_in, inner_in, root, root_box, up_box,
     last_box, a_send, a_recv, near_send, near_recv, far_send, far_recv,
     b_send, b_recv, edge_send, edge_recv, inner_send, inner_recv, over_send, over_recv,
     up_send, up_recv, out_send, out_recv) = scratch
    middle = head_size // 2
    blocks = grads[0][0].shape[2]
    slots = blocks * head_size
    pieces = 2 * each
    shares = [carrier(q, head_size, seq_size) for q in range(head_size)]
    stride = seq_size // head_size
    share = shard // stride
    carries = lax.rem(shard, stride) == 0
    before = jnp.maximum(shard - 1, 0)
    has_after, has_before = shard + 1 < seq_size, shard > 0

    def slice_out(d, c):
        other = lax.rem(part + d, head_size)
        return send(
            grads[c // 2][2].at[other, c % 2],
            slots_in.at[c, rows_of(part * blocks, blocks)],
            a_send.at[d, c], a_recv.at[d, c], (shard, other),
        )

    def far_copy(c):
        return send(
            sections.at[c, rows_of(0, slots)], far_in.at[c],
            far_send.at[c], far_recv.at[c], (before, part),
        )

    def near_copy(c):
        return send(
            sections.at[c, rows_of(slots, slots)], near_in.at[c],
            near_send.at[c], near_recv.at[c], (before, part),
        )

    def slice_back(d, c):
        other = lax.rem(part + d, head_size)
        return send(
            sections.at[c, rows_of(2 * slots + other * blocks, blocks)], back.at[c, part],
            b_send.at[d, c], b_recv.at[d, c], (shard, other),
        )

    def edge_copy(h, side):
        other = (
            jnp.where(part == 0, before, shard),
            jnp.where(part == 0, head_size - 1, part - 1),
        )
        slices = pl.ds(side * middle, middle)
        return send(
            grads[h][1].at[slices], edge_in.at[h, slices], edge_send.at[h, side],
            edge_recv.at[h, side], other,
        )

    gives_edge = jnp.logical_or(part > 0, has_before)
    gets_edge = jnp.logical_or(part < head_size - 1, has_after)
    gives_side = (
        jnp.logical_and(gives_edge, part != 0),
        jnp.logical_and(gives_edge, part != middle),
    )
    gets_side = (
        jnp.logical_and(gets_edge, part != head_size - 1),
        jnp.logical_and(gets_edge, part != middle - 1),
    )
    lower = part < middle
    inner_from = jnp.where(lower, 0, middle)
    has_inner = jnp.logical_or(part >= middle, has_before)
    gives_inner = jnp.logical_and(has_inner, part == inner_from)
    gets_inner = jnp.logical_and(has_inner, part != inner_from)

    def inner_copy(d, c):
        other = inner_from + d
        return send(
            grads[c // 2][1].at[other, c % 2], inner_in.at[c], inner_send.at[d, c],
            inner_recv.at[c], (shard, other),
        )

    def give_edges(h):
        for side in range(2):
            pl.when(gives_side[side])(edge_copy(h, side).start)

        @pl.when(gives_inner)
        def _():
            for c in (2 * h, 2 * h + 1):
                for d in range(1, middle):
                    inner_copy(d, c).start()
                inner_in[c] = grads[h][1][part, c % 2]

    def root_over(h, q):
        return send(
            grads[h][3].at[q], root_box.at[h, shard], over_send.at[h, q], over_recv.at[h, shard],
            (jnp.int32(carrier(q, head_size, seq_size)), part),
        )

    def root_up(h):
        return send(
            root.at[h, share], up_box.at[h, part], up_send.at[h], up_recv.at[h, part], (shard, 0)
        )

    def root_out(h):
        return send(
            root.at[h, share], last_box.at[h, share], out_send.at[h], out_recv.at[h, share], (0, part)
        )

    sends_up = jnp.logical_and(carries, part > 0)
    sends_out = jnp.logical_and(jnp.logical_and(carries, part == 0), shard > 0)

    def landed(box, sem):
        send(box, box, sem, sem, (shard, part)).wait_recv()

    def root_event(h, e):
        if e == 1:

            @pl.when(carries)
            def _():
                total = grads[h][3][share]
                for d in range(1, seq_size):
                    other = lax.rem(shard + d, seq_size)
                    landed(root_box.at[h, other], over_recv.at[h, other])
                    total += root_box[h, other]
                root[h, share] = total

            pl.when(sends_up)(root_up(h).start)
        else:

            @pl.when(jnp.logical_and(carries, part == 0))
            def _():
                total = root[h, share]
                for z in range(1, head_size):
                    landed(up_box.at[h, z], up_recv.at[h, z])
                    total += up_box[h, z]
                root[h, share] = total

            pl.when(sends_out)(root_out(h).start)

    def keep(c):
        slots_in[c, rows_of(part * blocks, blocks)] = grads[c // 2][2][part, c % 2]

    def section(t):
        at = last[t]
        found = chain[jnp.maximum(at, 0)]
        return jnp.where(at >= 0, found, 0.0)

    def collect(c):
        for d in range(1, head_size):
            slice_out(d, c).wait_recv()
        for n in range(slots):
            term = slots_in[c, n].astype(jnp.float32)
            if n > 0:
                same = earlier[n]
                found = chain[jnp.maximum(same, 0)]
                term = term + jnp.where(same >= 0, found, 0.0)
            chain[n] = term
        for t in range(slots):
            sections[c, t] = section(t).astype(jnp.bfloat16)
        pl.when(shard > 1)(far_copy(c).start)
        pl.when(gets_inner)(inner_copy(1, c).wait_recv)
        for t in range(slots, 3 * slots):
            total = section(t)
            here = None
            if t == 2 * slots - 1:
                here = jnp.logical_and(lower, has_inner)
            elif t == 2 * slots - 1 + middle * blocks:
                here = jnp.logical_not(lower)
            if here is not None:
                total += jnp.where(here, inner_in[c].astype(jnp.float32), 0.0)
            sections[c, t] = total.astype(jnp.bfloat16)

    def add_to(c, where, came):
        sections[c, where] = (
            sections[c, where].astype(jnp.float32) + came[c].astype(jnp.float32)
        ).astype(jnp.bfloat16)

    def relay(c):
        @pl.when(jnp.logical_and(has_before, has_after))
        def _():
            far_copy(c).wait_recv()
            add_to(c, rows_of(slots, slots), far_in)

        pl.when(has_before)(near_copy(c).start)

    def give_back(c):
        @pl.when(has_after)
        def _():
            near_copy(c).wait_recv()
            add_to(c, rows_of(2 * slots, slots), near_in)

        for d in range(1, head_size):
            slice_back(d, c).start()

    def after_head(h, i):
        z, _ = chunk_head(i, h, head_size, each)
        pl.when(shard != carrier(z, head_size, seq_size))(root_over(h, z).start)

        @pl.when(i < head_size - 1)
        def _():
            for kv in range(2):
                slice_out(i + 1, 2 * h + kv).start()

    def after_chunk(h):
        give_edges(h)
        for c in (2 * h, 2 * h + 1):
            keep(c)

    def finish(c, z, came):
        h, kv = c // 2, c % 2
        where = pl.ds(pl.multiple_of((z * each + h) * HEAD_SIZE, HEAD_SIZE), HEAD_SIZE)
        for n in range(blocks):
            total = grads[h][0][z, kv, n] + came[n].astype(jnp.float32)
            if n == 0:
                total += root[h, z, kv]
            if n == blocks - 1:
                total += edge_in[h, z, kv].astype(jnp.float32)
            outputs[kv][pl.ds(n * BLOCK, BLOCK), where] = total.astype(jnp.bfloat16)

    def finish_all():
        for side in range(2):
            slices = pl.ds(side * middle, middle)
            for h in range(each):
                pl.when(gets_side[side])(edge_copy(h, side).wait_recv)

            @pl.when(jnp.logical_not(gets_side[side]))
            def _(slices=slices):
                edge_in[:, slices] = jnp.zeros_like(edge_in[:, slices])

        first = jnp.logical_and(shard == 0, part == 0)

        @pl.when(first)
        def _():
            for h in range(each):
                for q in range(1, head_size):
                    landed(last_box.at[h, q], out_recv.at[h, q])
                    root[h, q] = last_box[h, q]

        @pl.when(jnp.logical_not(first))
        def _():
            for h in range(each):
                pl.when(sends_up)(root_up(h).wait_send)
                pl.when(sends_out)(root_out(h).wait_send)
            root[...] = jnp.zeros_like(root)

        for c in range(pieces):
            finish(c, part, sections.at[c, rows_of(2 * slots + part * blocks, blocks)])
            for d in range(1, head_size):
                came = lax.rem(part + head_size - d, head_size)
                slice_back(d, c).wait_recv()
                finish(c, came, back.at[c, came])

    def drain():
        for c in range(pieces):
            for d in range(1, head_size):
                slice_out(d, c).wait_send()
                slice_back(d, c).wait_send()
            pl.when(shard > 1)(far_copy(c).wait_send)
            pl.when(has_before)(near_copy(c).wait_send)
        for h in range(each):
            for side in range(2):
                pl.when(gives_side[side])(edge_copy(h, side).wait_send)

            @pl.when(gives_inner)
            def _(h=h):
                for c in (2 * h, 2 * h + 1):
                    for d in range(1, middle):
                        inner_copy(d, c).wait_send()

            for q in range(head_size):
                pl.when(shard != shares[q])(root_over(h, q).wait_send)

    return after_head, after_chunk, collect, relay, give_back, root_event, finish_all, drain


def kernel(
    head_size, seq_size, each, ancestors, k_ref, v_ref, q_ref, up_ref,
    att_ref, dq_ref, k_out, v_out, *rest,
):
    shard, part = lax.axis_index("seq"), lax.axis_index("head")
    blocks, _, width = k_ref.shape
    slots = blocks * head_size
    pieces = 2 * each
    rest = list(rest)

    def take(count):
        taken = rest[:count]
        del rest[:count]
        return taken

    window = take(pieces)
    rand = take(each)
    grads = [take(4) for _ in range(each)]
    work = [take(6) for _ in range(each)]
    kvx, root_block, stage = take(3)
    given = take(12)
    earlier, last = take(2)
    (kv_sem,) = take(1)
    fetch_sems = take(18)
    inputs, outputs = (k_ref, v_ref), (k_out, v_out)
    shard, part = lax.axis_index("seq"), lax.axis_index("head")
    origin = (shard - 2) * slots

    def place(n):
        entry = ancestors[1, n]
        return jnp.where(entry >= 0, entry - origin, -1)

    def chosen(n):
        at = place(n)
        return jnp.where(at >= 0, at, 2 * slots)

    def uses(j):
        n = part * blocks + j
        first_entry, last_entry = ancestors[0, n], ancestors[1, n]
        return first_entry >= 0, jnp.logical_and(last_entry >= 0, last_entry != first_entry)

    def write_links():
        places = [place(n) for n in range(slots)]
        for n in range(slots):
            found = jnp.int32(-1)
            for m in range(n):
                found = jnp.where(places[m] == places[n], m, found)
            earlier[n] = found

        def one(t, carry):
            found = jnp.int32(-1)
            for n in range(slots):
                found = jnp.where(places[n] == t, n, found)
            last[t] = found
            return carry

        lax.fori_loop(0, 3 * slots, one, 0)

    chunks = [
        Chunk(
            h, each, head_size, uses, (q_ref, up_ref), (att_ref, dq_ref), kvx, root_block, rand[h],
            grads[h], work[h],
        )
        for h in range(each)
    ]

    def kv_load(kv):
        return pltpu.make_async_copy(inputs[kv], kvx.at[kv, pl.ds(1, blocks)], kv_sem.at[kv])

    for kv in range(2):
        kv_load(kv).start()
    greet(head_size, seq_size)
    begin, pass_on, relay, pick, arrive, root_event, finish_edge, drain = fetch_steps(
        head_size, seq_size, each, chosen, inputs, window, rand, kvx, root_block, kv_load,
        [stage, *fetch_sems],
    )
    after_head, after_chunk, collect, give_on, give_back, root_sum, finish_all, drain_grads = (
        give_steps(
            head_size, seq_size, each, earlier, last, grads, outputs, [*given, *rest],
        )
    )
    begin()
    for chunk in chunks:
        chunk.start_loads()
    write_links()
    for at in range(pieces + 1):
        if at >= 2:
            pick(at - 2)
        if at >= 1:
            relay(at - 1)
        if at < pieces:
            pass_on(at)
        if at < 2:
            root_event(at)
    root_event(2)
    finish_edge()
    final = pieces - 1
    if each == 1:
        pick(final)
    do = functools.partial
    for h, chunk in enumerate(chunks):
        for c in (2 * h, 2 * h + 1):
            arrive(c)
        if h == 0:
            events = [(3, do(pick, final))] if each > 1 else []
        else:
            events = [
                (2, do(give_on, 2 * h - 2)),
                (4, do(give_on, 2 * h - 1)),
                (9, do(root_sum, h - 1, 1)),
                (11, do(give_back, 2 * h - 2)),
                (13, do(root_sum, h - 1, 2)),
                (15, do(give_back, 2 * h - 1)),
            ]
        chunk.run(events, do(after_head, h))
        after_chunk(h)
        if h < each - 1:
            collect(2 * h)
            collect(2 * h + 1)
    h = each - 1
    collect(2 * h)
    collect(2 * h + 1)
    give_on(2 * h)
    give_on(2 * h + 1)
    root_sum(h, 1)
    give_back(2 * h)
    give_back(2 * h + 1)
    root_sum(h, 2)
    finish_all()
    for chunk in chunks:
        chunk.wait_stores()
    drain()
    drain_grads()


def attention(ancestors, key_rows, value_rows, queries, upstream, head_size, seq_size):
    blocks, _, width = key_rows.shape
    heads = width // HEAD_SIZE
    each = heads // head_size
    pieces = 2 * each
    slots = blocks * head_size
    vmem, smem = pltpu.MemorySpace.VMEM, pltpu.MemorySpace.SMEM
    dma = pltpu.SemaphoreType.DMA
    picked = pltpu.VMEM((head_size, 2, blocks, BLOCK, HEAD_SIZE), jnp.bfloat16)
    box = pltpu.VMEM((pieces, slots, BLOCK, HEAD_SIZE), jnp.bfloat16)
    edge = (head_size, 2, BLOCK, HEAD_SIZE)
    outs = [(queries.shape, jnp.bfloat16)] * 2 + [((blocks * BLOCK, width), jnp.bfloat16)] * 2
    hops = [
        dma((head_size, pieces)), dma((head_size, pieces)),
        dma((pieces,)), dma((pieces,)), dma((pieces,)), dma((pieces,)),
        dma((head_size, pieces)), dma((head_size, pieces)),
    ]
    return pl.pallas_call(
        functools.partial(kernel, head_size, seq_size, each),
        in_specs=[pl.BlockSpec(memory_space=smem)] + [pl.BlockSpec(memory_space=pl.ANY)] * 4,
        out_specs=[pl.BlockSpec(memory_space=pl.ANY)] * 2 + [pl.BlockSpec(memory_space=vmem)] * 2,
        out_shape=[jax.ShapeDtypeStruct(*out) for out in outs],
        scratch_shapes=[
            *[pltpu.VMEM((3 * slots, BLOCK, HEAD_SIZE), jnp.bfloat16)] * pieces,
            *[picked] * each,
            *[pltpu.VMEM(*shape) for shape in grad_shapes(head_size, blocks) * each],
            *chunk_scratch(head_size, blocks, queries.shape[-1] // heads) * each,
            pltpu.VMEM((2, blocks + 1, BLOCK, width), jnp.bfloat16),
            pltpu.VMEM((head_size, 2, BLOCK, each * HEAD_SIZE), jnp.bfloat16),
            box,
            box,
            pltpu.VMEM((slots, BLOCK, HEAD_SIZE), jnp.float32),
            pltpu.VMEM((pieces, 3 * slots, BLOCK, HEAD_SIZE), jnp.bfloat16),
            box,
            box,
            pltpu.VMEM((pieces, head_size, blocks, BLOCK, HEAD_SIZE), jnp.bfloat16),
            pltpu.VMEM((each,) + edge, jnp.bfloat16),
            pltpu.VMEM((pieces, BLOCK, HEAD_SIZE), jnp.bfloat16),
            pltpu.VMEM((each,) + edge, jnp.float32),
            pltpu.VMEM((each, seq_size) + edge[1:], jnp.float32),
            pltpu.VMEM((each,) + edge, jnp.float32),
            pltpu.VMEM((each,) + edge, jnp.float32),
            pltpu.SMEM((slots,), jnp.int32),
            pltpu.SMEM((3 * slots,), jnp.int32),
            dma((2,)),
            *hops, dma((2, 2)), dma((2, 2)), dma((pieces,)), dma((head_size, pieces)),
            dma((head_size,)), dma((1,)), dma((head_size,)), dma((1,)),
            dma((seq_size,)), dma((head_size,)),
            *hops, dma((each, 2)), dma((each, 2)), dma((head_size, pieces)), dma((pieces,)),
            dma((each, head_size)), dma((each, seq_size)), dma((each,)), dma((each, head_size)),
            dma((each,)), dma((each, head_size)),
        ],
        compiler_params=pltpu.CompilerParams(
            collective_id=0, has_side_effects=True, vmem_limit_bytes=42 * 1024 * 1024
        ),
        name="attention",
    )(ancestors, key_rows, value_rows, queries, upstream)


def local(queries, key_rows, value_rows, upstream, ancestors):
    tokens, _ = key_rows.shape
    blocks = tokens // BLOCK
    head_size, seq_size = lax.axis_size("head"), lax.axis_size("seq")

    def blocked(x):
        return x.reshape(blocks, BLOCK, x.shape[1])

    attended, query_grad, key_grad, value_grad = attention(
        ancestors.T, blocked(key_rows), blocked(value_rows), blocked(queries),
        blocked(upstream), head_size, seq_size,
    )
    wide = queries.shape[-1]
    return attended.reshape(tokens, wide), query_grad.reshape(tokens, wide), key_grad, value_grad


def solution(mesh):
    tokens = P(("seq", "head"), None)
    return jax.shard_map(
        local,
        mesh=mesh,
        in_specs=(tokens, tokens, tokens, tokens, P("seq", None)),
        out_specs=(tokens, tokens, tokens, tokens),
        check_vma=False,
    )
```

```python
import functools
import math

import jax
import jax.numpy as jnp
from jax import lax
from jax.experimental import pallas as pl
from jax.experimental.pallas import tpu as pltpu
from jax.sharding import PartitionSpec as P

HEAD_SIZE = 128
BLOCK = 64
NEGATIVE = -1e30
MESH = pl.DeviceIdType.MESH


def attend(first, use_prev, use_rand, q_tile, up_tile, keys, values, groups):
    scale = HEAD_SIZE ** (-0.5)
    rows = groups * BLOCK
    q = jnp.concatenate(
        [q_tile[:, r * HEAD_SIZE : (r + 1) * HEAD_SIZE] for r in range(groups)], axis=0
    )
    up = jnp.concatenate(
        [up_tile[:, r * HEAD_SIZE : (r + 1) * HEAD_SIZE] for r in range(groups)], axis=0
    )
    up_t = up.T
    scores = lax.dot_general(
        keys, q, (((1,), (1,)), ((), ())), preferred_element_type=jnp.float32
    ) * (scale * math.log2(math.e))
    key_at = lax.broadcasted_iota(jnp.int32, (BLOCK, rows), 0)
    query_at = lax.broadcasted_iota(jnp.int32, (BLOCK, rows), 1) & (BLOCK - 1)
    causal = key_at <= query_at
    never = jnp.float32(NEGATIVE)
    zero = jnp.float32(0.0)
    root_off = jnp.where(causal, zero, jnp.where(first, never, zero))
    own_off = jnp.where(causal, jnp.where(first, never, zero), never)
    prev_off = jnp.where(use_prev, zero, never)
    rand_off = jnp.where(use_rand, zero, never)
    scores = jnp.concatenate(
        [
            scores[:BLOCK] + root_off,
            scores[BLOCK : 2 * BLOCK] + own_off,
            scores[2 * BLOCK : 3 * BLOCK] + prev_off,
            scores[3 * BLOCK :] + rand_off,
        ],
        axis=0,
    )
    top = jnp.max(scores, axis=0, keepdims=True)
    weights = jnp.exp2(scores - top)
    total = jnp.sum(weights, axis=0, keepdims=True)
    probs = (weights * (1.0 / total)).astype(jnp.bfloat16)
    att_t = lax.dot_general(
        values, probs, (((0,), (0,)), ((), ())), preferred_element_type=jnp.float32
    ).astype(jnp.bfloat16)
    delta = jnp.sum(
        att_t.astype(jnp.float32) * up_t.astype(jnp.float32), axis=0, keepdims=True
    )
    dprob = lax.dot_general(
        values, up_t, (((1,), (0,)), ((), ())), preferred_element_type=jnp.float32
    )
    dscore = (probs.astype(jnp.float32) * (dprob - delta)).astype(jnp.bfloat16)
    dq_t = lax.dot_general(
        keys, dscore, (((0,), (0,)), ((), ())), preferred_element_type=jnp.float32
    )
    dq = (dq_t * scale).astype(jnp.bfloat16).T
    grads = (
        scale * jnp.dot(dscore, q, preferred_element_type=jnp.float32),
        jnp.dot(probs, up, preferred_element_type=jnp.float32),
    )
    return att_t.T, dq, grads


def chunk_head(i, h, head_size, each):
    z = lax.rem(lax.axis_index("head") + i, head_size)
    return z, z * each + h


class Chunk:
    def __init__(self, h, each, head_size, uses, wide, tokens, kvx, root, rand, grads, scratch):
        self.h, self.each, self.head_size, self.uses = h, each, head_size, uses
        self.wide, self.tokens, self.kvx, self.root, self.rand = wide, tokens, kvx, root, rand
        self.acc, self.g_edge, self.g_rand, self.g_root = grads
        self.buffers, self.load_sem, self.store_sem = scratch[:4], scratch[4], scratch[5]
        self.blocks = wide[0].shape[0]
        self.width = self.buffers[0].shape[-1]

    def columns(self, i):
        _, g = chunk_head(i, self.h, self.head_size, self.each)
        return pl.ds(pl.multiple_of(g * self.width, self.width), self.width)

    def load(self, i, which):
        return pltpu.make_async_copy(
            self.wide[which].at[:, :, self.columns(i)],
            self.buffers[which].at[i],
            self.load_sem.at[i, which],
        )

    def store(self, i, which):
        return pltpu.make_async_copy(
            self.buffers[2 + which].at[i],
            self.tokens[which].at[:, :, self.columns(i)],
            self.store_sem.at[i, which],
        )

    def wait_stores(self):
        for i in range(self.head_size):
            for which in range(2):
                self.store(i, which).wait()

    def start_loads(self):
        for i in range(self.head_size):
            for which in range(2):
                self.load(i, which).start()

    def run(self, events, before_head, after_head):
        blocks = self.blocks
        steps = self.head_size * blocks
        shard, part = lax.axis_index("seq"), lax.axis_index("head")
        at_first = jnp.logical_and(shard == 0, part == 0)
        q_buf, up_buf, att_buf, dq_buf = self.buffers
        groups = self.width // HEAD_SIZE

        def step(t, carry):
            i, j = t // blocks, t % blocks
            z, g = chunk_head(i, self.h, self.head_size, self.each)

            @pl.when(j == 0)
            def _():
                for which in range(2):
                    self.load(i, which).wait()
                before_head(i)

            here = pl.ds(pl.multiple_of(g * HEAD_SIZE, HEAD_SIZE), HEAD_SIZE)
            mine = slice(self.h * HEAD_SIZE, (self.h + 1) * HEAD_SIZE)
            keys, values = (
                jnp.concatenate(
                    [
                        self.root[z, kv, :, mine],
                        self.kvx[kv, j + 1, :, here],
                        self.kvx[kv, j, :, here],
                        self.rand[z, kv, j],
                    ],
                    axis=0,
                )
                for kv in range(2)
            )
            att, dq, grads = attend(
                jnp.logical_and(at_first, j == 0),
                *self.uses(j),
                q_buf[i, j], up_buf[i, j], keys, values, groups,
            )
            for r in range(groups):
                where = slice(r * HEAD_SIZE, (r + 1) * HEAD_SIZE)
                att_buf[i, j, :, where] = att[r * BLOCK : (r + 1) * BLOCK]
                dq_buf[i, j, :, where] = dq[r * BLOCK : (r + 1) * BLOCK]
            for kv, grad in enumerate(grads):
                self.acc[z, kv, j] = grad[BLOCK : 2 * BLOCK]
                self.g_rand[z, kv, j] = grad[3 * BLOCK :].astype(jnp.bfloat16)

            @pl.when(j == 0)
            def _():
                for kv, grad in enumerate(grads):
                    self.g_root[z, kv] = grad[:BLOCK]
                    self.g_edge[z, kv] = grad[2 * BLOCK : 3 * BLOCK].astype(jnp.bfloat16)

            @pl.when(j > 0)
            def _():
                for kv, grad in enumerate(grads):
                    self.g_root[z, kv] += grad[:BLOCK]
                    self.acc[z, kv, j - 1] += grad[2 * BLOCK : 3 * BLOCK]

            @pl.when(j == blocks - 1)
            def _():
                for which in range(2):
                    self.store(i, which).start()
                after_head(i)

            for at, event in events:
                pl.when(t == at * steps // 16)(event)
            return carry

        lax.fori_loop(0, steps, step, 0)


def grad_shapes(head_size, blocks):
    block = (BLOCK, HEAD_SIZE)
    return [
        ((head_size, 2, blocks) + block, jnp.float32),
        ((head_size, 2) + block, jnp.bfloat16),
        ((head_size, 2, blocks) + block, jnp.bfloat16),
        ((head_size, 2) + block, jnp.float32),
    ]


def chunk_scratch(head_size, blocks, wide):
    return [pltpu.VMEM((head_size, blocks, BLOCK, wide), jnp.bfloat16)] * 4 + [
        pltpu.SemaphoreType.DMA((head_size, 2)),
        pltpu.SemaphoreType.DMA((head_size, 2)),
    ]


def carrier(q, head_size, seq_size):
    return q * seq_size // head_size


def greet(head_size, seq_size):
    shard, part = lax.axis_index("seq"), lax.axis_index("head")
    barrier = pltpu.get_barrier_semaphore()
    count = 0

    def signal(other):
        pl.semaphore_signal(barrier, inc=1, device_id=other, device_id_type=MESH)

    for d in range(1, head_size):
        signal((shard, lax.rem(part + d, head_size)))
        count += 1
    for d in range(1, seq_size):
        signal((lax.rem(shard + d, seq_size), part))
        count += 1
    after, before = lax.rem(shard + 1, seq_size), lax.rem(shard + seq_size - 1, seq_size)

    @pl.when(part == head_size - 1)
    def _():
        signal((after, 0))

    @pl.when(part == 0)
    def _():
        signal((before, head_size - 1))

    at_end = jnp.logical_or(part == 0, part == head_size - 1)
    pl.semaphore_wait(barrier, count + jnp.where(at_end, 1, 0))


def send(source, target, send_sem, recv_sem, other):
    return pltpu.make_async_remote_copy(
        src_ref=source,
        dst_ref=target,
        send_sem=send_sem,
        recv_sem=recv_sem,
        device_id=other,
        device_id_type=MESH,
    )


def rows_of(at, count):
    return pl.ds(at, count)


def fetch_steps(
    head_size, seq_size, each, chosen, inputs, window, rand, kvx, root, kv_load, scratch
):
    shard, part = lax.axis_index("seq"), lax.axis_index("head")
    blocks = inputs[0].shape[0]
    slots = blocks * head_size
    pieces = 2 * each
    (stage, a_send, a_recv, near_send, near_recv, far_send, far_recv,
     b_send, b_recv, edge_send, edge_recv, inner_send, inner_recv, out_send, out_recv,
     up_send, up_recv, over_send, over_recv) = scratch
    middle = head_size // 2
    half = inputs[0].shape[-1] // 2
    shares = [carrier(q, head_size, seq_size) for q in range(head_size)]
    stride = seq_size // head_size
    share = shard // stride
    carries = lax.rem(shard, stride) == 0
    after = jnp.minimum(shard + 1, seq_size - 1)
    has_after, has_before = shard + 1 < seq_size, shard > 0
    at_first = jnp.logical_and(shard == 0, part == 0)

    def columns(p, c):
        return pl.ds(pl.multiple_of((p * each + c // 2) * HEAD_SIZE, HEAD_SIZE), HEAD_SIZE)

    def slice_out(d, c):
        other = lax.rem(part + d, head_size)
        return send(
            inputs[c % 2].at[:, :, columns(other, c)],
            window[c].at[rows_of(2 * slots + part * blocks, blocks)],
            a_send.at[d, c], a_recv.at[d, c], (shard, other),
        )

    def near_copy(c):
        return send(
            window[c].at[rows_of(2 * slots, slots)], window[c].at[rows_of(slots, slots)],
            near_send.at[c], near_recv.at[c], (after, part),
        )

    def far_copy(c):
        return send(
            window[c].at[rows_of(slots, slots)], window[c].at[rows_of(0, slots)],
            far_send.at[c], far_recv.at[c], (after, part),
        )

    def slice_back(d, c):
        other = lax.rem(part + d, head_size)
        return send(
            stage.at[c, rows_of(other * blocks, blocks)], rand[c // 2].at[part, c % 2],
            b_send.at[d, c], b_recv.at[d, c], (shard, other),
        )

    def edge_copy(kv, side):
        last = part == head_size - 1
        other = (jnp.where(last, after, shard), jnp.where(last, 0, part + 1))
        columns = slice(side * half, (side + 1) * half)
        return send(
            inputs[kv].at[blocks - 1, :, columns], kvx.at[kv, 0, :, columns],
            edge_send.at[kv, side], edge_recv.at[kv, side], other,
        )

    gives_edge = jnp.logical_or(part < head_size - 1, has_after)
    gets_edge = jnp.logical_or(part > 0, has_before)
    gives_side = (
        jnp.logical_and(gives_edge, part != head_size - 1),
        jnp.logical_and(gives_edge, part != middle - 1),
    )
    gets_side = (
        jnp.logical_and(gets_edge, part != 0),
        jnp.logical_and(gets_edge, part != middle),
    )
    lower = part < middle
    near_end = 2 * slots - 1
    inner_at = jnp.where(lower, near_end, near_end + middle * blocks)
    inner_to = jnp.where(lower, 0, middle)
    has_inner = jnp.logical_or(part >= middle, has_before)

    def inner_copy(q, c):
        return send(
            window[c].at[inner_at], kvx.at[c % 2, 0, :, columns(q, c)],
            inner_send.at[c], inner_recv.at[q, c], (shard, inner_to),
        )

    gives_inner = jnp.logical_and(has_inner, part != inner_to)

    def inner(c):
        pl.when(gives_inner)(inner_copy(part, c).start)

        @pl.when(jnp.logical_and(has_inner, part == inner_to))
        def _():
            kvx[c % 2, 0, :, columns(part, c)] = window[c][inner_at]

    def root_out(q):
        return send(
            root.at[q], root.at[q], out_send.at[q], out_recv.at[0], (jnp.int32(shares[q]), part)
        )

    def root_up(z):
        return send(root.at[share], root.at[share], up_send.at[z], up_recv.at[0], (shard, z))

    def root_over(d):
        other = lax.rem(shard + d, seq_size)
        copy = send(
            root.at[share], root.at[share], over_send.at[d], over_recv.at[share], (other, part)
        )
        return copy, jnp.logical_or(part > 0, other > 0)

    def spread():
        for d in range(1, seq_size):
            copy, wanted = root_over(d)
            pl.when(wanted)(copy.start)

    def root_event(e):
        if e == 0:

            @pl.when(jnp.logical_and(carries, part == 0))
            def _():
                pl.when(shard > 0)(root_out(0).wait_recv)
                for z in range(1, head_size):
                    root_up(z).start()
                spread()

        elif e == 1:

            @pl.when(jnp.logical_and(carries, part > 0))
            def _():
                root_up(0).wait_recv()
                spread()

        else:

            @pl.when(jnp.logical_not(at_first))
            def _():
                for q in range(head_size):
                    copy = send(root.at[q], root.at[q], over_send.at[0], over_recv.at[q], (shard, part))
                    pl.when(shard != shares[q])(copy.wait_recv)

    def start_slices(c):
        for d in range(1, head_size):
            slice_out(d, c).start()

    def begin():
        for c in range(2):
            start_slices(c)
        for kv in range(2):
            for side in range(2):
                pl.when(gives_side[side])(edge_copy(kv, side).start)
            kv_load(kv).wait()

        @pl.when(at_first)
        def _():
            for q in range(head_size):
                for kv in range(2):
                    root[q, kv] = kvx[kv, 1, :, q * each * HEAD_SIZE : (q + 1) * each * HEAD_SIZE]
            for q in range(1, head_size):
                root_out(q).start()

        for c in range(pieces):
            window[c][rows_of(2 * slots + part * blocks, blocks)] = kvx[
                c % 2, 1:, :, columns(part, c)
            ]

        @pl.when(jnp.logical_not(gets_edge))
        def _():
            for kv in range(2):
                kvx[kv, 0] = kvx[kv, 1]

    def pass_on(c):
        for d in range(1, head_size):
            slice_out(d, c).wait_recv()
        if c + 2 < pieces:
            start_slices(c + 2)
        pl.when(has_after)(near_copy(c).start)

    def relay(c):
        pl.when(has_before)(near_copy(c).wait_recv)
        pl.when(jnp.logical_and(has_before, has_after))(far_copy(c).start)
        inner(c)

    def pick(c):
        pl.when(shard > 1)(far_copy(c).wait_recv)
        for d in range(1, head_size):
            other = lax.rem(part + d, head_size)
            for n in range(blocks):
                stage[c, other * blocks + n] = window[c][chosen(other * blocks + n)]
            slice_back(d, c).start()
        for n in range(blocks):
            rand[c // 2][part, c % 2, n] = window[c][chosen(part * blocks + n)]

    def arrive(h, i):
        @pl.when(i > 0)
        def _():
            for c in (2 * h, 2 * h + 1):
                slice_back(head_size - i, c).wait_recv()

    def finish_edge():
        for kv in range(2):
            for side in range(2):
                pl.when(gets_side[side])(edge_copy(kv, side).wait_recv)

        @pl.when(jnp.logical_and(has_inner, part == inner_to))
        def _():
            for d in range(1, middle):
                for c in range(pieces):
                    inner_copy(part + d, c).wait_recv()

    def drain():
        for c in range(pieces):
            for d in range(1, head_size):
                slice_out(d, c).wait_send()
                slice_back(d, c).wait_send()
            pl.when(has_after)(near_copy(c).wait_send)
            pl.when(jnp.logical_and(has_before, has_after))(far_copy(c).wait_send)
        for c in range(pieces):
            pl.when(gives_inner)(inner_copy(part, c).wait_send)
        for kv in range(2):
            for side in range(2):
                pl.when(gives_side[side])(edge_copy(kv, side).wait_send)

        @pl.when(at_first)
        def _():
            for q in range(1, head_size):
                root_out(q).wait_send()

        @pl.when(carries)
        def _():
            @pl.when(part == 0)
            def _():
                for z in range(1, head_size):
                    root_up(z).wait_send()

            for d in range(1, seq_size):
                copy, wanted = root_over(d)
                pl.when(wanted)(copy.wait_send)

    return begin, pass_on, relay, pick, arrive, root_event, finish_edge, drain


def give_steps(head_size, seq_size, each, earlier, last, grads, outputs, scratch):
    shard, part = lax.axis_index("seq"), lax.axis_index("head")
    (slots_in, chain, sections, near_in, far_in, back, edge_in, inner_in, root, root_box, up_box,
     last_box, sent, a_send, a_recv, near_send, near_recv, far_send, far_recv,
     b_send, b_recv, edge_send, edge_recv, inner_send, inner_recv, over_send, over_recv,
     up_send, up_recv, out_send, out_recv) = scratch
    middle = head_size // 2
    blocks = grads[0][0].shape[2]
    slots = blocks * head_size
    pieces = 2 * each
    shares = [carrier(q, head_size, seq_size) for q in range(head_size)]
    stride = seq_size // head_size
    share = shard // stride
    carries = lax.rem(shard, stride) == 0
    before = jnp.maximum(shard - 1, 0)
    has_after, has_before = shard + 1 < seq_size, shard > 0

    def slice_out(d, c):
        other = lax.rem(part + d, head_size)
        return send(
            grads[c // 2][2].at[other, c % 2],
            slots_in.at[c, rows_of(part * blocks, blocks)],
            a_send.at[d, c], a_recv.at[d, c], (shard, other),
        )

    def far_copy(c):
        return send(
            sections.at[c, rows_of(0, slots)], far_in.at[c],
            far_send.at[c], far_recv.at[c], (before, part),
        )

    def near_copy(c):
        return send(
            sections.at[c, rows_of(slots, slots)], near_in.at[c],
            near_send.at[c], near_recv.at[c], (before, part),
        )

    def slice_back(d, c):
        other = lax.rem(part + d, head_size)
        return send(
            sections.at[c, rows_of(2 * slots + other * blocks, blocks)], back.at[c, part],
            b_send.at[d, c], b_recv.at[d, c], (shard, other),
        )

    def edge_copy(h, side):
        other = (
            jnp.where(part == 0, before, shard),
            jnp.where(part == 0, head_size - 1, part - 1),
        )
        slices = pl.ds(side * middle, middle)
        return send(
            grads[h][1].at[slices], edge_in.at[h, slices], edge_send.at[h, side],
            edge_recv.at[h, side], other,
        )

    gives_edge = jnp.logical_or(part > 0, has_before)
    gets_edge = jnp.logical_or(part < head_size - 1, has_after)
    gives_side = (
        jnp.logical_and(gives_edge, part != 0),
        jnp.logical_and(gives_edge, part != middle),
    )
    gets_side = (
        jnp.logical_and(gets_edge, part != head_size - 1),
        jnp.logical_and(gets_edge, part != middle - 1),
    )
    lower = part < middle
    inner_from = jnp.where(lower, 0, middle)
    has_inner = jnp.logical_or(part >= middle, has_before)
    gives_inner = jnp.logical_and(has_inner, part == inner_from)
    gets_inner = jnp.logical_and(has_inner, part != inner_from)

    def inner_copy(d, c):
        other = inner_from + d
        return send(
            grads[c // 2][1].at[other, c % 2], inner_in.at[c], inner_send.at[d, c],
            inner_recv.at[c], (shard, other),
        )

    def give_edges(h):
        for side in range(2):
            pl.when(gives_side[side])(edge_copy(h, side).start)

        @pl.when(gives_inner)
        def _():
            for c in (2 * h, 2 * h + 1):
                for d in range(1, middle):
                    inner_copy(d, c).start()
                inner_in[c] = grads[h][1][part, c % 2]

    def root_over(h, q):
        return send(
            grads[h][3].at[q], root_box.at[h, shard], over_send.at[h, q], over_recv.at[h, shard],
            (jnp.int32(carrier(q, head_size, seq_size)), part),
        )

    def root_up(h):
        return send(
            sent.at[h, 0], up_box.at[h, part], up_send.at[h], up_recv.at[h, part], (shard, 0)
        )

    def root_out(h):
        return send(
            sent.at[h, 1], last_box.at[h, share], out_send.at[h], out_recv.at[h, share], (0, part)
        )

    sends_up = jnp.logical_and(carries, part > 0)
    sends_out = jnp.logical_and(jnp.logical_and(carries, part == 0), shard > 0)

    def landed(box, sem):
        send(box, box, sem, sem, (shard, part)).wait_recv()

    def root_event(h, e):
        if e == 1:

            @pl.when(carries)
            def _():
                total = grads[h][3][share]
                for d in range(1, seq_size):
                    other = lax.rem(shard + d, seq_size)
                    landed(root_box.at[h, other], over_recv.at[h, other])
                    total += root_box[h, other]
                root[h, share] = total
                sent[h, 0] = total.astype(jnp.bfloat16)

            pl.when(sends_up)(root_up(h).start)
        else:

            @pl.when(jnp.logical_and(carries, part == 0))
            def _():
                total = root[h, share]
                for z in range(1, head_size):
                    landed(up_box.at[h, z], up_recv.at[h, z])
                    total += up_box[h, z].astype(jnp.float32)
                root[h, share] = total
                sent[h, 1] = total.astype(jnp.bfloat16)

            pl.when(sends_out)(root_out(h).start)

    def keep(c):
        slots_in[c, rows_of(part * blocks, blocks)] = grads[c // 2][2][part, c % 2]

    def section(t):
        at = last[t]
        found = chain[jnp.maximum(at, 0)]
        return jnp.where(at >= 0, found, 0.0)

    def collect(c):
        for d in range(1, head_size):
            slice_out(d, c).wait_recv()
        for n in range(slots):
            term = slots_in[c, n].astype(jnp.float32)
            if n > 0:
                same = earlier[n]
                found = chain[jnp.maximum(same, 0)]
                term = term + jnp.where(same >= 0, found, 0.0)
            chain[n] = term
        for t in range(slots):
            sections[c, t] = section(t).astype(jnp.bfloat16)
        pl.when(shard > 1)(far_copy(c).start)
        pl.when(gets_inner)(inner_copy(1, c).wait_recv)
        for t in range(slots, 3 * slots):
            total = section(t)
            here = None
            if t == 2 * slots - 1:
                here = jnp.logical_and(lower, has_inner)
            elif t == 2 * slots - 1 + middle * blocks:
                here = jnp.logical_not(lower)
            if here is not None:
                total += jnp.where(here, inner_in[c].astype(jnp.float32), 0.0)
            sections[c, t] = total.astype(jnp.bfloat16)

    def add_to(c, where, came):
        sections[c, where] = (
            sections[c, where].astype(jnp.float32) + came[c].astype(jnp.float32)
        ).astype(jnp.bfloat16)

    def relay(c):
        @pl.when(jnp.logical_and(has_before, has_after))
        def _():
            far_copy(c).wait_recv()
            add_to(c, rows_of(slots, slots), far_in)

        pl.when(has_before)(near_copy(c).start)

    def give_back(c):
        @pl.when(has_after)
        def _():
            near_copy(c).wait_recv()
            add_to(c, rows_of(2 * slots, slots), near_in)

        for d in range(1, head_size):
            slice_back(d, c).start()

    def after_head(h, i):
        z, _ = chunk_head(i, h, head_size, each)
        pl.when(shard != carrier(z, head_size, seq_size))(root_over(h, z).start)

        @pl.when(i > 0)
        def _():
            for kv in range(2):
                slice_out(i, 2 * h + kv).start()

    def after_chunk(h):
        give_edges(h)
        for c in (2 * h, 2 * h + 1):
            keep(c)

    def finish(c, z, came):
        h, kv = c // 2, c % 2
        where = pl.ds(pl.multiple_of((z * each + h) * HEAD_SIZE, HEAD_SIZE), HEAD_SIZE)
        for n in range(blocks):
            total = grads[h][0][z, kv, n] + came[n].astype(jnp.float32)
            if n == 0:
                total += root[h, z, kv]
            if n == blocks - 1:
                total += edge_in[h, z, kv].astype(jnp.float32)
            outputs[kv][pl.ds(n * BLOCK, BLOCK), where] = total.astype(jnp.bfloat16)

    def finish_all():
        for side in range(2):
            slices = pl.ds(side * middle, middle)
            for h in range(each):
                pl.when(gets_side[side])(edge_copy(h, side).wait_recv)

            @pl.when(jnp.logical_not(gets_side[side]))
            def _(slices=slices):
                edge_in[:, slices] = jnp.zeros_like(edge_in[:, slices])

        first = jnp.logical_and(shard == 0, part == 0)

        @pl.when(first)
        def _():
            for h in range(each):
                for q in range(1, head_size):
                    landed(last_box.at[h, q], out_recv.at[h, q])
                    root[h, q] = last_box[h, q].astype(jnp.float32)

        @pl.when(jnp.logical_not(first))
        def _():
            for h in range(each):
                pl.when(sends_up)(root_up(h).wait_send)
                pl.when(sends_out)(root_out(h).wait_send)
            root[...] = jnp.zeros_like(root)

        for c in range(pieces):
            finish(c, part, sections.at[c, rows_of(2 * slots + part * blocks, blocks)])
            for d in range(1, head_size):
                came = lax.rem(part + head_size - d, head_size)
                slice_back(d, c).wait_recv()
                finish(c, came, back.at[c, came])

    def drain():
        for c in range(pieces):
            for d in range(1, head_size):
                slice_out(d, c).wait_send()
                slice_back(d, c).wait_send()
            pl.when(shard > 1)(far_copy(c).wait_send)
            pl.when(has_before)(near_copy(c).wait_send)
        for h in range(each):
            for side in range(2):
                pl.when(gives_side[side])(edge_copy(h, side).wait_send)

            @pl.when(gives_inner)
            def _(h=h):
                for c in (2 * h, 2 * h + 1):
                    for d in range(1, middle):
                        inner_copy(d, c).wait_send()

            for q in range(head_size):
                pl.when(shard != shares[q])(root_over(h, q).wait_send)

    return after_head, after_chunk, collect, relay, give_back, root_event, finish_all, drain


def kernel(
    head_size, seq_size, each, ancestors, k_ref, v_ref, q_ref, up_ref,
    att_ref, dq_ref, k_out, v_out, *rest,
):
    shard, part = lax.axis_index("seq"), lax.axis_index("head")
    blocks, _, width = k_ref.shape
    slots = blocks * head_size
    pieces = 2 * each
    rest = list(rest)

    def take(count):
        taken = rest[:count]
        del rest[:count]
        return taken

    window = take(pieces)
    rand = take(each)
    grads = [take(4) for _ in range(each)]
    work = [take(6) for _ in range(each)]
    kvx, root_block, stage = take(3)
    given = take(13)
    earlier, last = take(2)
    (kv_sem,) = take(1)
    fetch_sems = take(18)
    inputs, outputs = (k_ref, v_ref), (k_out, v_out)
    shard, part = lax.axis_index("seq"), lax.axis_index("head")
    origin = (shard - 2) * slots

    def place(n):
        entry = ancestors[1, n]
        return jnp.where(entry >= 0, entry - origin, -1)

    def chosen(n):
        at = place(n)
        return jnp.where(at >= 0, at, 2 * slots)

    def uses(j):
        n = part * blocks + j
        first_entry, last_entry = ancestors[0, n], ancestors[1, n]
        return first_entry >= 0, jnp.logical_and(last_entry >= 0, last_entry != first_entry)

    def write_links():
        places = [place(n) for n in range(slots)]
        for n in range(slots):
            found = jnp.int32(-1)
            for m in range(n):
                found = jnp.where(places[m] == places[n], m, found)
            earlier[n] = found

        def one(t, carry):
            found = jnp.int32(-1)
            for n in range(slots):
                found = jnp.where(places[n] == t, n, found)
            last[t] = found
            return carry

        lax.fori_loop(0, 3 * slots, one, 0)

    chunks = [
        Chunk(
            h, each, head_size, uses, (q_ref, up_ref), (att_ref, dq_ref), kvx, root_block, rand[h],
            grads[h], work[h],
        )
        for h in range(each)
    ]

    def kv_load(kv):
        return pltpu.make_async_copy(inputs[kv], kvx.at[kv, pl.ds(1, blocks)], kv_sem.at[kv])

    for kv in range(2):
        kv_load(kv).start()
    greet(head_size, seq_size)
    begin, pass_on, relay, pick, arrive, root_event, finish_edge, drain = fetch_steps(
        head_size, seq_size, each, chosen, inputs, window, rand, kvx, root_block, kv_load,
        [stage, *fetch_sems],
    )
    after_head, after_chunk, collect, give_on, give_back, root_sum, finish_all, drain_grads = (
        give_steps(
            head_size, seq_size, each, earlier, last, grads, outputs, [*given, *rest],
        )
    )
    begin()
    for chunk in chunks:
        chunk.start_loads()
    write_links()
    for at in range(pieces + 1):
        if at >= 2:
            pick(at - 2)
        if at >= 1:
            relay(at - 1)
        if at < pieces:
            pass_on(at)
        if at < 2:
            root_event(at)
    root_event(2)
    finish_edge()
    final = pieces - 1
    pick(final)
    do = functools.partial
    for h, chunk in enumerate(chunks):
        if h == 0:
            events = []
        else:
            events = [
                (2, do(collect, 2 * h - 2)),
                (3, do(collect, 2 * h - 1)),
                (5, do(give_on, 2 * h - 2)),
                (7, do(give_on, 2 * h - 1)),
                (9, do(root_sum, h - 1, 1)),
                (11, do(give_back, 2 * h - 2)),
                (13, do(root_sum, h - 1, 2)),
                (15, do(give_back, 2 * h - 1)),
            ]
        chunk.run(events, do(arrive, h), do(after_head, h))
        after_chunk(h)
    h = each - 1
    collect(2 * h)
    collect(2 * h + 1)
    give_on(2 * h)
    give_on(2 * h + 1)
    root_sum(h, 1)
    give_back(2 * h)
    give_back(2 * h + 1)
    root_sum(h, 2)
    finish_all()
    for chunk in chunks:
        chunk.wait_stores()
    drain()
    drain_grads()


def attention(ancestors, key_rows, value_rows, queries, upstream, head_size, seq_size):
    blocks, _, width = key_rows.shape
    heads = width // HEAD_SIZE
    each = heads // head_size
    pieces = 2 * each
    slots = blocks * head_size
    vmem, smem = pltpu.MemorySpace.VMEM, pltpu.MemorySpace.SMEM
    dma = pltpu.SemaphoreType.DMA
    picked = pltpu.VMEM((head_size, 2, blocks, BLOCK, HEAD_SIZE), jnp.bfloat16)
    box = pltpu.VMEM((pieces, slots, BLOCK, HEAD_SIZE), jnp.bfloat16)
    edge = (head_size, 2, BLOCK, HEAD_SIZE)
    outs = [(queries.shape, jnp.bfloat16)] * 2 + [((blocks * BLOCK, width), jnp.bfloat16)] * 2
    hops = [
        dma((head_size, pieces)), dma((head_size, pieces)),
        dma((pieces,)), dma((pieces,)), dma((pieces,)), dma((pieces,)),
        dma((head_size, pieces)), dma((head_size, pieces)),
    ]
    return pl.pallas_call(
        functools.partial(kernel, head_size, seq_size, each),
        in_specs=[pl.BlockSpec(memory_space=smem)] + [pl.BlockSpec(memory_space=pl.ANY)] * 4,
        out_specs=[pl.BlockSpec(memory_space=pl.ANY)] * 2 + [pl.BlockSpec(memory_space=vmem)] * 2,
        out_shape=[jax.ShapeDtypeStruct(*out) for out in outs],
        scratch_shapes=[
            *[pltpu.VMEM((3 * slots, BLOCK, HEAD_SIZE), jnp.bfloat16)] * pieces,
            *[picked] * each,
            *[pltpu.VMEM(*shape) for shape in grad_shapes(head_size, blocks) * each],
            *chunk_scratch(head_size, blocks, queries.shape[-1] // heads) * each,
            pltpu.VMEM((2, blocks + 1, BLOCK, width), jnp.bfloat16),
            pltpu.VMEM((head_size, 2, BLOCK, each * HEAD_SIZE), jnp.bfloat16),
            box,
            box,
            pltpu.VMEM((slots, BLOCK, HEAD_SIZE), jnp.float32),
            pltpu.VMEM((pieces, 3 * slots, BLOCK, HEAD_SIZE), jnp.bfloat16),
            box,
            box,
            pltpu.VMEM((pieces, head_size, blocks, BLOCK, HEAD_SIZE), jnp.bfloat16),
            pltpu.VMEM((each,) + edge, jnp.bfloat16),
            pltpu.VMEM((pieces, BLOCK, HEAD_SIZE), jnp.bfloat16),
            pltpu.VMEM((each,) + edge, jnp.float32),
            pltpu.VMEM((each, seq_size) + edge[1:], jnp.float32),
            pltpu.VMEM((each,) + edge, jnp.bfloat16),
            pltpu.VMEM((each,) + edge, jnp.bfloat16),
            pltpu.VMEM((each, 2) + edge[1:], jnp.bfloat16),
            pltpu.SMEM((slots,), jnp.int32),
            pltpu.SMEM((3 * slots,), jnp.int32),
            dma((2,)),
            *hops, dma((2, 2)), dma((2, 2)), dma((pieces,)), dma((head_size, pieces)),
            dma((head_size,)), dma((1,)), dma((head_size,)), dma((1,)),
            dma((seq_size,)), dma((head_size,)),
            *hops, dma((each, 2)), dma((each, 2)), dma((head_size, pieces)), dma((pieces,)),
            dma((each, head_size)), dma((each, seq_size)), dma((each,)), dma((each, head_size)),
            dma((each,)), dma((each, head_size)),
        ],
        compiler_params=pltpu.CompilerParams(
            collective_id=0, has_side_effects=True, vmem_limit_bytes=42 * 1024 * 1024
        ),
        name="attention",
    )(ancestors, key_rows, value_rows, queries, upstream)


def local(queries, key_rows, value_rows, upstream, ancestors):
    tokens, _ = key_rows.shape
    blocks = tokens // BLOCK
    head_size, seq_size = lax.axis_size("head"), lax.axis_size("seq")

    def blocked(x):
        return x.reshape(blocks, BLOCK, x.shape[1])

    attended, query_grad, key_grad, value_grad = attention(
        ancestors.T, blocked(key_rows), blocked(value_rows), blocked(queries),
        blocked(upstream), head_size, seq_size,
    )
    wide = queries.shape[-1]
    return attended.reshape(tokens, wide), query_grad.reshape(tokens, wide), key_grad, value_grad


def solution(mesh):
    tokens = P(("seq", "head"), None)
    return jax.shard_map(
        local,
        mesh=mesh,
        in_specs=(tokens, tokens, tokens, tokens, P("seq", None)),
        out_specs=(tokens, tokens, tokens, tokens),
        check_vma=False,
    )
```
